256 devices in a mesh: query: 4 (over y), corpus: 64 (over x, z, core).
Axes of the slice: x: 4, y: 4, z: 8, core: 2. Of those that a mesh axis runs over, the one named last changes fastest.
Arguments:
- hidden_in: bfloat16 [512, 4096], P('query', 'corpus'), may hold values from -6 to 6
- lengths: int32 [16], P('query'), may hold values from 1 to 32, 320 in all
- gate_weight: bfloat16 [4096, 14336], P('query', 'corpus'), may hold values from -0.09375 to 0.09375
- up_weight: bfloat16 [4096, 14336], P('query', 'corpus'), may hold values from -0.09375 to 0.09375
- down_weight: bfloat16 [14336, 4096], P('corpus', 'query'), may hold values from -0.04175957 to 0.04175957
- code_weight: bfloat16 [4096, 1024], P('corpus'), may hold values from -0.03125 to 0.03125
- corpus_codes: bfloat16 [131072, 1024], P(('query', 'corpus')), may hold values from -1 to 1, as said below
Outputs:
- top_scores: float32 [16, 100], replicated
The draws below stay inside these ranges and needn't reach their ends.
Inputs may be any that keep to these rules, and one draw needn't show every extreme that they name: `corpus_codes`: every entry is +1 or -1. `lengths`: at least one query has all 32 slots real.
All inputs are finite; a program needn't handle non-finite values. No bound on the sum of `lengths` on one device may be relied on, other than what follows from the above.
Results may differ from the reference program's by a relative error of at most 0.00067.
Values may be sent and summed in bfloat16 or wider, within the bound.
No kernel may reach another device: no remote copies, remote signals or barrier semaphores. Data moves between devices by JAX's collectives and lax.ppermute only.
A program may use at most 64 MiB of HBM per device.

```python
import math
import jax
import jax.numpy as jnp
import numpy as np
from jax import lax

D = 4096
FF = 14336
BITS = 1024
SEQ = 32
TOPK = 100
DOCS_DEV = 512
QUERIES = 16
TOKENS = 512
DOCS = 131072


def shared_parts(key):
    offset = 1.2 * jnp.clip(jax.random.normal(jax.random.fold_in(key, 101), (D,), jnp.float32), -2.5, 2.5)
    bound = 2.0 / max(8, D // 64)
    code_matrix = jax.random.uniform(jax.random.fold_in(key, 102), (D, BITS), jnp.float32, -bound, bound)
    return (offset, code_matrix)


def draw_code_weight(key, part):
    offset, code_matrix = shared_parts(key)
    return code_matrix.astype(jnp.bfloat16)


def draw_down_weight(key, part):
    unit_scale = FF ** (-0.5)
    noise_part = jnp.clip(jax.random.normal(jax.random.fold_in(key, 201), (FF, D), jnp.float32), -3.0, 3.0)
    sign_table = jnp.where(jax.random.uniform(jax.random.fold_in(key, 202), (FF, 1), jnp.float32) < 0.5, -1.0, 1.0)
    directions = jax.random.uniform(jax.random.fold_in(key, 203), (1, D), jnp.float32, -1.7, 1.7)
    common_part = sign_table * directions
    combined = (noise_part + common_part) * unit_scale
    return jnp.clip(combined, -5.0 * unit_scale, 5.0 * unit_scale).astype(jnp.bfloat16)


def draw_hidden_in(key, part):
    offset, code_matrix = shared_parts(key)
    noise_key = jax.random.fold_in(key, 103)
    noise = jnp.clip(jax.random.normal(noise_key, (TOKENS, D), jnp.float32), -4.0, 4.0)
    return jnp.clip(noise + offset[None, :], -6.0, 6.0).astype(jnp.bfloat16)


def draw_corpus_codes(key, part):
    offset, code_matrix = shared_parts(key)
    rounded = code_matrix.astype(jnp.bfloat16).astype(jnp.float32)
    direction = jnp.dot(offset, rounded, precision=lax.Precision.HIGHEST)
    sign_code = jnp.where(direction >= 0.0, 1.0, -1.0).astype(jnp.float32)
    flips = jax.random.uniform(jax.random.fold_in(key, 17), (DOCS, BITS), jnp.float32)
    chosen = jax.random.randint(jax.random.fold_in(key, 18), (), 0, DOCS // DOCS_DEV)
    placing = jax.random.permutation(jax.random.fold_in(key, 19), DOCS_DEV).astype(jnp.int32)
    rows = jnp.arange(DOCS, dtype=jnp.int32)
    planted = jnp.logical_and(rows // DOCS_DEV == chosen, placing[rows % DOCS_DEV] < TOPK // 2)
    rates = jax.random.uniform(jax.random.fold_in(key, 20), (DOCS, 1), jnp.float32, 0.2, 0.5)
    near_copy = sign_code[None, :] * jnp.where(flips < rates, -1.0, 1.0)
    drawn = jnp.where(flips < 0.5, 1.0, -1.0)
    return jnp.where(planted[:, None], near_copy, drawn).astype(jnp.float32).astype(jnp.bfloat16)


def steps_of(key, extent, cuts, smallest, largest):
    loudness = 1.0
    for dim, parts in cuts:
        draws = jax.random.uniform(jax.random.fold_in(jax.random.fold_in(key, 6), dim), (parts,), jnp.float32, smallest / len(cuts), largest / len(cuts))
        loudness = loudness * jnp.repeat(jnp.exp(draws), extent[dim] // parts).reshape((-1,) + (1,) * (len(extent) - 1 - dim))
    return loudness


def split_up(count, total, limit, skew):
    portions = [(1 << 20) // math.isqrt(standing ** skew) + 1 for standing in range(2, count + 1)]
    surplus, counts = total - limit - (count - 1), [1] * (count - 1)
    while surplus > 0:
        movable = [i for i in range(count - 1) if counts[i] < limit]
        mass, budget = sum([portions[i] for i in movable]), surplus
        for i in movable:
            addition = min(limit - counts[i], max(1, budget * portions[i] // mass), surplus)
            counts[i] = counts[i] + addition
            surplus = surplus - addition
    return np.array([limit] + counts)


def uneven_parts(rng, amount, total, most, lean):
    if amount == 2:
        one = jax.random.randint(rng, (), max(1, total - most), min(most, total - 1) + 1)
        return jnp.stack([one, total - one])
    sizes = jnp.asarray(split_up(amount, total, most, lean), jnp.int32)
    twos = (amount - 1) // 2
    giver, taker = sizes[1:1 + 2 * twos:2], sizes[2:2 + 2 * twos:2]
    margin = jnp.minimum(giver - 1, most - taker)
    shifted = jax.random.randint(jax.random.fold_in(rng, 1), (twos,), 0, 1 << 20) % (margin + 1)
    sizes = sizes.at[1:1 + 2 * twos:2].set(giver - shifted).at[2:2 + 2 * twos:2].set(taker + shifted)
    return sizes[jax.random.permutation(jax.random.fold_in(rng, 2), amount)]


def centred(own_key, shape, scale, reach, pieces=(), held_as=jnp.bfloat16):
    result = scale * jax.random.normal(own_key, shape, jnp.float32)
    if pieces:
        result = result * steps_of(own_key, shape, pieces, -0.22, 0.18)
    return jnp.clip(result, -reach, reach).astype(held_as)


def setup_inputs(seed: int = 0) -> dict:
    arg_keys = jax.random.split(jax.random.key(seed), 8)
    return {
        "hidden_in": draw_hidden_in(jax.random.fold_in(arg_keys[7], 71), 0),
        "lengths": uneven_parts(arg_keys[1], QUERIES, QUERIES * SEQ * 5 // 8, SEQ, 2).astype(jnp.int32),
        "gate_weight": centred(arg_keys[2], (D, FF), D ** -0.5, 0.09375, ((0, 4), (1, 64))),
        "up_weight": centred(arg_keys[3], (D, FF), D ** -0.5, 0.09375, ((0, 4), (1, 64))),
        "down_weight": draw_down_weight(jax.random.fold_in(arg_keys[7], 71), 0),
        "code_weight": draw_code_weight(jax.random.fold_in(arg_keys[7], 71), 0),
        "corpus_codes": draw_corpus_codes(jax.random.fold_in(arg_keys[7], 71), 0),
    }


epsilon = 1e-05

def keep_best(first, second):
    return lax.top_k(jnp.concatenate([first, second], axis=1), TOPK)[0]

def reference(hidden_in, lengths, gate_weight, up_weight, down_weight, code_weight, corpus_codes):
    widened = hidden_in.astype(jnp.float32)
    normed = (widened * lax.rsqrt(lax.optimization_barrier(jnp.mean(widened * widened, axis=1, keepdims=True)) + epsilon)).astype(jnp.bfloat16)
    gate_sum = jnp.dot(normed, gate_weight, preferred_element_type=jnp.float32)
    up_sum = jnp.dot(normed, up_weight, preferred_element_type=jnp.float32)
    hidden_units = (jax.nn.silu(gate_sum) * up_sum).astype(jnp.bfloat16)
    branch_out = jnp.dot(hidden_units, down_weight, preferred_element_type=jnp.float32)
    residual = widened + branch_out
    final_rows = residual * lax.rsqrt(lax.optimization_barrier(jnp.mean(residual * residual, axis=1, keepdims=True)) + epsilon)
    grouped = final_rows.reshape(QUERIES, SEQ, D)
    valid_mask = (jnp.arange(SEQ, dtype=jnp.int32)[None, :] < lengths[:, None]).astype(jnp.float32)
    pooled = lax.optimization_barrier(jnp.sum(grouped * valid_mask[:, :, None], axis=1)) / lengths[:, None].astype(jnp.float32)
    pooled = pooled.astype(jnp.bfloat16)
    query_codes = jnp.dot(pooled, code_weight, preferred_element_type=jnp.float32).astype(jnp.bfloat16)
    scale = 1.0 / math.sqrt(BITS)
    shards = corpus_codes.reshape(DOCS // DOCS_DEV, DOCS_DEV, BITS)

    def visit(carry, shard_codes):
        scores = lax.dot_general(query_codes, shard_codes, (((1,), (1,)), ((), ())), preferred_element_type=jnp.float32) * scale
        return (keep_best(carry, scores), None)
    start_best = jnp.full((QUERIES, TOPK), -1e+30, jnp.float32)
    top_scores, unused = lax.scan(visit, start_best, shards)
    return top_scores
```

```python
import math

import jax
import jax.numpy as jnp
from jax import lax
from jax.experimental import pallas as pl
from jax.experimental.pallas import tpu as pltpu
from jax.sharding import Mesh
from jax.sharding import PartitionSpec as P

D = 4096
SEQ = 32
TOPK = 100
Z = ("zh", "zb")
XZ = ("x", "zh", "zb")
YXZ = ("y", "x", "zh", "zb")
CORPUS = ("x", "zh", "zb", "k")
QUERY_CORPUS = ("y", "x", "zh", "zb", "k")
EPS = 1e-05
F32 = jnp.float32
BF16 = jnp.bfloat16
PARAMS = pltpu.CompilerParams(vmem_limit_bytes=32 * 1024 * 1024)
VMEM = pl.BlockSpec(memory_space=pltpu.VMEM)
SMEM = pl.BlockSpec(memory_space=pltpu.SMEM)


def shape(dims, dtype):
    return jax.ShapeDtypeStruct(dims, dtype)


def to_peer(x):
    return lax.ppermute(x, "k", [(0, 1), (1, 0)])


def shifted(x, d):
    return lax.ppermute(x, "y", [(i, (i + d) % 4) for i in range(4)])


def spread(x, axes, peers):
    copies = jnp.broadcast_to(x[None], (peers, *x.shape))
    return lax.all_to_all(copies, axes, 0, 0, tiled=True)


def lanes(like):
    return lax.broadcasted_iota(jnp.int32, like, 1)


def gate_up_kernel(place, h, g0, u0, g1, u1, o0, o1, o2, o3, lhs, wide):
    y = place[0]
    for d in range(4):
        i = (y + d) % 4
        for z in range(8):
            lhs[d * 64 : d * 64 + 64, z * 128 : z * 128 + 128] = h[i * 8 + z]
    left = lhs[...]
    widened = left.astype(F32)
    sq = jnp.sum(widened * widened, axis=1, keepdims=True)
    top = sq.astype(BF16).astype(F32)
    mid = (sq - top).astype(BF16).astype(F32)
    low = sq - top - mid
    col = lanes((256, 256))
    wide[...] = jnp.zeros((256, 256), F32)
    for b, w in enumerate((g0, u0, g1, u1)):
        wide[:, 0:224] = jnp.dot(left, w[...], preferred_element_type=F32)
        block = wide[...]
        if b == 0:
            block = jnp.where(col == 224, top, block)
            block = jnp.where(col == 225, mid, block)
            block = jnp.where(col == 226, low, block)
        block = block.astype(BF16)
        for d, o in enumerate((o0, o1, o2, o3)):
            o[:, b * 256 : b * 256 + 256] = block[d * 64 : d * 64 + 64]


def gate_up(place, h, g0, u0, g1, u1):
    part = shape((64, 1024), BF16)
    return pl.pallas_call(
        gate_up_kernel,
        out_shape=(part,) * 4,
        in_specs=[SMEM] + [VMEM] * 5,
        out_specs=(VMEM,) * 4,
        scratch_shapes=[pltpu.VMEM((256, 1024), BF16), pltpu.VMEM((256, 256), F32)],
        compiler_params=PARAMS,
        name="gate_up",
    )(place, h, g0, u0, g1, u1)


def hidden_kernel(a, b, c, d, out):
    total = a[...].astype(F32) + b[...].astype(F32) + c[...].astype(F32) + d[...].astype(F32)
    col = lanes((64, 256))
    first = total[:, 0:256]
    sq = jnp.sum(jnp.where((col >= 224) & (col < 227), first, 0.0), axis=1, keepdims=True)
    r = lax.rsqrt(sq / D + EPS)
    for b in range(2):
        gate = total[:, b * 512 : b * 512 + 256] * r
        up = total[:, b * 512 + 256 : b * 512 + 512] * r
        units = gate / (1.0 + jnp.exp(-gate)) * up
        out[:, b * 256 : b * 256 + 256] = jnp.where(col < 224, units, 0.0).astype(BF16)


def hidden_of(a, b, c, d):
    return pl.pallas_call(
        hidden_kernel,
        out_shape=shape((64, 512), BF16),
        in_specs=[VMEM] * 4,
        out_specs=VMEM,
        compiler_params=PARAMS,
        name="hidden_units",
    )(a, b, c, d)


def down_kernel(place, a, b, c, d, w0, w1, out, lhs):
    y = place[0]
    for s, part in enumerate((a, b, c, d)):
        at = pl.multiple_of(((y - s + 4) % 4) * 64, 64)
        lhs[pl.ds(at, 64), :] = part[...]
    total = jnp.dot(lhs[:, 0:224], w0[...], preferred_element_type=F32)
    total += jnp.dot(lhs[:, 256:480], w1[...], preferred_element_type=F32)
    out[...] = total.astype(BF16)


def down(place, parts, w0, w1):
    return pl.pallas_call(
        down_kernel,
        out_shape=shape((256, 1024), BF16),
        in_specs=[SMEM] + [VMEM] * 6,
        out_specs=VMEM,
        scratch_shapes=[pltpu.VMEM((256, 512), BF16)],
        compiler_params=PARAMS,
        name="down",
    )(place, *parts, w0, w1)


def residual_kernel(parts, h, res, sq):
    total = h[...].astype(F32)
    for p in range(32):
        total += parts[p].astype(F32)
    res[...] = total
    sq[...] = jnp.broadcast_to(jnp.sum(total * total, axis=1, keepdims=True), (8, 128))


def residual_of(parts, h):
    return pl.pallas_call(
        residual_kernel,
        out_shape=(shape((8, 1024), F32), shape((8, 128), F32)),
        in_specs=[VMEM] * 2,
        out_specs=(VMEM,) * 2,
        compiler_params=PARAMS,
        name="residual",
    )(parts, h)


def pool_kernel(place, length, res, a, b, c, d, keep, send):
    k, first = place[1], place[2]
    sq = (a[...] + b[...] + c[...] + d[...])[:, 0:1]
    rows = lax.broadcasted_iota(jnp.int32, (8, 1), 0) + first
    count = length[0]
    weight = jnp.where(rows < count, lax.rsqrt(sq / D + EPS), 0.0)
    pooled = jnp.sum(res[...] * weight, axis=0, keepdims=True) / count.astype(F32)
    low, high = pooled[:, 0:512], pooled[:, 512:1024]
    keep[...] = jnp.where(k == 0, low, high)
    send[...] = jnp.where(k == 0, high, low)


def pool(place, length, res, sqs):
    half = shape((1, 512), F32)
    return pl.pallas_call(
        pool_kernel,
        out_shape=(half, half),
        in_specs=[SMEM] * 2 + [VMEM] * 5,
        out_specs=(VMEM,) * 2,
        compiler_params=PARAMS,
        name="pool",
    )(place, length, res, *sqs)


def code_kernel(place, a, b, w, keep, send):
    k = place[1]
    pooled = a[...] + b[...]
    top = pooled.astype(BF16).astype(F32)
    row = lax.broadcasted_iota(jnp.int32, (8, 512), 0)
    left = jnp.where(row == 0, top, jnp.where(row == 1, pooled - top, 0.0)).astype(BF16)
    both = jnp.dot(left, w[...], preferred_element_type=F32)
    part = both[0:1] + both[1:2]
    low, high = part[:, 0:512], part[:, 512:1024]
    keep[...] = jnp.where(k == 0, low, high)
    send[...] = jnp.where(k == 0, high, low)


def code_part(place, a, b, w):
    half = shape((1, 512), F32)
    return pl.pallas_call(
        code_kernel,
        out_shape=(half, half),
        in_specs=[SMEM] + [VMEM] * 3,
        out_specs=(VMEM,) * 2,
        compiler_params=PARAMS,
        name="code_part",
    )(place, a, b, w)


def exchange(x, step, falling):
    col = lanes(x.shape)
    upper = (col & step) != 0
    other = jnp.where(upper, pltpu.roll(x, step, 1), pltpu.roll(x, 128 - step, 1))
    return jnp.where(upper ^ falling, jnp.maximum(x, other), jnp.minimum(x, other))


def bitonic_merge(x, falling):
    for step in (64, 32, 16, 8, 4, 2, 1):
        x = exchange(x, step, falling)
    return x


def bitonic_sort(x, falling):
    col = lanes(x.shape)
    for size in (2, 4, 8, 16, 32, 64, 128):
        way = falling if size == 128 else falling ^ ((col & size) != 0)
        step = size // 2
        while step:
            x = exchange(x, step, way)
            step //= 2
    return x


def rows_of(like):
    return lax.broadcasted_iota(jnp.int32, like, 0)


def score_kernel(place, mine, theirs, docs, keep, send, *, scale):
    k = place[1]
    own, peer = mine[...], theirs[...]
    low = jnp.where(k == 0, own, peer)
    high = jnp.where(k == 0, peer, own)
    dims = (((1,), (1,)), ((), ()))
    scores = lax.dot_general(low, docs[:, 0:512], dims, preferred_element_type=F32)
    scores += lax.dot_general(high, docs[:, 512:1024], dims, preferred_element_type=F32)
    scores = scores * scale
    x = jnp.concatenate([scores[:, c * 128 : c * 128 + 128] for c in range(4)], axis=0)
    x = bitonic_sort(x, rows_of((64, 128)) < 32)
    x = jnp.maximum(x[0:32], x[32:64])
    x = bitonic_merge(x, rows_of((32, 128)) < 16)
    x = jnp.maximum(x[0:16], x[16:32])
    kept = (rows_of((16, 128)) // 8) == k
    x = bitonic_merge(x, kept)
    keep[...] = jnp.where(k == 0, x[0:8], x[8:16])
    send[...] = jnp.where(k == 0, x[8:16], x[0:8])


def local_lists(place, mine, theirs, docs):
    half = shape((8, 128), F32)

    def body(*refs):
        score_kernel(*refs, scale=1.0 / math.sqrt(docs.shape[1]))

    return pl.pallas_call(
        body,
        out_shape=(half, half),
        in_specs=[SMEM] + [VMEM] * 3,
        out_specs=(VMEM,) * 2,
        compiler_params=PARAMS,
        name="scores",
    )(place, mine, theirs, docs)


def pair_kernel(place, a, b, o0, o1, o2, o3, held):
    y = place[0]
    x = jnp.maximum(a[...], b[...])
    turn = (rows_of((8, 128)) // 2 - y + 4) % 4
    held[...] = bitonic_merge(x, turn % 2 == 0)
    for d, o in enumerate((o0, o1, o2, o3)):
        q = (y + d) % 4
        for r in range(2):
            o[r : r + 1, :] = held[pl.ds(q * 2 + r, 1), :]


def pair_lists(place, a, b):
    two = shape((2, 128), F32)
    return pl.pallas_call(
        pair_kernel,
        out_shape=(two,) * 4,
        in_specs=[SMEM] + [VMEM] * 2,
        out_specs=(VMEM,) * 4,
        scratch_shapes=[pltpu.VMEM((8, 128), F32)],
        compiler_params=PARAMS,
        name="pair_lists",
    )(place, a, b)


def four_kernel(place, a, b, c, d, out, held):
    odd = place[3]
    held[0:2] = jnp.maximum(a[...], b[...])
    held[2:4] = jnp.maximum(c[...], d[...])
    held[4:8] = jnp.zeros((4, 128), F32)
    x = bitonic_merge(held[...], rows_of((8, 128)) < 2)
    held[...] = x
    held[0:2] = jnp.maximum(held[0:2], held[2:4])
    x = bitonic_merge(held[...], (rows_of((8, 128)) * 0 + odd) == 0)
    held[...] = x
    for p in range(128):
        out[p] = held[0:2]


def four_lists(place, lists):
    return pl.pallas_call(
        four_kernel,
        out_shape=shape((128, 2, 128), F32),
        in_specs=[SMEM] + [VMEM] * 4,
        out_specs=VMEM,
        scratch_shapes=[pltpu.VMEM((8, 128), F32)],
        compiler_params=PARAMS,
        name="four_lists",
    )(place, *lists)


def final_kernel(x_ref, out):
    x = x_ref[...]
    lists = 32
    while lists > 1:
        x = x.reshape(lists // 2, 2, 8, 128)
        x = jnp.maximum(x[:, 0], x[:, 1])
        lists //= 2
        x = x.reshape(lists * 8, 128)
        falling = (rows_of(x.shape) // 8) % 2 == 0
        x = bitonic_merge(x, falling)
    out[...] = x


def final_lists(x):
    return pl.pallas_call(
        final_kernel,
        out_shape=shape((8, 128), F32),
        in_specs=[VMEM],
        out_specs=VMEM,
        compiler_params=PARAMS,
        name="final_lists",
    )(x)


def per_device(hidden_in, lengths, gate_weight, up_weight, down_weight, code_weight, corpus_codes):
    y, x, zh, zb, k = (lax.axis_index(a) for a in QUERY_CORPUS)
    place = jnp.stack([y, k, 16 * k + 8 * zb, zb]).astype(jnp.int32)

    halves = hidden_in.reshape(4, 2, 16, 64)
    first, second = halves[:, 0].reshape(64, 64), halves[:, 1].reshape(64, 64)
    counts = jnp.broadcast_to(jnp.repeat(lengths.astype(BF16), 4)[:, None], (16, 64))
    own = jnp.concatenate([jnp.where(k == 0, first, second), counts], axis=0)
    other = jnp.where(k == 0, second, first)
    swap = [(a * 4 + b, b * 4 + a) for a in range(4) for b in range(4)]
    straight = [(s * 2 + c, t * 2 + c) for s, t in swap for c in range(2)]
    crossed = [(s * 2 + c, t * 2 + 1 - c) for s, t in swap for c in range(2)]
    own = lax.ppermute(own, ("y", "x", "k"), straight)
    other = lax.ppermute(other, ("y", "x", "k"), crossed)
    length = lax.dynamic_slice(own[:, 0], (64 + 4 * zh,), (1,)).astype(jnp.int32)
    own = own[:64]
    block = jnp.where(
        k == 0, jnp.concatenate([own, other], axis=1), jnp.concatenate([other, own], axis=1)
    )
    gathered = spread(block, XZ, 32)

    gate_peer, up_peer, down_peer = (to_peer(w) for w in (gate_weight, up_weight, down_weight))

    moves = []
    for i in range(4):
        for j in range(4):
            for z in range(8):
                for c in range(2):
                    source = ((i * 4 + j) * 8 + z) * 2 + c
                    target = ((j * 4 + i) * 8 + (z % 4) * 2 + c) * 2 + z // 4
                    moves.append((source, target))
    code_rows = lax.ppermute(code_weight, QUERY_CORPUS, moves)
    code_rows = lax.all_gather(code_rows, Z, axis=0, tiled=True)

    parts = gate_up(place, gathered, gate_weight, up_weight, gate_peer, up_peer)
    units = hidden_of(parts[0], *(shifted(parts[d], d) for d in (1, 2, 3)))
    groups = (units, *(shifted(units, d) for d in (1, 2, 3)))
    branch = down(place, groups, down_weight, down_peer)
    branch = lax.all_to_all(branch.reshape(32, 8, 1024), XZ, 0, 0, tiled=True)
    here = lax.dynamic_slice(
        gathered.reshape(4, 8, 64, 128), (x, 0, zh * 16 + zb * 8, 0), (1, 8, 8, 128)
    )[0]
    here = jnp.moveaxis(here, 0, 1).reshape(8, 1024)
    res, sq = residual_of(branch, here)
    sqs = (sq, *(shifted(sq, d) for d in (1, 2, 3)))
    keep, send = pool(place, length, res, sqs)
    keep, send = code_part(place, keep, to_peer(send), code_rows)
    part = (keep + to_peer(send)).reshape(4, 128)
    codes = spread(part, YXZ, 128).reshape(4, 4, 4, 2, 512).sum(axis=(0, 3))
    codes = codes.reshape(16, 512).astype(BF16)

    keep, send = local_lists(place, codes, to_peer(codes), corpus_codes)
    lists = pair_lists(place, keep, to_peer(send))
    lists = (lists[0], *(shifted(lists[d], d) for d in (1, 2, 3)))
    lists = four_lists(place, lists)
    arrived = lax.all_to_all(lists, YXZ, 0, 0, tiled=True)
    arrived = jnp.moveaxis(arrived.reshape(4, 32, 2, 128), 0, 1).reshape(256, 128)
    best = final_lists(arrived)
    peer = to_peer(best)
    best = jnp.where(
        k == 0, jnp.concatenate([best, peer], axis=0), jnp.concatenate([peer, best], axis=0)
    )
    return best[:, :TOPK]


def solution(mesh):
    split = Mesh(mesh.devices.reshape(4, 4, 4, 2, 2), QUERY_CORPUS)
    return jax.shard_map(
        per_device,
        mesh=split,
        in_specs=(
            P("y", CORPUS),
            P("y"),
            P("y", CORPUS),
            P("y", CORPUS),
            P(CORPUS, "y"),
            P(CORPUS, None),
            P(QUERY_CORPUS, None),
        ),
        out_specs=P(),
        check_vma=False,
    )
```

```python
import math

import jax
import jax.numpy as jnp
from jax import lax
from jax.experimental import pallas as pl
from jax.experimental.pallas import tpu as pltpu
from jax.sharding import Mesh
from jax.sharding import PartitionSpec as P

D = 4096
SEQ = 32
TOPK = 100
Z = ("zh", "zb")
XZ = ("x", "zh", "zb")
YXZ = ("y", "x", "zh", "zb")
CORPUS = ("x", "zh", "zb", "k")
QUERY_CORPUS = ("y", "x", "zh", "zb", "k")
EPS = 1e-05
F32 = jnp.float32
BF16 = jnp.bfloat16
PARAMS = pltpu.CompilerParams(vmem_limit_bytes=32 * 1024 * 1024)
VMEM = pl.BlockSpec(memory_space=pltpu.VMEM)
SMEM = pl.BlockSpec(memory_space=pltpu.SMEM)


def shape(dims, dtype):
    return jax.ShapeDtypeStruct(dims, dtype)


def to_peer(x):
    return lax.ppermute(x, "k", [(0, 1), (1, 0)])


def shifted(x, d):
    return lax.ppermute(x, "y", [(i, (i + d) % 4) for i in range(4)])


def spread(x, axes, peers):
    copies = jnp.broadcast_to(x[None], (peers, *x.shape))
    return lax.all_to_all(copies, axes, 0, 0, tiled=True)


def lanes(like):
    return lax.broadcasted_iota(jnp.int32, like, 1)


def gate_up_kernel(place, h, g0, u0, g1, u1, o0, o1, o2, o3, lhs, wide):
    y = place[0]
    for d in range(4):
        i = (y + d) % 4
        for z in range(8):
            lhs[d * 64 : d * 64 + 64, z * 128 : z * 128 + 128] = h[i * 8 + z]
    left = lhs[...]
    widened = left.astype(F32)
    sq = jnp.sum(widened * widened, axis=1, keepdims=True)
    top = sq.astype(BF16).astype(F32)
    mid = (sq - top).astype(BF16).astype(F32)
    low = sq - top - mid
    col = lanes((256, 256))
    wide[...] = jnp.zeros((256, 256), F32)
    for b, w in enumerate((g0, u0, g1, u1)):
        wide[:, 0:224] = lax.dot_general(
            left, w[...], (((1,), (1,)), ((), ())), preferred_element_type=F32
        )
        block = wide[...]
        if b == 0:
            block = jnp.where(col == 224, top, block)
            block = jnp.where(col == 225, mid, block)
            block = jnp.where(col == 226, low, block)
        block = block.astype(BF16)
        for d, o in enumerate((o0, o1, o2, o3)):
            o[:, b * 256 : b * 256 + 256] = block[d * 64 : d * 64 + 64]


def gate_up(place, h, g0, u0, g1, u1):
    part = shape((64, 1024), BF16)
    return pl.pallas_call(
        gate_up_kernel,
        out_shape=(part,) * 4,
        in_specs=[SMEM] + [VMEM] * 5,
        out_specs=(VMEM,) * 4,
        scratch_shapes=[pltpu.VMEM((256, 1024), BF16), pltpu.VMEM((256, 256), F32)],
        compiler_params=PARAMS,
        name="gate_up",
    )(place, h, g0, u0, g1, u1)


def hidden_kernel(a, b, c, d, out):
    total = a[...].astype(F32) + b[...].astype(F32) + c[...].astype(F32) + d[...].astype(F32)
    col = lanes((64, 256))
    first = total[:, 0:256]
    sq = jnp.sum(jnp.where((col >= 224) & (col < 227), first, 0.0), axis=1, keepdims=True)
    r = lax.rsqrt(sq / D + EPS)
    for b in range(2):
        gate = total[:, b * 512 : b * 512 + 256] * r
        up = total[:, b * 512 + 256 : b * 512 + 512] * r
        units = gate / (1.0 + jnp.exp(-gate)) * up
        out[:, b * 256 : b * 256 + 256] = jnp.where(col < 224, units, 0.0).astype(BF16)


def hidden_of(a, b, c, d):
    return pl.pallas_call(
        hidden_kernel,
        out_shape=shape((64, 512), BF16),
        in_specs=[VMEM] * 4,
        out_specs=VMEM,
        compiler_params=PARAMS,
        name="hidden_units",
    )(a, b, c, d)


def down_kernel(place, a, b, c, d, w0, w1, out, lhs):
    y = place[0]
    for s, part in enumerate((a, b, c, d)):
        at = pl.multiple_of(((y - s + 4) % 4) * 64, 64)
        lhs[pl.ds(at, 64), :] = part[...]
    total = jnp.dot(lhs[:, 0:224], w0[...], preferred_element_type=F32)
    total += jnp.dot(lhs[:, 256:480], w1[...], preferred_element_type=F32)
    out[...] = total.astype(BF16)


def down(place, parts, w0, w1):
    return pl.pallas_call(
        down_kernel,
        out_shape=shape((256, 1024), BF16),
        in_specs=[SMEM] + [VMEM] * 6,
        out_specs=VMEM,
        scratch_shapes=[pltpu.VMEM((256, 512), BF16)],
        compiler_params=PARAMS,
        name="down",
    )(place, *parts, w0, w1)


def residual_kernel(parts, h, res, sq):
    total = h[...].astype(F32)
    for p in range(32):
        total += parts[p].astype(F32)
    res[...] = total
    sq[...] = jnp.broadcast_to(jnp.sum(total * total, axis=1, keepdims=True), (8, 128))


def residual_of(parts, h):
    return pl.pallas_call(
        residual_kernel,
        out_shape=(shape((8, 1024), F32), shape((8, 128), F32)),
        in_specs=[VMEM] * 2,
        out_specs=(VMEM,) * 2,
        compiler_params=PARAMS,
        name="residual",
    )(parts, h)


def pool_kernel(place, counts, res, a, b, c, d, keep, send):
    k, first, row = place[1], place[2], place[4]
    sq = (a[...] + b[...] + c[...] + d[...])[:, 0:1]
    slots = lax.broadcasted_iota(jnp.int32, (8, 1), 0) + first
    held = counts[...].astype(F32)
    held = jnp.where(lax.broadcasted_iota(jnp.int32, (16, 64), 0) == row, held, 0.0)
    count = jnp.max(jnp.max(held, axis=1, keepdims=True), axis=0, keepdims=True)
    weight = jnp.where(slots.astype(F32) < count, lax.rsqrt(sq / D + EPS), 0.0)
    pooled = jnp.sum(res[...] * weight, axis=0, keepdims=True) / count
    low = lanes((1, 128)) < 64
    for t in range(4):
        one = pooled[:, t * 256 : t * 256 + 128]
        two = pooled[:, t * 256 + 128 : t * 256 + 256]
        even = jnp.where(low, one, pltpu.roll(two, 64, 1))
        odd = jnp.where(low, pltpu.roll(one, 64, 1), two)
        keep[:, t * 128 : t * 128 + 128] = jnp.where(k == 0, even, odd)
        send[:, t * 128 : t * 128 + 128] = jnp.where(k == 0, odd, even)


def pool(place, counts, res, sqs):
    half = shape((1, 512), F32)
    return pl.pallas_call(
        pool_kernel,
        out_shape=(half, half),
        in_specs=[SMEM] + [VMEM] * 6,
        out_specs=(VMEM,) * 2,
        compiler_params=PARAMS,
        name="pool",
    )(place, counts, res, *sqs)


def code_kernel(place, a, b, w, keep, send):
    k = place[1]
    pooled = a[...] + b[...]
    top = pooled.astype(BF16).astype(F32)
    row = lax.broadcasted_iota(jnp.int32, (8, 512), 0)
    left = jnp.where(row == 0, top, jnp.where(row == 1, pooled - top, 0.0)).astype(BF16)
    both = jnp.dot(left, w[...], preferred_element_type=F32)
    part = both[0:1] + both[1:2]
    low, high = part[:, 0:512], part[:, 512:1024]
    keep[...] = jnp.where(k == 0, low, high)
    send[...] = jnp.where(k == 0, high, low)


def code_part(place, a, b, w):
    half = shape((1, 512), F32)
    return pl.pallas_call(
        code_kernel,
        out_shape=(half, half),
        in_specs=[SMEM] + [VMEM] * 3,
        out_specs=(VMEM,) * 2,
        compiler_params=PARAMS,
        name="code_part",
    )(place, a, b, w)


def exchange(x, step, falling):
    col = lanes(x.shape)
    upper = (col & step) != 0
    other = jnp.where(upper, pltpu.roll(x, step, 1), pltpu.roll(x, 128 - step, 1))
    return jnp.where(upper ^ falling, jnp.maximum(x, other), jnp.minimum(x, other))


def bitonic_merge(x, falling):
    for step in (64, 32, 16, 8, 4, 2, 1):
        x = exchange(x, step, falling)
    return x


def bitonic_sort(x, falling):
    col = lanes(x.shape)
    for size in (2, 4, 8, 16, 32, 64, 128):
        way = falling if size == 128 else falling ^ ((col & size) != 0)
        step = size // 2
        while step:
            x = exchange(x, step, way)
            step //= 2
    return x


def rows_of(like):
    return lax.broadcasted_iota(jnp.int32, like, 0)


def score_kernel(place, mine, theirs, docs, lists, *, scale):
    k = place[1]
    own, peer = mine[...], theirs[...]
    low = jnp.where(k == 0, own, peer)
    high = jnp.where(k == 0, peer, own)
    dims = (((1,), (1,)), ((), ()))
    scores = lax.dot_general(low, docs[:, 0:512], dims, preferred_element_type=F32)
    scores += lax.dot_general(high, docs[:, 512:1024], dims, preferred_element_type=F32)
    scores = scores * scale
    x = jnp.concatenate([scores[:, c * 128 : c * 128 + 128] for c in range(4)], axis=0)
    x = bitonic_sort(x, rows_of((64, 128)) < 32)
    x = jnp.maximum(x[0:32], x[32:64])
    x = bitonic_merge(x, rows_of((32, 128)) < 16)
    x = jnp.maximum(x[0:16], x[16:32])
    lists[...] = bitonic_merge(x, rows_of((16, 128)) * 0 + k == 0)


def local_lists(place, mine, theirs, docs):
    def body(*refs):
        score_kernel(*refs, scale=1.0 / math.sqrt(docs.shape[1]))

    return pl.pallas_call(
        body,
        out_shape=shape((16, 128), F32),
        in_specs=[SMEM] + [VMEM] * 3,
        out_specs=VMEM,
        compiler_params=PARAMS,
        name="scores",
    )(place, mine, theirs, docs)


def pair_kernel(place, a, b, o0, o1, o2, o3, held):
    y = place[0]
    x = jnp.maximum(a[...], b[...])
    turn = (rows_of((16, 128)) // 4 - y + 4) % 4
    held[...] = bitonic_merge(x, turn % 2 == 0)
    for d, o in enumerate((o0, o1, o2, o3)):
        o[...] = held[pl.ds(pl.multiple_of(((y + d) % 4) * 4, 4), 4), :]


def pair_lists(place, a, b):
    four = shape((4, 128), F32)
    return pl.pallas_call(
        pair_kernel,
        out_shape=(four,) * 4,
        in_specs=[SMEM] + [VMEM] * 2,
        out_specs=(VMEM,) * 4,
        scratch_shapes=[pltpu.VMEM((16, 128), F32)],
        compiler_params=PARAMS,
        name="pair_lists",
    )(place, a, b)


def four_kernel(place, a, b, c, d, out):
    odd = place[3]
    x = jnp.concatenate(
        [jnp.maximum(a[...], b[...]), jnp.maximum(c[...], d[...])], axis=0
    )
    x = bitonic_merge(x, rows_of((8, 128)) < 4)
    x = jnp.maximum(x, pltpu.roll(x, 4, 0))
    x = bitonic_merge(x, (rows_of((8, 128)) * 0 + odd) == 0)
    out[...] = jnp.broadcast_to(x[0:4][None], (128, 4, 128))


def four_lists(place, lists):
    return pl.pallas_call(
        four_kernel,
        out_shape=shape((128, 4, 128), F32),
        in_specs=[SMEM] + [VMEM] * 4,
        out_specs=VMEM,
        compiler_params=PARAMS,
        name="four_lists",
    )(place, *lists)


def final_kernel(x_ref, out):
    x = x_ref[...]
    for groups in (32, 16, 8, 4):
        x = x.reshape(groups, 2, 8, 128)
        x = jnp.maximum(x[:, 0], x[:, 1]).reshape(groups * 8, 128)
        row = rows_of(x.shape)
        x = bitonic_merge(x, row % 8 < 4 if groups == 4 else (row // 8) % 2 == 0)
    x = jnp.maximum(x, pltpu.roll(x, 4, 0))
    x = bitonic_merge(x, rows_of(x.shape) >= 0)
    for y in range(4):
        out[y * 4 : y * 4 + 4, :] = x[y * 8 + 4 : y * 8 + 8, 0:TOPK]


def final_lists(x):
    return pl.pallas_call(
        final_kernel,
        out_shape=shape((16, TOPK), F32),
        in_specs=[VMEM],
        out_specs=VMEM,
        compiler_params=PARAMS,
        name="final_lists",
    )(x)


def per_device(hidden_in, lengths, gate_weight, up_weight, down_weight, code_weight, corpus_codes):
    y, x, zh, zb, k = (lax.axis_index(a) for a in QUERY_CORPUS)
    place = jnp.stack([y, k, 16 * k + 8 * zb, zh % 2, 4 * zh]).astype(jnp.int32)

    halves = hidden_in.reshape(4, 2, 16, 64)
    first, second = halves[:, 0].reshape(64, 64), halves[:, 1].reshape(64, 64)
    counts = jnp.broadcast_to(jnp.repeat(lengths.astype(BF16), 4)[:, None], (16, 64))
    own = jnp.concatenate([jnp.where(k == 0, first, second), counts], axis=0)
    other = jnp.where(k == 0, second, first)
    swap = [(a * 4 + b, b * 4 + a) for a in range(4) for b in range(4)]
    straight = [(s * 2 + c, t * 2 + c) for s, t in swap for c in range(2)]
    crossed = [(s * 2 + c, t * 2 + 1 - c) for s, t in swap for c in range(2)]
    own = lax.ppermute(own, ("y", "x", "k"), straight)
    other = lax.ppermute(other, ("y", "x", "k"), crossed)
    counts, own = own[64:], own[:64]
    block = jnp.where(
        k == 0, jnp.concatenate([own, other], axis=1), jnp.concatenate([other, own], axis=1)
    )
    gate_rows, up_rows = gate_weight.T, up_weight.T
    gate_peer, up_peer, down_peer = (to_peer(w) for w in (gate_rows, up_rows, down_weight))
    block, gate_peer, up_peer, down_peer = lax.optimization_barrier(
        (block, gate_peer, up_peer, down_peer)
    )
    gathered = spread(block, XZ, 32)

    code_rows = lax.ppermute(code_weight, ("y", "x"), swap)
    code_rows, gathered = lax.optimization_barrier((code_rows, gathered))
    code_rows = lax.all_gather(code_rows, Z, axis=0, tiled=True)

    parts = gate_up(place, gathered, gate_rows, up_rows, gate_peer, up_peer)
    units = hidden_of(parts[0], *(shifted(parts[d], d) for d in (1, 2, 3)))
    groups = (units, *(shifted(units, d) for d in (1, 2, 3)))
    branch = down(place, groups, down_weight, down_peer)
    branch = lax.all_to_all(branch.reshape(32, 8, 1024), XZ, 0, 0, tiled=True)
    here = lax.dynamic_slice(
        gathered.reshape(4, 8, 64, 128), (x, 0, zh * 16 + zb * 8, 0), (1, 8, 8, 128)
    )[0]
    here = jnp.moveaxis(here, 0, 1).reshape(8, 1024)
    res, sq = residual_of(branch, here)
    sqs = (sq, *(shifted(sq, d) for d in (1, 2, 3)))
    keep, send = pool(place, counts, res, sqs)
    keep, send = code_part(place, keep, to_peer(send), code_rows)
    part = (keep + to_peer(send)).reshape(4, 128)
    codes = spread(part, YXZ, 128).reshape(4, 4, 4, 2, 512).sum(axis=(0, 3))
    codes = codes.reshape(16, 512).astype(BF16)

    lists = local_lists(place, codes, to_peer(codes), corpus_codes)
    lists = pair_lists(place, lists, to_peer(lists))
    lists = (lists[0], *(shifted(lists[d], d) for d in (1, 2, 3)))
    lists = four_lists(place, lists)
    arrived = lax.all_to_all(lists, YXZ, 0, 0, tiled=True)
    return final_lists(arrived.reshape(512, 128))


def solution(mesh):
    split = Mesh(mesh.devices.reshape(4, 4, 4, 2, 2), QUERY_CORPUS)
    return jax.shard_map(
        per_device,
        mesh=split,
        in_specs=(
            P("y", CORPUS),
            P("y"),
            P("y", CORPUS),
            P("y", CORPUS),
            P(CORPUS, "y"),
            P(CORPUS, None),
            P(QUERY_CORPUS, None),
        ),
        out_specs=P(),
        check_vma=False,
    )
```

```python
import math

import jax
import jax.numpy as jnp
from jax import lax
from jax.experimental import pallas as pl
from jax.experimental.pallas import tpu as pltpu
from jax.sharding import Mesh
from jax.sharding import PartitionSpec as P

D = 4096
SEQ = 32
TOPK = 100
Z = ("zh", "zb")
XZ = ("x", "zh", "zb")
YXZ = ("y", "x", "zh", "zb")
CORPUS = ("x", "zh", "zb", "k")
QUERY_CORPUS = ("y", "x", "zh", "zb", "k")
EPS = 1e-05
F32 = jnp.float32
BF16 = jnp.bfloat16
PARAMS = pltpu.CompilerParams(vmem_limit_bytes=32 * 1024 * 1024)
VMEM = pl.BlockSpec(memory_space=pltpu.VMEM)
SMEM = pl.BlockSpec(memory_space=pltpu.SMEM)


def shape(dims, dtype):
    return jax.ShapeDtypeStruct(dims, dtype)


def to_peer(x):
    return lax.ppermute(x, "k", [(0, 1), (1, 0)])


def shifted(x, d):
    return lax.ppermute(x, "y", [(i, (i + d) % 4) for i in range(4)])


def spread(x, axes, peers):
    copies = jnp.broadcast_to(x[None], (peers, *x.shape))
    return lax.all_to_all(copies, axes, 0, 0, tiled=True)


def lanes(like):
    return lax.broadcasted_iota(jnp.int32, like, 1)


def pack_kernel(place, lengths, h, own, other):
    k = place[1]
    for q in range(4):
        one = h[q * 32 : q * 32 + 16, :]
        two = h[q * 32 + 16 : q * 32 + 32, :]
        own[q * 16 : q * 16 + 16, :] = jnp.where(k == 0, one, two)
        other[q * 16 : q * 16 + 16, :] = jnp.where(k == 0, two, one)
    query = lax.broadcasted_iota(jnp.int32, (16, 64), 0) // 4
    counts = jnp.zeros((16, 64), jnp.int32)
    for q in range(4):
        counts = jnp.where(query == q, lengths[q], counts)
    own[64:80, :] = counts.astype(F32).astype(BF16)


def pack(place, lengths, h):
    return pl.pallas_call(
        pack_kernel,
        out_shape=(shape((80, 64), BF16), shape((64, 64), BF16)),
        in_specs=[SMEM, SMEM, VMEM],
        out_specs=(VMEM,) * 2,
        compiler_params=PARAMS,
        name="pack",
    )(place, lengths, h)


def gate_up_kernel(place, h, g0, u0, g1, u1, o0, o1, o2, o3, lhs, wide):
    y = place[0]
    for d in range(4):
        i = (y + d) % 4
        for z in range(8):
            lhs[d * 64 : d * 64 + 64, z * 128 : z * 128 + 128] = h[i * 8 + z]
    left = lhs[...]
    widened = left.astype(F32)
    sq = jnp.sum(widened * widened, axis=1, keepdims=True)
    top = sq.astype(BF16).astype(F32)
    mid = (sq - top).astype(BF16).astype(F32)
    low = sq - top - mid
    col = lanes((256, 256))
    wide[...] = jnp.zeros((256, 256), F32)
    for b, w in enumerate((g0, u0, g1, u1)):
        wide[:, 0:224] = lax.dot_general(
            left, w[...], (((1,), (1,)), ((), ())), preferred_element_type=F32
        )
        block = wide[...]
        if b == 0:
            block = jnp.where(col == 224, top, block)
            block = jnp.where(col == 225, mid, block)
            block = jnp.where(col == 226, low, block)
        block = block.astype(BF16)
        for d, o in enumerate((o0, o1, o2, o3)):
            o[:, b * 256 : b * 256 + 256] = block[d * 64 : d * 64 + 64]


def gate_up(place, h, g0, u0, g1, u1):
    part = shape((64, 1024), BF16)
    return pl.pallas_call(
        gate_up_kernel,
        out_shape=(part,) * 4,
        in_specs=[SMEM] + [VMEM] * 5,
        out_specs=(VMEM,) * 4,
        scratch_shapes=[pltpu.VMEM((256, 1024), BF16), pltpu.VMEM((256, 256), F32)],
        compiler_params=PARAMS,
        name="gate_up",
    )(place, h, g0, u0, g1, u1)


def hidden_kernel(a, b, c, d, out):
    total = a[...].astype(F32) + b[...].astype(F32) + c[...].astype(F32) + d[...].astype(F32)
    col = lanes((64, 256))
    first = total[:, 0:256]
    sq = jnp.sum(jnp.where((col >= 224) & (col < 227), first, 0.0), axis=1, keepdims=True)
    r = lax.rsqrt(sq / D + EPS)
    for b in range(2):
        gate = total[:, b * 512 : b * 512 + 256] * r
        up = total[:, b * 512 + 256 : b * 512 + 512] * r
        units = gate / (1.0 + jnp.exp(-gate)) * up
        out[:, b * 256 : b * 256 + 256] = jnp.where(col < 224, units, 0.0).astype(BF16)


def hidden_of(a, b, c, d):
    return pl.pallas_call(
        hidden_kernel,
        out_shape=shape((64, 512), BF16),
        in_specs=[VMEM] * 4,
        out_specs=VMEM,
        compiler_params=PARAMS,
        name="hidden_units",
    )(a, b, c, d)


def down_kernel(place, a, b, c, d, w0, w1, out, lhs):
    y = place[0]
    for s, part in enumerate((a, b, c, d)):
        at = pl.multiple_of(((y - s + 4) % 4) * 64, 64)
        lhs[pl.ds(at, 64), :] = part[...]
    total = jnp.dot(lhs[:, 0:224], w0[...], preferred_element_type=F32)
    total += jnp.dot(lhs[:, 256:480], w1[...], preferred_element_type=F32)
    out[...] = total.astype(BF16)


def down(place, parts, w0, w1):
    return pl.pallas_call(
        down_kernel,
        out_shape=shape((256, 1024), BF16),
        in_specs=[SMEM] + [VMEM] * 6,
        out_specs=VMEM,
        scratch_shapes=[pltpu.VMEM((256, 512), BF16)],
        compiler_params=PARAMS,
        name="down",
    )(place, *parts, w0, w1)


def residual_kernel(parts, h, res, sq):
    total = h[...].astype(F32)
    for p in range(32):
        total += parts[p].astype(F32)
    res[...] = total
    sq[...] = jnp.broadcast_to(jnp.sum(total * total, axis=1, keepdims=True), (8, 128))


def residual_of(parts, h):
    return pl.pallas_call(
        residual_kernel,
        out_shape=(shape((8, 1024), F32), shape((8, 128), F32)),
        in_specs=[VMEM] * 2,
        out_specs=(VMEM,) * 2,
        compiler_params=PARAMS,
        name="residual",
    )(parts, h)


def pool_kernel(place, counts, res, a, b, c, d, keep, send):
    k, first, row = place[1], place[2], place[4]
    sq = (a[...] + b[...] + c[...] + d[...])[:, 0:1]
    slots = lax.broadcasted_iota(jnp.int32, (8, 1), 0) + first
    held = counts[...].astype(F32)
    held = jnp.where(lax.broadcasted_iota(jnp.int32, (16, 64), 0) == row, held, 0.0)
    count = jnp.max(jnp.max(held, axis=1, keepdims=True), axis=0, keepdims=True)
    weight = jnp.where(slots.astype(F32) < count, lax.rsqrt(sq / D + EPS), 0.0)
    pooled = jnp.sum(res[...] * weight, axis=0, keepdims=True) / count
    low = lanes((1, 128)) < 64
    for t in range(4):
        one = pooled[:, t * 256 : t * 256 + 128]
        two = pooled[:, t * 256 + 128 : t * 256 + 256]
        even = jnp.where(low, one, pltpu.roll(two, 64, 1))
        odd = jnp.where(low, pltpu.roll(one, 64, 1), two)
        keep[:, t * 128 : t * 128 + 128] = jnp.where(k == 0, even, odd)
        send[:, t * 128 : t * 128 + 128] = jnp.where(k == 0, odd, even)


def pool(place, counts, res, sqs):
    half = shape((1, 512), F32)
    return pl.pallas_call(
        pool_kernel,
        out_shape=(half, half),
        in_specs=[SMEM] + [VMEM] * 6,
        out_specs=(VMEM,) * 2,
        compiler_params=PARAMS,
        name="pool",
    )(place, counts, res, *sqs)


def code_kernel(place, a, b, w0, w1, w2, w3, keep, send, left):
    k, zh = place[1], place[5]
    pooled = a[...] + b[...]
    top = pooled.astype(BF16).astype(F32)
    row = lax.broadcasted_iota(jnp.int32, (8, 512), 0)
    both = jnp.where(row == 0, top, jnp.where(row == 1, pooled - top, 0.0))
    for t in range(4):
        left[t] = both[:, t * 128 : t * 128 + 128]
    total = jnp.zeros((8, 1024), F32)
    for d, w in enumerate((w0, w1, w2, w3)):
        piece = left[(zh - d + 4) % 4].astype(BF16)
        total += jnp.dot(piece, w[...], preferred_element_type=F32)
    part = total[0:1] + total[1:2]
    low, high = part[:, 0:512], part[:, 512:1024]
    keep[...] = jnp.where(k == 0, low, high)
    send[...] = jnp.where(k == 0, high, low)


def code_part(place, a, b, ws):
    half = shape((1, 512), F32)
    return pl.pallas_call(
        code_kernel,
        out_shape=(half, half),
        in_specs=[SMEM] + [VMEM] * 6,
        out_specs=(VMEM,) * 2,
        scratch_shapes=[pltpu.VMEM((4, 8, 128), F32)],
        compiler_params=PARAMS,
        name="code_part",
    )(place, a, b, *ws)


def exchange(x, step, falling):
    col = lanes(x.shape)
    upper = (col & step) != 0
    other = jnp.where(upper, pltpu.roll(x, step, 1), pltpu.roll(x, 128 - step, 1))
    return jnp.where(upper ^ falling, jnp.maximum(x, other), jnp.minimum(x, other))


def bitonic_merge(x, falling):
    for step in (64, 32, 16, 8, 4, 2, 1):
        x = exchange(x, step, falling)
    return x


def bitonic_sort(x, falling):
    col = lanes(x.shape)
    for size in (2, 4, 8, 16, 32, 64, 128):
        way = falling if size == 128 else falling ^ ((col & size) != 0)
        step = size // 2
        while step:
            x = exchange(x, step, way)
            step //= 2
    return x


def rows_of(like):
    return lax.broadcasted_iota(jnp.int32, like, 0)


def score_kernel(place, mine, theirs, docs, lists, *, scale):
    k = place[1]
    own, peer = mine[...], theirs[...]
    low = jnp.where(k == 0, own, peer)
    high = jnp.where(k == 0, peer, own)
    dims = (((1,), (1,)), ((), ()))
    scores = lax.dot_general(low, docs[:, 0:512], dims, preferred_element_type=F32)
    scores += lax.dot_general(high, docs[:, 512:1024], dims, preferred_element_type=F32)
    scores = scores * scale
    x = jnp.concatenate([scores[:, c * 128 : c * 128 + 128] for c in range(4)], axis=0)
    x = bitonic_sort(x, rows_of((64, 128)) < 32)
    x = jnp.maximum(x[0:32], x[32:64])
    x = bitonic_merge(x, rows_of((32, 128)) < 16)
    x = jnp.maximum(x[0:16], x[16:32])
    lists[...] = bitonic_merge(x, rows_of((16, 128)) * 0 + k == 0)


def local_lists(place, mine, theirs, docs):
    def body(*refs):
        score_kernel(*refs, scale=1.0 / math.sqrt(docs.shape[1]))

    return pl.pallas_call(
        body,
        out_shape=shape((16, 128), F32),
        in_specs=[SMEM] + [VMEM] * 3,
        out_specs=VMEM,
        compiler_params=PARAMS,
        name="scores",
    )(place, mine, theirs, docs)


def pair_kernel(place, a, b, o0, o1, o2, o3, held):
    y = place[0]
    x = jnp.maximum(a[...], b[...])
    turn = (rows_of((16, 128)) // 4 - y + 4) % 4
    held[...] = bitonic_merge(x, turn % 2 == 0)
    for d, o in enumerate((o0, o1, o2, o3)):
        o[...] = held[pl.ds(pl.multiple_of(((y + d) % 4) * 4, 4), 4), :]


def pair_lists(place, a, b):
    four = shape((4, 128), F32)
    return pl.pallas_call(
        pair_kernel,
        out_shape=(four,) * 4,
        in_specs=[SMEM] + [VMEM] * 2,
        out_specs=(VMEM,) * 4,
        scratch_shapes=[pltpu.VMEM((16, 128), F32)],
        compiler_params=PARAMS,
        name="pair_lists",
    )(place, a, b)


def four_kernel(place, a, b, c, d, out):
    odd = place[3]
    x = jnp.concatenate(
        [jnp.maximum(a[...], b[...]), jnp.maximum(c[...], d[...])], axis=0
    )
    x = bitonic_merge(x, rows_of((8, 128)) < 4)
    x = jnp.maximum(x, pltpu.roll(x, 4, 0))
    x = bitonic_merge(x, (rows_of((8, 128)) * 0 + odd) == 0)
    out[...] = jnp.broadcast_to(x[0:4][None], (128, 4, 128))


def four_lists(place, lists):
    return pl.pallas_call(
        four_kernel,
        out_shape=shape((128, 4, 128), F32),
        in_specs=[SMEM] + [VMEM] * 4,
        out_specs=VMEM,
        compiler_params=PARAMS,
        name="four_lists",
    )(place, *lists)


def final_kernel(x_ref, out):
    x = x_ref[...]
    for groups in (32, 16, 8, 4):
        x = x.reshape(groups, 2, 8, 128)
        x = jnp.maximum(x[:, 0], x[:, 1]).reshape(groups * 8, 128)
        row = rows_of(x.shape)
        x = bitonic_merge(x, row % 8 < 4 if groups == 4 else (row // 8) % 2 == 0)
    x = jnp.maximum(x, pltpu.roll(x, 4, 0))
    x = bitonic_merge(x, rows_of(x.shape) >= 0)
    for y in range(4):
        out[y * 4 : y * 4 + 4, :] = x[y * 8 + 4 : y * 8 + 8, 0:TOPK]


def final_lists(x):
    return pl.pallas_call(
        final_kernel,
        out_shape=shape((16, TOPK), F32),
        in_specs=[VMEM],
        out_specs=VMEM,
        compiler_params=PARAMS,
        name="final_lists",
    )(x)


def per_device(hidden_in, lengths, gate_weight, up_weight, down_weight, code_weight, corpus_codes):
    y, x, zh, zb, k = (lax.axis_index(a) for a in QUERY_CORPUS)
    place = jnp.stack([y, k, 16 * k + 8 * zb, zh % 2, 4 * zh, zh]).astype(jnp.int32)

    own, other = pack(place, lengths, hidden_in)
    swap = [(a * 4 + b, b * 4 + a) for a in range(4) for b in range(4)]
    straight = [(s * 2 + c, t * 2 + c) for s, t in swap for c in range(2)]
    crossed = [(s * 2 + c, t * 2 + 1 - c) for s, t in swap for c in range(2)]
    own = lax.ppermute(own, ("y", "x", "k"), straight)
    other = lax.ppermute(other, ("y", "x", "k"), crossed)
    counts, own = own[64:], own[:64]
    block = jnp.where(
        k == 0, jnp.concatenate([own, other], axis=1), jnp.concatenate([other, own], axis=1)
    )
    gate_rows, up_rows = gate_weight.T, up_weight.T
    gate_peer, up_peer, down_peer = (to_peer(w) for w in (gate_rows, up_rows, down_weight))
    block, gate_peer, up_peer, down_peer = lax.optimization_barrier(
        (block, gate_peer, up_peer, down_peer)
    )
    gathered = spread(block, XZ, 32)

    rows = lax.ppermute(code_weight, ("y", "x"), swap)
    peer = lax.ppermute(rows, "zb", [(0, 1), (1, 0)])
    rows = jnp.concatenate(
        [jnp.where(zb == 0, rows, peer), jnp.where(zb == 0, peer, rows)], axis=0
    )
    rows, gathered = lax.optimization_barrier((rows, gathered))
    code_rows = (rows, *(lax.ppermute(rows, "zh", [(i, (i + d) % 4) for i in range(4)]) for d in (1, 2, 3)))

    parts = gate_up(place, gathered, gate_rows, up_rows, gate_peer, up_peer)
    units = hidden_of(parts[0], *(shifted(parts[d], d) for d in (1, 2, 3)))
    groups = (units, *(shifted(units, d) for d in (1, 2, 3)))
    branch = down(place, groups, down_weight, down_peer)
    branch = lax.all_to_all(branch.reshape(32, 8, 1024), XZ, 0, 0, tiled=True)
    here = lax.dynamic_slice(
        gathered.reshape(4, 8, 64, 128), (x, 0, zh * 16 + zb * 8, 0), (1, 8, 8, 128)
    )[0]
    here = jnp.moveaxis(here, 0, 1).reshape(8, 1024)
    res, sq = residual_of(branch, here)
    sqs = (sq, *(shifted(sq, d) for d in (1, 2, 3)))
    keep, send = pool(place, counts, res, sqs)
    keep, send = code_part(place, keep, to_peer(send), code_rows)
    part = (keep + to_peer(send)).reshape(4, 128)
    codes = spread(part, YXZ, 128).reshape(4, 4, 4, 2, 512).sum(axis=(0, 3))
    codes = codes.reshape(16, 512).astype(BF16)

    lists = local_lists(place, codes, to_peer(codes), corpus_codes)
    lists = pair_lists(place, lists, to_peer(lists))
    lists = (lists[0], *(shifted(lists[d], d) for d in (1, 2, 3)))
    lists = four_lists(place, lists)
    arrived = lax.all_to_all(lists, YXZ, 0, 0, tiled=True)
    return final_lists(arrived.reshape(512, 128))


def solution(mesh):
    split = Mesh(mesh.devices.reshape(4, 4, 4, 2, 2), QUERY_CORPUS)
    return jax.shard_map(
        per_device,
        mesh=split,
        in_specs=(
            P("y", CORPUS),
            P("y"),
            P("y", CORPUS),
            P("y", CORPUS),
            P(CORPUS, "y"),
            P(CORPUS, None),
            P(QUERY_CORPUS, None),
        ),
        out_specs=P(),
        check_vma=False,
    )
```

```python
import math

import jax
import jax.numpy as jnp
from jax import lax
from jax.experimental import pallas as pl
from jax.experimental.pallas import tpu as pltpu
from jax.sharding import Mesh
from jax.sharding import PartitionSpec as P

D = 4096
SEQ = 32
TOPK = 100
Z = ("zh", "zb")
XZ = ("x", "zh", "zb")
YXZ = ("y", "x", "zh", "zb")
CORPUS = ("x", "zh", "zb", "k")
QUERY_CORPUS = ("y", "x", "zh", "zb", "k")
EPS = 1e-05
F32 = jnp.float32
BF16 = jnp.bfloat16
PARAMS = pltpu.CompilerParams(vmem_limit_bytes=32 * 1024 * 1024)
VMEM = pl.BlockSpec(memory_space=pltpu.VMEM)
SMEM = pl.BlockSpec(memory_space=pltpu.SMEM)


def shape(dims, dtype):
    return jax.ShapeDtypeStruct(dims, dtype)


def to_peer(x):
    return lax.ppermute(x, "k", [(0, 1), (1, 0)])


def shifted(x, d):
    return lax.ppermute(x, "y", [(i, (i + d) % 4) for i in range(4)])


def spread(x, axes, peers):
    copies = jnp.broadcast_to(x[None], (peers, *x.shape))
    return lax.all_to_all(copies, axes, 0, 0, tiled=True)


def lanes(like):
    return lax.broadcasted_iota(jnp.int32, like, 1)


def pack_kernel(place, lengths, h, own, other):
    k = place[1]
    for q in range(4):
        one = h[q * 32 : q * 32 + 16, :]
        two = h[q * 32 + 16 : q * 32 + 32, :]
        own[q * 16 : q * 16 + 16, :] = jnp.where(k == 0, one, two)
        other[q * 16 : q * 16 + 16, :] = jnp.where(k == 0, two, one)
    query = lax.broadcasted_iota(jnp.int32, (16, 64), 0) // 4
    counts = jnp.zeros((16, 64), jnp.int32)
    for q in range(4):
        counts = jnp.where(query == q, lengths[q], counts)
    own[64:80, :] = counts.astype(F32).astype(BF16)


def pack(place, lengths, h):
    return pl.pallas_call(
        pack_kernel,
        out_shape=(shape((80, 64), BF16), shape((64, 64), BF16)),
        in_specs=[SMEM, SMEM, VMEM],
        out_specs=(VMEM,) * 2,
        compiler_params=PARAMS,
        name="pack",
    )(place, lengths, h)


def gate_up_kernel(place, h, g0, u0, g1, u1, o0, o1, o2, o3, lhs, wide):
    y = place[0]
    for d in range(4):
        i = (y + d) % 4
        for z in range(8):
            lhs[d * 64 : d * 64 + 64, z * 128 : z * 128 + 128] = h[i * 8 + z]
    left = lhs[...]
    widened = left.astype(F32)
    sq = jnp.sum(widened * widened, axis=1, keepdims=True)
    top = sq.astype(BF16).astype(F32)
    mid = (sq - top).astype(BF16).astype(F32)
    low = sq - top - mid
    col = lanes((256, 256))
    wide[...] = jnp.zeros((256, 256), F32)
    for b, w in enumerate((g0, u0, g1, u1)):
        wide[:, 0:224] = lax.dot_general(
            left, w[...], (((1,), (1,)), ((), ())), preferred_element_type=F32
        )
        block = wide[...]
        if b == 0:
            block = jnp.where(col == 224, top, block)
            block = jnp.where(col == 225, mid, block)
            block = jnp.where(col == 226, low, block)
        block = block.astype(BF16)
        for d, o in enumerate((o0, o1, o2, o3)):
            o[:, b * 256 : b * 256 + 256] = block[d * 64 : d * 64 + 64]


def gate_up(place, h, g0, u0, g1, u1):
    part = shape((64, 1024), BF16)
    return pl.pallas_call(
        gate_up_kernel,
        out_shape=(part,) * 4,
        in_specs=[SMEM] + [VMEM] * 5,
        out_specs=(VMEM,) * 4,
        scratch_shapes=[pltpu.VMEM((256, 1024), BF16), pltpu.VMEM((256, 256), F32)],
        compiler_params=PARAMS,
        name="gate_up",
    )(place, h, g0, u0, g1, u1)


def hidden_kernel(a, b, c, d, out):
    total = a[...].astype(F32) + b[...].astype(F32) + c[...].astype(F32) + d[...].astype(F32)
    col = lanes((64, 256))
    first = total[:, 0:256]
    sq = jnp.sum(jnp.where((col >= 224) & (col < 227), first, 0.0), axis=1, keepdims=True)
    r = lax.rsqrt(sq / D + EPS)
    for b in range(2):
        gate = total[:, b * 512 : b * 512 + 256] * r
        up = total[:, b * 512 + 256 : b * 512 + 512] * r
        units = gate / (1.0 + jnp.exp(-gate)) * up
        out[:, b * 256 : b * 256 + 256] = jnp.where(col < 224, units, 0.0).astype(BF16)


def hidden_of(a, b, c, d):
    return pl.pallas_call(
        hidden_kernel,
        out_shape=shape((64, 512), BF16),
        in_specs=[VMEM] * 4,
        out_specs=VMEM,
        compiler_params=PARAMS,
        name="hidden_units",
    )(a, b, c, d)


def down_kernel(place, a, b, c, d, w0, w1, out, lhs):
    y = place[0]
    for s, part in enumerate((a, b, c, d)):
        at = pl.multiple_of(((y - s + 4) % 4) * 64, 64)
        lhs[pl.ds(at, 64), :] = part[...]
    total = jnp.dot(lhs[:, 0:224], w0[...], preferred_element_type=F32)
    total += jnp.dot(lhs[:, 256:480], w1[...], preferred_element_type=F32)
    out[...] = total.astype(BF16)


def down(place, parts, w0, w1):
    return pl.pallas_call(
        down_kernel,
        out_shape=shape((256, 1024), BF16),
        in_specs=[SMEM] + [VMEM] * 6,
        out_specs=VMEM,
        scratch_shapes=[pltpu.VMEM((256, 512), BF16)],
        compiler_params=PARAMS,
        name="down",
    )(place, *parts, w0, w1)


def residual_kernel(parts, h, res, sq):
    total = h[...].astype(F32)
    for p in range(32):
        total += parts[p].astype(F32)
    res[...] = total
    sq[...] = jnp.broadcast_to(jnp.sum(total * total, axis=1, keepdims=True), (8, 128))


def residual_of(parts, h):
    return pl.pallas_call(
        residual_kernel,
        out_shape=(shape((8, 1024), F32), shape((8, 128), F32)),
        in_specs=[VMEM] * 2,
        out_specs=(VMEM,) * 2,
        compiler_params=PARAMS,
        name="residual",
    )(parts, h)


def pool_kernel(place, counts, res, a, b, c, d, o0, o1, o2, o3):
    k, first, row, zb = place[1], place[2], place[4], place[6]
    sq = (a[...] + b[...] + c[...] + d[...])[:, 0:1]
    slots = lax.broadcasted_iota(jnp.int32, (8, 1), 0) + first
    held = counts[...].astype(F32)
    held = jnp.where(lax.broadcasted_iota(jnp.int32, (16, 64), 0) == row, held, 0.0)
    count = jnp.max(jnp.max(held, axis=1, keepdims=True), axis=0, keepdims=True)
    weight = jnp.where(slots.astype(F32) < count, lax.rsqrt(sq / D + EPS), 0.0)
    pooled = jnp.sum(res[...] * weight, axis=0, keepdims=True) / count
    ahead = jnp.concatenate([pooled[:, t * 256 : t * 256 + 128] for t in range(4)], axis=0)
    behind = jnp.concatenate([pooled[:, t * 256 + 128 : t * 256 + 256] for t in range(4)], axis=0)
    for r, out in enumerate((o0, o1, o2, o3)):
        part = jnp.where(zb == r // 2, ahead, behind)
        out[...] = jnp.where(k == r % 2, part, pltpu.roll(part, 64, 1))


def pool(place, counts, res, sqs):
    part = shape((4, 128), F32)
    return pl.pallas_call(
        pool_kernel,
        out_shape=(part,) * 4,
        in_specs=[SMEM] + [VMEM] * 6,
        out_specs=(VMEM,) * 4,
        compiler_params=PARAMS,
        name="pool",
    )(place, counts, res, *sqs)


def code_kernel(place, a, b, c, d, w0, w1, w2, w3, keep, send, left):
    k, zh = place[1], place[5]
    left[...] = a[...] + b[...] + c[...] + d[...]
    total = jnp.zeros((8, 1024), F32)
    for s, w in enumerate((w0, w1, w2, w3)):
        piece = jnp.broadcast_to(left[pl.ds((zh - s + 4) % 4, 1), :], (8, 128))
        total += jnp.dot(piece[:, 0:64].astype(BF16), w[...], preferred_element_type=F32)
    low, high = total[0:1, 0:512], total[0:1, 512:1024]
    keep[...] = jnp.where(k == 0, low, high)
    send[...] = jnp.where(k == 0, high, low)


def code_part(place, pieces, ws):
    half = shape((1, 512), F32)
    return pl.pallas_call(
        code_kernel,
        out_shape=(half, half),
        in_specs=[SMEM] + [VMEM] * 8,
        out_specs=(VMEM,) * 2,
        scratch_shapes=[pltpu.VMEM((4, 128), F32)],
        compiler_params=PARAMS,
        name="code_part",
    )(place, *pieces, *ws)


def exchange(x, step, falling):
    col = lanes(x.shape)
    upper = (col & step) != 0
    other = jnp.where(upper, pltpu.roll(x, step, 1), pltpu.roll(x, 128 - step, 1))
    return jnp.where(upper ^ falling, jnp.maximum(x, other), jnp.minimum(x, other))


def bitonic_merge(x, falling):
    for step in (64, 32, 16, 8, 4, 2, 1):
        x = exchange(x, step, falling)
    return x


def bitonic_sort(x, falling):
    col = lanes(x.shape)
    for size in (2, 4, 8, 16, 32, 64, 128):
        way = falling if size == 128 else falling ^ ((col & size) != 0)
        step = size // 2
        while step:
            x = exchange(x, step, way)
            step //= 2
    return x


def rows_of(like):
    return lax.broadcasted_iota(jnp.int32, like, 0)


def score_kernel(place, mine, theirs, docs, lists, *, scale):
    k = place[1]
    own, peer = mine[...], theirs[...]
    low = jnp.where(k == 0, own, peer)
    high = jnp.where(k == 0, peer, own)
    dims = (((1,), (1,)), ((), ()))
    scores = lax.dot_general(low, docs[:, 0:512], dims, preferred_element_type=F32)
    scores += lax.dot_general(high, docs[:, 512:1024], dims, preferred_element_type=F32)
    scores = scores * scale
    x = jnp.concatenate([scores[:, c * 128 : c * 128 + 128] for c in range(4)], axis=0)
    x = bitonic_sort(x, rows_of((64, 128)) < 32)
    x = jnp.maximum(x[0:32], x[32:64])
    x = bitonic_merge(x, rows_of((32, 128)) < 16)
    x = jnp.maximum(x[0:16], x[16:32])
    lists[...] = bitonic_merge(x, rows_of((16, 128)) * 0 + k == 0)


def local_lists(place, mine, theirs, docs):
    def body(*refs):
        score_kernel(*refs, scale=1.0 / math.sqrt(docs.shape[1]))

    return pl.pallas_call(
        body,
        out_shape=shape((16, 128), F32),
        in_specs=[SMEM] + [VMEM] * 3,
        out_specs=VMEM,
        compiler_params=PARAMS,
        name="scores",
    )(place, mine, theirs, docs)


def pair_kernel(place, a, b, o0, o1, o2, o3, held):
    y = place[0]
    x = jnp.maximum(a[...], b[...])
    turn = (rows_of((16, 128)) // 4 - y + 4) % 4
    held[...] = bitonic_merge(x, turn % 2 == 0)
    for d, o in enumerate((o0, o1, o2, o3)):
        o[...] = held[pl.ds(pl.multiple_of(((y + d) % 4) * 4, 4), 4), :]


def pair_lists(place, a, b):
    four = shape((4, 128), F32)
    return pl.pallas_call(
        pair_kernel,
        out_shape=(four,) * 4,
        in_specs=[SMEM] + [VMEM] * 2,
        out_specs=(VMEM,) * 4,
        scratch_shapes=[pltpu.VMEM((16, 128), F32)],
        compiler_params=PARAMS,
        name="pair_lists",
    )(place, a, b)


def four_kernel(place, a, b, c, d, out):
    odd = place[3]
    x = jnp.concatenate(
        [jnp.maximum(a[...], b[...]), jnp.maximum(c[...], d[...])], axis=0
    )
    x = bitonic_merge(x, rows_of((8, 128)) < 4)
    x = jnp.maximum(x, pltpu.roll(x, 4, 0))
    x = bitonic_merge(x, (rows_of((8, 128)) * 0 + odd) == 0)
    out[...] = jnp.broadcast_to(x[0:4][None], (128, 4, 128))


def four_lists(place, lists):
    return pl.pallas_call(
        four_kernel,
        out_shape=shape((128, 4, 128), F32),
        in_specs=[SMEM] + [VMEM] * 4,
        out_specs=VMEM,
        compiler_params=PARAMS,
        name="four_lists",
    )(place, *lists)


def final_kernel(x_ref, out):
    x = x_ref[...]
    for groups in (32, 16, 8, 4):
        x = x.reshape(groups, 2, 8, 128)
        x = jnp.maximum(x[:, 0], x[:, 1]).reshape(groups * 8, 128)
        row = rows_of(x.shape)
        x = bitonic_merge(x, row % 8 < 4 if groups == 4 else (row // 8) % 2 == 0)
    x = jnp.maximum(x, pltpu.roll(x, 4, 0))
    x = bitonic_merge(x, rows_of(x.shape) >= 0)
    for y in range(4):
        out[y * 4 : y * 4 + 4, :] = x[y * 8 + 4 : y * 8 + 8, 0:TOPK]


def final_lists(x):
    return pl.pallas_call(
        final_kernel,
        out_shape=shape((16, TOPK), F32),
        in_specs=[VMEM],
        out_specs=VMEM,
        compiler_params=PARAMS,
        name="final_lists",
    )(x)


def per_device(hidden_in, lengths, gate_weight, up_weight, down_weight, code_weight, corpus_codes):
    y, x, zh, zb, k = (lax.axis_index(a) for a in QUERY_CORPUS)
    place = jnp.stack([y, k, 16 * k + 8 * zb, zh % 2, 4 * zh, zh, zb]).astype(jnp.int32)

    own, other = pack(place, lengths, hidden_in)
    swap = [(a * 4 + b, b * 4 + a) for a in range(4) for b in range(4)]
    straight = [(s * 2 + c, t * 2 + c) for s, t in swap for c in range(2)]
    crossed = [(s * 2 + c, t * 2 + 1 - c) for s, t in swap for c in range(2)]
    own = lax.ppermute(own, ("y", "x", "k"), straight)
    other = lax.ppermute(other, ("y", "x", "k"), crossed)
    counts, own = own[64:], own[:64]
    block = jnp.where(
        k == 0, jnp.concatenate([own, other], axis=1), jnp.concatenate([other, own], axis=1)
    )
    gate_rows, up_rows = gate_weight.T, up_weight.T
    gate_peer, up_peer, down_peer = (to_peer(w) for w in (gate_rows, up_rows, down_weight))
    block, gate_peer, up_peer, down_peer = lax.optimization_barrier(
        (block, gate_peer, up_peer, down_peer)
    )
    gathered = spread(block, XZ, 32)

    rows = lax.ppermute(code_weight, ("y", "x"), swap)
    rows, gathered = lax.optimization_barrier((rows, gathered))
    turned = [[(i, (i + d) % 4) for i in range(4)] for d in range(4)]
    code_rows = (rows, *(lax.ppermute(rows, "zh", turned[d]) for d in (1, 2, 3)))

    parts = gate_up(place, gathered, gate_rows, up_rows, gate_peer, up_peer)
    units = hidden_of(parts[0], *(shifted(parts[d], d) for d in (1, 2, 3)))
    groups = (units, *(shifted(units, d) for d in (1, 2, 3)))
    groups, code_rows = lax.optimization_barrier((groups, code_rows))
    branch = down(place, groups, down_weight, down_peer)
    branch = lax.all_to_all(branch.reshape(32, 8, 1024), XZ, 0, 0, tiled=True)
    here = lax.dynamic_slice(
        gathered.reshape(4, 8, 64, 128), (x, 0, zh * 16 + zb * 8, 0), (1, 8, 8, 128)
    )[0]
    here = jnp.moveaxis(here, 0, 1).reshape(8, 1024)
    res, sq = residual_of(branch, here)
    sqs = (sq, *(shifted(sq, d) for d in (1, 2, 3)))
    mine = pool(place, counts, res, sqs)
    flips = [[(i, i ^ r) for i in range(4)] for r in range(4)]
    pieces = (mine[0], *(lax.ppermute(mine[r], ("zb", "k"), flips[r]) for r in (1, 2, 3)))
    keep, send = code_part(place, pieces, code_rows)
    part = (keep + to_peer(send)).reshape(4, 128)
    codes = spread(part, YXZ, 128).reshape(4, 4, 4, 2, 512).sum(axis=(0, 3))
    codes = codes.reshape(16, 512).astype(BF16)

    lists = local_lists(place, codes, to_peer(codes), corpus_codes)
    lists = pair_lists(place, lists, to_peer(lists))
    lists = (lists[0], *(shifted(lists[d], d) for d in (1, 2, 3)))
    lists = four_lists(place, lists)
    arrived = lax.all_to_all(lists, YXZ, 0, 0, tiled=True)
    return final_lists(arrived.reshape(512, 128))


def solution(mesh):
    split = Mesh(mesh.devices.reshape(4, 4, 4, 2, 2), QUERY_CORPUS)
    return jax.shard_map(
        per_device,
        mesh=split,
        in_specs=(
            P("y", CORPUS),
            P("y"),
            P("y", CORPUS),
            P("y", CORPUS),
            P(CORPUS, "y"),
            P(CORPUS, None),
            P(QUERY_CORPUS, None),
        ),
        out_specs=P(),
        check_vma=False,
    )
```

```python
import math

import jax
import jax.numpy as jnp
from jax import lax
from jax.experimental import pallas as pl
from jax.experimental.pallas import tpu as pltpu
from jax.sharding import Mesh
from jax.sharding import PartitionSpec as P

D = 4096
SEQ = 32
TOPK = 100
Z = ("zh", "zb")
XZ = ("x", "zh", "zb")
YXZ = ("y", "x", "zh", "zb")
CORPUS = ("x", "zh", "zb", "k")
QUERY_CORPUS = ("y", "x", "zh", "zb", "k")
EPS = 1e-05
F32 = jnp.float32
BF16 = jnp.bfloat16
PARAMS = pltpu.CompilerParams(vmem_limit_bytes=32 * 1024 * 1024)
VMEM = pl.BlockSpec(memory_space=pltpu.VMEM)
SMEM = pl.BlockSpec(memory_space=pltpu.SMEM)


def shape(dims, dtype):
    return jax.ShapeDtypeStruct(dims, dtype)


def to_peer(x):
    return lax.ppermute(x, "k", [(0, 1), (1, 0)])


def shifted(x, d):
    return lax.ppermute(x, "y", [(i, (i + d) % 4) for i in range(4)])


def spread(x, axes, peers):
    copies = jnp.broadcast_to(x[None], (peers, *x.shape))
    return lax.all_to_all(copies, axes, 0, 0, tiled=True)


def lanes(like):
    return lax.broadcasted_iota(jnp.int32, like, 1)


def pack_kernel(place, lengths, h, own, other):
    k = place[1]
    for q in range(4):
        one = h[q * 32 : q * 32 + 16, :]
        two = h[q * 32 + 16 : q * 32 + 32, :]
        own[q * 16 : q * 16 + 16, :] = jnp.where(k == 0, one, two)
        other[q * 16 : q * 16 + 16, :] = jnp.where(k == 0, two, one)
    query = lax.broadcasted_iota(jnp.int32, (16, 64), 0) // 4
    counts = jnp.zeros((16, 64), jnp.int32)
    for q in range(4):
        counts = jnp.where(query == q, lengths[q], counts)
    own[64:80, :] = counts.astype(F32).astype(BF16)


def pack(place, lengths, h):
    return pl.pallas_call(
        pack_kernel,
        out_shape=(shape((80, 64), BF16), shape((64, 64), BF16)),
        in_specs=[SMEM, SMEM, VMEM],
        out_specs=(VMEM,) * 2,
        compiler_params=PARAMS,
        name="pack",
    )(place, lengths, h)


def gate_up_kernel(place, h, g0, u0, g1, u1, o0, o1, o2, o3, lhs, wide):
    y = place[0]
    for d in range(4):
        i = (y + d) % 4
        for z in range(8):
            lhs[d * 64 : d * 64 + 64, z * 128 : z * 128 + 128] = h[i * 8 + z]
    left = lhs[...]
    widened = left.astype(F32)
    sq = jnp.sum(widened * widened, axis=1, keepdims=True)
    top = sq.astype(BF16).astype(F32)
    mid = (sq - top).astype(BF16).astype(F32)
    low = sq - top - mid
    col = lanes((256, 256))
    wide[...] = jnp.zeros((256, 256), F32)
    for b, w in enumerate((g0, u0, g1, u1)):
        wide[:, 0:224] = lax.dot_general(
            left, w[...], (((1,), (1,)), ((), ())), preferred_element_type=F32
        )
        block = wide[...]
        if b == 0:
            block = jnp.where(col == 224, top, block)
            block = jnp.where(col == 225, mid, block)
            block = jnp.where(col == 226, low, block)
        block = block.astype(BF16)
        for d, o in enumerate((o0, o1, o2, o3)):
            o[:, b * 256 : b * 256 + 256] = block[d * 64 : d * 64 + 64]


def gate_up(place, h, g0, u0, g1, u1):
    part = shape((64, 1024), BF16)
    return pl.pallas_call(
        gate_up_kernel,
        out_shape=(part,) * 4,
        in_specs=[SMEM] + [VMEM] * 5,
        out_specs=(VMEM,) * 4,
        scratch_shapes=[pltpu.VMEM((256, 1024), BF16), pltpu.VMEM((256, 256), F32)],
        compiler_params=PARAMS,
        name="gate_up",
    )(place, h, g0, u0, g1, u1)


def hidden_kernel(a, b, c, d, out):
    total = a[...].astype(F32) + b[...].astype(F32) + c[...].astype(F32) + d[...].astype(F32)
    col = lanes((64, 256))
    first = total[:, 0:256]
    sq = jnp.sum(jnp.where((col >= 224) & (col < 227), first, 0.0), axis=1, keepdims=True)
    r = lax.rsqrt(sq / D + EPS)
    for b in range(2):
        gate = total[:, b * 512 : b * 512 + 256] * r
        up = total[:, b * 512 + 256 : b * 512 + 512] * r
        units = gate / (1.0 + jnp.exp(-gate)) * up
        out[:, b * 256 : b * 256 + 256] = jnp.where(col < 224, units, 0.0).astype(BF16)


def hidden_of(a, b, c, d):
    return pl.pallas_call(
        hidden_kernel,
        out_shape=shape((64, 512), BF16),
        in_specs=[VMEM] * 4,
        out_specs=VMEM,
        compiler_params=PARAMS,
        name="hidden_units",
    )(a, b, c, d)


def down_kernel(place, a, b, c, d, w0, w1, out, lhs):
    y = place[0]
    for s, part in enumerate((a, b, c, d)):
        at = pl.multiple_of(((y - s + 4) % 4) * 64, 64)
        lhs[pl.ds(at, 64), :] = part[...]
    total = jnp.dot(lhs[:, 0:224], w0[...], preferred_element_type=F32)
    total += jnp.dot(lhs[:, 256:480], w1[...], preferred_element_type=F32)
    out[...] = total.astype(BF16)


def down(place, parts, w0, w1):
    return pl.pallas_call(
        down_kernel,
        out_shape=shape((256, 1024), BF16),
        in_specs=[SMEM] + [VMEM] * 6,
        out_specs=VMEM,
        scratch_shapes=[pltpu.VMEM((256, 512), BF16)],
        compiler_params=PARAMS,
        name="down",
    )(place, *parts, w0, w1)


def residual_kernel(parts, h, res, sq):
    total = h[...].astype(F32)
    for p in range(32):
        total += parts[p].astype(F32)
    res[...] = total
    sq[...] = jnp.broadcast_to(jnp.sum(total * total, axis=1, keepdims=True), (8, 128))


def residual_of(parts, h):
    return pl.pallas_call(
        residual_kernel,
        out_shape=(shape((8, 1024), F32), shape((8, 128), F32)),
        in_specs=[VMEM] * 2,
        out_specs=(VMEM,) * 2,
        compiler_params=PARAMS,
        name="residual",
    )(parts, h)


def pool_kernel(place, counts, res, a, b, c, d, same, other):
    first, row, zb = place[2], place[4], place[6]
    sq = (a[...] + b[...] + c[...] + d[...])[:, 0:1]
    slots = lax.broadcasted_iota(jnp.int32, (8, 1), 0) + first
    held = counts[...].astype(F32)
    held = jnp.where(lax.broadcasted_iota(jnp.int32, (16, 64), 0) == row, held, 0.0)
    count = jnp.max(jnp.max(held, axis=1, keepdims=True), axis=0, keepdims=True)
    weight = jnp.where(slots.astype(F32) < count, lax.rsqrt(sq / D + EPS), 0.0)
    pooled = jnp.sum(res[...] * weight, axis=0, keepdims=True) / count
    ahead = jnp.concatenate([pooled[:, t * 256 : t * 256 + 128] for t in range(4)], axis=0)
    behind = jnp.concatenate([pooled[:, t * 256 + 128 : t * 256 + 256] for t in range(4)], axis=0)
    same[...] = jnp.where(zb == 0, ahead, behind)
    other[...] = jnp.where(zb == 0, behind, ahead)


def pool(place, counts, res, sqs):
    part = shape((4, 128), F32)
    return pl.pallas_call(
        pool_kernel,
        out_shape=(part,) * 2,
        in_specs=[SMEM] + [VMEM] * 6,
        out_specs=(VMEM,) * 2,
        compiler_params=PARAMS,
        name="pool",
    )(place, counts, res, *sqs)


def code_kernel(place, a, b, c, d, w0, w1, w2, w3, out, left):
    zh = place[5]
    left[...] = a[...] + b[...] + c[...] + d[...]
    total = jnp.zeros((8, 512), F32)
    for s, w in enumerate((w0, w1, w2, w3)):
        piece = jnp.broadcast_to(left[pl.ds((zh - s + 4) % 4, 1), :], (8, 128))
        total += jnp.dot(piece.astype(BF16), w[...], preferred_element_type=F32)
    for t in range(4):
        left[t : t + 1, :] = total[0:1, t * 128 : t * 128 + 128]
    out[...] = jnp.broadcast_to(left[...][None], (128, 4, 128))


def code_part(place, pieces, ws):
    return pl.pallas_call(
        code_kernel,
        out_shape=shape((128, 4, 128), F32),
        in_specs=[SMEM] + [VMEM] * 8,
        out_specs=VMEM,
        scratch_shapes=[pltpu.VMEM((4, 128), F32)],
        compiler_params=PARAMS,
        name="code_part",
    )(place, *pieces, *ws)


def exchange(x, step, falling):
    col = lanes(x.shape)
    upper = (col & step) != 0
    other = jnp.where(upper, pltpu.roll(x, step, 1), pltpu.roll(x, 128 - step, 1))
    return jnp.where(upper ^ falling, jnp.maximum(x, other), jnp.minimum(x, other))


def bitonic_merge(x, falling):
    for step in (64, 32, 16, 8, 4, 2, 1):
        x = exchange(x, step, falling)
    return x


def bitonic_sort(x, falling):
    col = lanes(x.shape)
    for size in (2, 4, 8, 16, 32, 64, 128):
        way = falling if size == 128 else falling ^ ((col & size) != 0)
        step = size // 2
        while step:
            x = exchange(x, step, way)
            step //= 2
    return x


def halves_far(v, apart, falling):
    out = list(v)
    for i in range(len(v)):
        if i & apart == 0:
            high, low = jnp.maximum(v[i], v[i + apart]), jnp.minimum(v[i], v[i + apart])
            way = falling(i)
            if way is True:
                out[i], out[i + apart] = high, low
            elif way is False:
                out[i], out[i + apart] = low, high
            else:
                out[i] = jnp.where(way, high, low)
                out[i + apart] = jnp.where(way, low, high)
    return out


def halves_near(v, step, falling):
    upper = (rows_of((8, 128)) & step) != 0
    out = []
    for i, x in enumerate(v):
        other = pltpu.roll(x, step, 0)
        if step != 4:
            other = jnp.where(upper, other, pltpu.roll(x, 8 - step, 0))
        way = falling(i)
        if way is True:
            take = ~upper
        elif way is False:
            take = upper
        else:
            take = upper ^ way
        out.append(jnp.where(take, jnp.maximum(x, other), jnp.minimum(x, other)))
    return out


def column_step(v, step, falling):
    if step >= 8:
        return halves_far(v, step // 8, falling)
    return halves_near(v, step, falling)


def column_merge(v, falling):
    for step in (64, 32, 16, 8, 4, 2, 1):
        v = column_step(v, step, lambda i: falling)
    return v


def column_sort(v, falling):
    sub = rows_of((8, 128))
    for size in (2, 4, 8, 16, 32, 64, 128):

        def way(i, size=size):
            if size == 128:
                return falling
            if size >= 8:
                return (i * 8) & size == 0
            return (sub & size) == 0

        step = size // 2
        while step:
            v = column_step(v, step, way)
            step //= 2
    return v


def columns_of(x):
    return [x[i * 8 : i * 8 + 8] for i in range(16)]


def rows_of(like):
    return lax.broadcasted_iota(jnp.int32, like, 0)


def score_kernel(place, mine, theirs, docs, lists, *, scale):
    k = place[1]
    own, peer = mine[...], theirs[...]
    low = jnp.where(k == 0, own, peer)
    high = jnp.where(k == 0, peer, own)
    dims = (((1,), (1,)), ((), ()))
    scores = lax.dot_general(low, docs[:, 0:512], dims, preferred_element_type=F32)
    scores += lax.dot_general(high, docs[:, 512:1024], dims, preferred_element_type=F32)
    scores = scores * scale
    x = jnp.concatenate([scores[:, c * 128 : c * 128 + 128] for c in range(4)] * 2, axis=0)
    lane = lanes((8, 128))
    v = column_sort(columns_of(x.T), lane & 32 == 0)
    v = [jnp.maximum(a, pltpu.roll(a, 96, 1)) for a in v]
    v = column_merge(v, lane & 16 == 0)
    v = [jnp.maximum(a, pltpu.roll(a, 112, 1)) for a in v]
    v = column_merge(v, lane * 0 + k == 0)
    lists[...] = jnp.concatenate(v, axis=0).T[0:16]


def local_lists(place, mine, theirs, docs):
    def body(*refs):
        score_kernel(*refs, scale=1.0 / math.sqrt(docs.shape[1]))

    return pl.pallas_call(
        body,
        out_shape=shape((16, 128), F32),
        in_specs=[SMEM] + [VMEM] * 3,
        out_specs=VMEM,
        compiler_params=PARAMS,
        name="scores",
    )(place, mine, theirs, docs)


def pair_kernel(place, a, b, o0, o1, o2, o3, held):
    y = place[0]
    x = jnp.maximum(a[...], b[...])
    turn = (rows_of((16, 128)) // 4 - y + 4) % 4
    held[...] = bitonic_merge(x, turn % 2 == 0)
    for d, o in enumerate((o0, o1, o2, o3)):
        o[...] = held[pl.ds(pl.multiple_of(((y + d) % 4) * 4, 4), 4), :]


def pair_lists(place, a, b):
    four = shape((4, 128), F32)
    return pl.pallas_call(
        pair_kernel,
        out_shape=(four,) * 4,
        in_specs=[SMEM] + [VMEM] * 2,
        out_specs=(VMEM,) * 4,
        scratch_shapes=[pltpu.VMEM((16, 128), F32)],
        compiler_params=PARAMS,
        name="pair_lists",
    )(place, a, b)


def four_kernel(place, a, b, c, d, out):
    odd = place[3]
    x = jnp.concatenate(
        [jnp.maximum(a[...], b[...]), jnp.maximum(c[...], d[...])], axis=0
    )
    x = bitonic_merge(x, rows_of((8, 128)) < 4)
    x = jnp.maximum(x, pltpu.roll(x, 4, 0))
    x = bitonic_merge(x, (rows_of((8, 128)) * 0 + odd) == 0)
    out[...] = jnp.broadcast_to(x[0:4][None], (128, 4, 128))


def four_lists(place, lists):
    return pl.pallas_call(
        four_kernel,
        out_shape=shape((128, 4, 128), F32),
        in_specs=[SMEM] + [VMEM] * 4,
        out_specs=VMEM,
        compiler_params=PARAMS,
        name="four_lists",
    )(place, *lists)


def final_kernel(x_ref, out):
    lane = lanes((8, 128))
    tiles = []
    for y in range(4):
        v = columns_of(x_ref[y * 128 : y * 128 + 128, :].T)
        tiles.append([jnp.maximum(a, pltpu.roll(a, 64, 1)) for a in v])
    first = [jnp.where(lane < 64, a, b) for a, b in zip(tiles[0], tiles[1])]
    second = [jnp.where(lane < 64, a, b) for a, b in zip(tiles[2], tiles[3])]
    first = column_merge(first, lane & 32 == 0)
    second = column_merge(second, lane & 32 == 0)
    v = [
        jnp.where(
            lane & 32 == 0,
            jnp.maximum(a, pltpu.roll(a, 96, 1)),
            jnp.maximum(b, pltpu.roll(b, 32, 1)),
        )
        for a, b in zip(first, second)
    ]
    for near in (16, 8, 4):
        v = column_merge(v, lane & near == 0)
        v = [jnp.maximum(a, pltpu.roll(a, 128 - near, 1)) for a in v]
    v = column_merge(v, True)
    x = jnp.concatenate(v, axis=0).T
    for y, row in enumerate((0, 64, 32, 96)):
        out[y * 4 : y * 4 + 4, :] = x[row : row + 4, 0:TOPK]


def final_lists(x):
    return pl.pallas_call(
        final_kernel,
        out_shape=shape((16, TOPK), F32),
        in_specs=[VMEM],
        out_specs=VMEM,
        compiler_params=PARAMS,
        name="final_lists",
    )(x)


def per_device(hidden_in, lengths, gate_weight, up_weight, down_weight, code_weight, corpus_codes):
    y, x, zh, zb, k = (lax.axis_index(a) for a in QUERY_CORPUS)
    place = jnp.stack([y, k, 16 * k + 8 * zb, x // 2, 4 * zh, zh, zb]).astype(jnp.int32)

    own, other = pack(place, lengths, hidden_in)
    swap = [(a * 4 + b, b * 4 + a) for a in range(4) for b in range(4)]
    straight = [(s * 2 + c, t * 2 + c) for s, t in swap for c in range(2)]
    crossed = [(s * 2 + c, t * 2 + 1 - c) for s, t in swap for c in range(2)]
    own = lax.ppermute(own, ("y", "x", "k"), straight)
    other = lax.ppermute(other, ("y", "x", "k"), crossed)
    counts, own = own[64:], own[:64]
    block = jnp.where(
        k == 0, jnp.concatenate([own, other], axis=1), jnp.concatenate([other, own], axis=1)
    )
    gate_rows, up_rows = gate_weight.T, up_weight.T
    gate_peer, up_peer, down_peer = (to_peer(w) for w in (gate_rows, up_rows, down_weight))
    block, gate_peer, up_peer, down_peer = lax.optimization_barrier(
        (block, gate_peer, up_peer, down_peer)
    )
    gathered = spread(block, XZ, 32)

    low, high = code_weight[:, :512], code_weight[:, 512:]
    mine = lax.ppermute(jnp.where(k == 0, low, high), ("y", "x", "k"), straight)
    theirs = lax.ppermute(jnp.where(k == 0, high, low), ("y", "x", "k"), crossed)
    rows = jnp.concatenate(
        [jnp.where(k == 0, mine, theirs), jnp.where(k == 0, theirs, mine)], axis=0
    )
    rows, gathered = lax.optimization_barrier((rows, gathered))
    turned = [[(i, (i + d) % 4) for i in range(4)] for d in range(4)]
    code_rows = (rows, *(lax.ppermute(rows, "zh", turned[d]) for d in (1, 2, 3)))

    parts = gate_up(place, gathered, gate_rows, up_rows, gate_peer, up_peer)
    units = hidden_of(parts[0], *(shifted(parts[d], d) for d in (1, 2, 3)))
    groups = (units, *(shifted(units, d) for d in (1, 2, 3)))
    branch = down(place, groups, down_weight, down_peer)
    branch = lax.all_to_all(branch.reshape(32, 8, 1024), XZ, 0, 0, tiled=True)
    here = lax.dynamic_slice(
        gathered.reshape(4, 8, 64, 128), (x, 0, zh * 16 + zb * 8, 0), (1, 8, 8, 128)
    )[0]
    here = jnp.moveaxis(here, 0, 1).reshape(8, 1024)
    res, sq = residual_of(branch, here)
    sqs = (sq, *(shifted(sq, d) for d in (1, 2, 3)))
    same, other = pool(place, counts, res, sqs)
    flips = [[(i, i ^ r) for i in range(4)] for r in range(4)]
    sent = ((same, 1), (other, 2), (other, 3))
    pieces = (same, *(lax.ppermute(a, ("zb", "k"), flips[r]) for a, r in sent))
    part = code_part(place, pieces, code_rows)
    codes = lax.all_to_all(part, YXZ, 0, 0, tiled=True)
    codes = codes.reshape(4, 4, 4, 2, 512).sum(axis=(0, 3))
    codes = codes.reshape(16, 512).astype(BF16)

    lists = local_lists(place, codes, to_peer(codes), corpus_codes)
    lists = pair_lists(place, lists, to_peer(lists))
    lists = (lists[0], *(shifted(lists[d], d) for d in (1, 2, 3)))
    lists = four_lists(place, lists)
    arrived = lax.all_to_all(lists, YXZ, 0, 0, tiled=True)
    return final_lists(arrived.reshape(512, 128))


def solution(mesh):
    split = Mesh(mesh.devices.reshape(4, 4, 4, 2, 2), QUERY_CORPUS)
    return jax.shard_map(
        per_device,
        mesh=split,
        in_specs=(
            P("y", CORPUS),
            P("y"),
            P("y", CORPUS),
            P("y", CORPUS),
            P(CORPUS, "y"),
            P(CORPUS, None),
            P(QUERY_CORPUS, None),
        ),
        out_specs=P(),
        check_vma=False,
    )
```

```python
import math

import jax
import jax.numpy as jnp
from jax import lax
from jax.experimental import pallas as pl
from jax.experimental.pallas import tpu as pltpu
from jax.sharding import Mesh
from jax.sharding import PartitionSpec as P

D = 4096
SEQ = 32
TOPK = 100
Z = ("zh", "zb")
XZ = ("x", "zh", "zb")
YXZ = ("y", "x", "zh", "zb")
CORPUS = ("x", "zh", "zb", "k")
QUERY_CORPUS = ("y", "x", "zh", "zb", "k")
EPS = 1e-05
F32 = jnp.float32
BF16 = jnp.bfloat16
PARAMS = pltpu.CompilerParams(vmem_limit_bytes=32 * 1024 * 1024)
VMEM = pl.BlockSpec(memory_space=pltpu.VMEM)
SMEM = pl.BlockSpec(memory_space=pltpu.SMEM)


def shape(dims, dtype):
    return jax.ShapeDtypeStruct(dims, dtype)


def to_peer(x):
    return lax.ppermute(x, "k", [(0, 1), (1, 0)])


def shifted(x, d):
    return lax.ppermute(x, "y", [(i, (i + d) % 4) for i in range(4)])


def spread(x, axes, peers):
    copies = jnp.broadcast_to(x[None], (peers, *x.shape))
    return lax.all_to_all(copies, axes, 0, 0, tiled=True)


def lanes(like):
    return lax.broadcasted_iota(jnp.int32, like, 1)


def pack_kernel(place, h, own, other):
    k = place[1]
    x = h[...].astype(F32).T
    for q in range(4):
        one = x[q * 32 : q * 32 + 16, :]
        two = x[q * 32 + 16 : q * 32 + 32, :]
        own[q * 16 : q * 16 + 16, :] = jnp.where(k == 0, one, two).astype(BF16)
        other[q * 16 : q * 16 + 16, :] = jnp.where(k == 0, two, one).astype(BF16)


def pack(place, h):
    part = shape((64, 64), BF16)
    return pl.pallas_call(
        pack_kernel,
        out_shape=(part, part),
        in_specs=[SMEM, VMEM],
        out_specs=(VMEM,) * 2,
        compiler_params=PARAMS,
        name="pack",
    )(place, h)


def gate_up_kernel(place, lengths, h, g0, u0, g1, u1, o0, o1, o2, o3, lhs, wide):
    y = place[0]
    for d in range(4):
        i = (y + d) % 4
        for z in range(8):
            lhs[d * 64 : d * 64 + 64, z * 128 : z * 128 + 128] = h[i * 8 + z]
    left = lhs[...]
    widened = left.astype(F32)
    sq = jnp.sum(widened * widened, axis=1, keepdims=True)
    top = sq.astype(BF16).astype(F32)
    mid = (sq - top).astype(BF16).astype(F32)
    low = sq - top - mid
    col = lanes((256, 256))
    wide[...] = jnp.zeros((256, 256), F32)
    for b, w in enumerate((g0, u0, g1, u1)):
        wide[:, 0:224] = lax.dot_general(
            left, w[...], (((1,), (1,)), ((), ())), preferred_element_type=F32
        )
        block = wide[...]
        if b == 0:
            block = jnp.where(col == 224, top, block)
            block = jnp.where(col == 225, mid, block)
            block = jnp.where(col == 226, low, block)
            for q in range(4):
                block = jnp.where(col == 228 + q, lengths[q].astype(F32), block)
        block = block.astype(BF16)
        for d, o in enumerate((o0, o1, o2, o3)):
            o[:, b * 256 : b * 256 + 256] = block[d * 64 : d * 64 + 64]


def gate_up(place, lengths, h, g0, u0, g1, u1):
    part = shape((64, 1024), BF16)
    return pl.pallas_call(
        gate_up_kernel,
        out_shape=(part,) * 4,
        in_specs=[SMEM] * 2 + [VMEM] * 5,
        out_specs=(VMEM,) * 4,
        scratch_shapes=[pltpu.VMEM((256, 1024), BF16), pltpu.VMEM((256, 256), F32)],
        compiler_params=PARAMS,
        name="gate_up",
    )(place, lengths, h, g0, u0, g1, u1)


def hidden_kernel(place, a, b, c, d, out, counts):
    y, x = place[0], place[7]
    held = jnp.zeros((8, 128), F32)
    for s, part in enumerate((a, b, c, d)):
        held = jnp.where((y - s + 4) % 4 == x, part[0:8, 128:256].astype(F32), held)
    counts[...] = held
    total = a[...].astype(F32) + b[...].astype(F32) + c[...].astype(F32) + d[...].astype(F32)
    col = lanes((64, 256))
    first = total[:, 0:256]
    sq = jnp.sum(jnp.where((col >= 224) & (col < 227), first, 0.0), axis=1, keepdims=True)
    r = lax.rsqrt(sq / D + EPS)
    for b in range(2):
        gate = total[:, b * 512 : b * 512 + 256] * r
        up = total[:, b * 512 + 256 : b * 512 + 512] * r
        units = gate / (1.0 + jnp.exp(-gate)) * up
        out[:, b * 256 : b * 256 + 256] = jnp.where(col < 224, units, 0.0).astype(BF16)


def hidden_of(place, a, b, c, d):
    return pl.pallas_call(
        hidden_kernel,
        out_shape=(shape((64, 512), BF16), shape((8, 128), F32)),
        in_specs=[SMEM] + [VMEM] * 4,
        out_specs=(VMEM,) * 2,
        compiler_params=PARAMS,
        name="hidden_units",
    )(place, a, b, c, d)


def down_kernel(place, a, b, c, d, w0, w1, out, lhs):
    y = place[0]
    for s, part in enumerate((a, b, c, d)):
        at = pl.multiple_of(((y - s + 4) % 4) * 64, 64)
        lhs[pl.ds(at, 64), :] = part[...]
    total = jnp.dot(lhs[:, 0:224], w0[...], preferred_element_type=F32)
    total += jnp.dot(lhs[:, 256:480], w1[...], preferred_element_type=F32)
    out[...] = total.astype(BF16)


def down(place, parts, w0, w1):
    return pl.pallas_call(
        down_kernel,
        out_shape=shape((256, 1024), BF16),
        in_specs=[SMEM] + [VMEM] * 6,
        out_specs=VMEM,
        scratch_shapes=[pltpu.VMEM((256, 512), BF16)],
        compiler_params=PARAMS,
        name="down",
    )(place, *parts, w0, w1)


def residual_kernel(parts, h, res, sq):
    total = h[...].astype(F32)
    for p in range(32):
        total += parts[p].astype(F32)
    res[...] = total
    sq[...] = jnp.broadcast_to(jnp.sum(total * total, axis=1, keepdims=True), (8, 128))


def residual_of(parts, h):
    return pl.pallas_call(
        residual_kernel,
        out_shape=(shape((8, 1024), F32), shape((8, 128), F32)),
        in_specs=[VMEM] * 2,
        out_specs=(VMEM,) * 2,
        compiler_params=PARAMS,
        name="residual",
    )(parts, h)


def pool_kernel(place, counts, res, a, b, c, d, o0, o1, o2, o3):
    k, first, zh, zb = place[1], place[2], place[5], place[6]
    sq = (a[...] + b[...] + c[...] + d[...])[:, 0:1]
    slots = lax.broadcasted_iota(jnp.int32, (8, 1), 0) + first
    held = jnp.where(lanes((1, 128)) == 100 + zh, counts[0:1, :], 0.0)
    count = jnp.max(held, axis=1, keepdims=True)
    weight = jnp.where(slots.astype(F32) < count, lax.rsqrt(sq / D + EPS), 0.0)
    pooled = jnp.sum(res[...] * weight, axis=0, keepdims=True) / count
    ahead = jnp.concatenate([pooled[:, t * 256 : t * 256 + 128] for t in range(4)], axis=0)
    behind = jnp.concatenate([pooled[:, t * 256 + 128 : t * 256 + 256] for t in range(4)], axis=0)
    for r, out in enumerate((o0, o1, o2, o3)):
        one = jnp.where(zb == r // 2, ahead, behind)
        two = jnp.where(zb == r // 2, behind, ahead)
        part = jnp.concatenate([one, two], axis=0)
        out[...] = jnp.where(k == r % 2, part, pltpu.roll(part, 64, 1))


def pool(place, counts, res, sqs):
    part = shape((8, 128), F32)
    return pl.pallas_call(
        pool_kernel,
        out_shape=(part,) * 4,
        in_specs=[SMEM] + [VMEM] * 6,
        out_specs=(VMEM,) * 4,
        compiler_params=PARAMS,
        name="pool",
    )(place, counts, res, *sqs)


def code_kernel(place, a, b, c, d, w0, w1, w2, w3, out, left):
    zh = place[5]
    left[...] = a[...] + b[...] + c[...] + d[...]
    total = jnp.zeros((8, 256), F32)
    for s, w in enumerate((w0, w1, w2, w3)):
        row = (zh - s + 4) % 4
        one = jnp.broadcast_to(left[pl.ds(row, 1), :], (8, 128))
        two = jnp.broadcast_to(left[pl.ds(row + 4, 1), :], (8, 128))
        piece = jnp.concatenate([one, two], axis=1).astype(BF16)
        total += jnp.dot(piece, w[...], preferred_element_type=F32)
    for t in range(2):
        left[t : t + 1, :] = total[0:1, t * 128 : t * 128 + 128]
    out[...] = jnp.broadcast_to(left[0:2][None], (64, 2, 128))


def code_part(place, pieces, ws):
    return pl.pallas_call(
        code_kernel,
        out_shape=shape((64, 2, 128), F32),
        in_specs=[SMEM] + [VMEM] * 8,
        out_specs=VMEM,
        scratch_shapes=[pltpu.VMEM((8, 128), F32)],
        compiler_params=PARAMS,
        name="code_part",
    )(place, *pieces, *ws)


def exchange(x, step, falling):
    col = lanes(x.shape)
    upper = (col & step) != 0
    other = jnp.where(upper, pltpu.roll(x, step, 1), pltpu.roll(x, 128 - step, 1))
    return jnp.where(upper ^ falling, jnp.maximum(x, other), jnp.minimum(x, other))


def bitonic_merge(x, falling):
    for step in (64, 32, 16, 8, 4, 2, 1):
        x = exchange(x, step, falling)
    return x


def bitonic_sort(x, falling):
    col = lanes(x.shape)
    for size in (2, 4, 8, 16, 32, 64, 128):
        way = falling if size == 128 else falling ^ ((col & size) != 0)
        step = size // 2
        while step:
            x = exchange(x, step, way)
            step //= 2
    return x


def halves_far(v, apart, falling):
    out = list(v)
    for i in range(len(v)):
        if i & apart == 0:
            high, low = jnp.maximum(v[i], v[i + apart]), jnp.minimum(v[i], v[i + apart])
            way = falling(i)
            if way is True:
                out[i], out[i + apart] = high, low
            elif way is False:
                out[i], out[i + apart] = low, high
            else:
                out[i] = jnp.where(way, high, low)
                out[i + apart] = jnp.where(way, low, high)
    return out


def halves_near(v, step, falling):
    upper = (rows_of((8, 128)) & step) != 0
    out = []
    for i, x in enumerate(v):
        other = pltpu.roll(x, step, 0)
        if step != 4:
            other = jnp.where(upper, other, pltpu.roll(x, 8 - step, 0))
        way = falling(i)
        if way is True:
            take = ~upper
        elif way is False:
            take = upper
        else:
            take = upper ^ way
        out.append(jnp.where(take, jnp.maximum(x, other), jnp.minimum(x, other)))
    return out


def column_step(v, step, falling):
    if step >= 8:
        return halves_far(v, step // 8, falling)
    return halves_near(v, step, falling)


def column_merge(v, falling):
    for step in (64, 32, 16, 8, 4, 2, 1):
        v = column_step(v, step, lambda i: falling)
    return v


def column_sort(v, falling):
    sub = rows_of((8, 128))
    for size in (2, 4, 8, 16, 32, 64, 128):

        def way(i, size=size):
            if size == 128:
                return falling
            if size >= 8:
                return (i * 8) & size == 0
            return (sub & size) == 0

        step = size // 2
        while step:
            v = column_step(v, step, way)
            step //= 2
    return v


def columns_of(x):
    return [x[i * 8 : i * 8 + 8] for i in range(16)]


def rows_of(like):
    return lax.broadcasted_iota(jnp.int32, like, 0)


def score_kernel(place, c0, c1, c2, c3, docs, lists, *, scale):
    k, zb = place[1], place[6]
    at = zb * 2 + k
    dims = (((1,), (1,)), ((), ()))
    scores = jnp.zeros((16, 512), F32)
    for j in range(4):
        piece = c0[...]
        for r, c in ((1, c1), (2, c2), (3, c3)):
            piece = jnp.where(at == j ^ r, c[...], piece)
        part = docs[:, j * 256 : j * 256 + 256]
        scores += lax.dot_general(piece, part, dims, preferred_element_type=F32)
    scores = scores * scale
    x = jnp.concatenate([scores[:, c * 128 : c * 128 + 128] for c in range(4)] * 2, axis=0)
    lane = lanes((8, 128))
    v = column_sort(columns_of(x.T), lane & 32 == 0)
    v = [jnp.maximum(a, pltpu.roll(a, 96, 1)) for a in v]
    v = column_merge(v, lane & 16 == 0)
    v = [jnp.maximum(a, pltpu.roll(a, 112, 1)) for a in v]
    v = column_merge(v, lane * 0 + k == 0)
    lists[...] = jnp.concatenate(v, axis=0).T[0:16]


def local_lists(place, pieces, docs):
    def body(*refs):
        score_kernel(*refs, scale=1.0 / math.sqrt(docs.shape[1]))

    return pl.pallas_call(
        body,
        out_shape=shape((16, 128), F32),
        in_specs=[SMEM] + [VMEM] * 5,
        out_specs=VMEM,
        compiler_params=PARAMS,
        name="scores",
    )(place, *pieces, docs)


def pair_kernel(place, a, b, o0, o1, o2, o3, held):
    y = place[0]
    x = jnp.maximum(a[...], b[...])
    turn = (rows_of((16, 128)) // 4 - y + 4) % 4
    held[...] = bitonic_merge(x, turn % 2 == 0)
    for d, o in enumerate((o0, o1, o2, o3)):
        o[...] = held[pl.ds(pl.multiple_of(((y + d) % 4) * 4, 4), 4), :]


def pair_lists(place, a, b):
    four = shape((4, 128), F32)
    return pl.pallas_call(
        pair_kernel,
        out_shape=(four,) * 4,
        in_specs=[SMEM] + [VMEM] * 2,
        out_specs=(VMEM,) * 4,
        scratch_shapes=[pltpu.VMEM((16, 128), F32)],
        compiler_params=PARAMS,
        name="pair_lists",
    )(place, a, b)


def four_kernel(place, a, b, c, d, out):
    odd = place[3]
    x = jnp.concatenate(
        [jnp.maximum(a[...], b[...]), jnp.maximum(c[...], d[...])], axis=0
    )
    x = bitonic_merge(x, rows_of((8, 128)) < 4)
    x = jnp.maximum(x, pltpu.roll(x, 4, 0))
    x = bitonic_merge(x, (rows_of((8, 128)) * 0 + odd) == 0)
    out[...] = jnp.broadcast_to(x[0:4][None], (128, 4, 128))


def four_lists(place, lists):
    return pl.pallas_call(
        four_kernel,
        out_shape=shape((128, 4, 128), F32),
        in_specs=[SMEM] + [VMEM] * 4,
        out_specs=VMEM,
        compiler_params=PARAMS,
        name="four_lists",
    )(place, *lists)


def final_kernel(x_ref, out):
    lane = lanes((8, 128))
    tiles = []
    for y in range(4):
        v = columns_of(x_ref[y * 128 : y * 128 + 128, :].T)
        tiles.append([jnp.maximum(a, pltpu.roll(a, 64, 1)) for a in v])
    first = [jnp.where(lane < 64, a, b) for a, b in zip(tiles[0], tiles[1])]
    second = [jnp.where(lane < 64, a, b) for a, b in zip(tiles[2], tiles[3])]
    first = column_merge(first, lane & 32 == 0)
    second = column_merge(second, lane & 32 == 0)
    v = [
        jnp.where(
            lane & 32 == 0,
            jnp.maximum(a, pltpu.roll(a, 96, 1)),
            jnp.maximum(b, pltpu.roll(b, 32, 1)),
        )
        for a, b in zip(first, second)
    ]
    for near in (16, 8, 4):
        v = column_merge(v, lane & near == 0)
        v = [jnp.maximum(a, pltpu.roll(a, 128 - near, 1)) for a in v]
    v = column_merge(v, True)
    x = jnp.concatenate(v, axis=0).T
    for y, row in enumerate((0, 64, 32, 96)):
        out[y * 4 : y * 4 + 4, :] = x[row : row + 4, 0:TOPK]


def final_lists(x):
    return pl.pallas_call(
        final_kernel,
        out_shape=shape((16, TOPK), F32),
        in_specs=[VMEM],
        out_specs=VMEM,
        compiler_params=PARAMS,
        name="final_lists",
    )(x)


def per_device(hidden_in, lengths, gate_weight, up_weight, down_weight, code_weight, corpus_codes):
    y, x, zh, zb, k = (lax.axis_index(a) for a in QUERY_CORPUS)
    place = jnp.stack([y, k, 16 * k + 8 * zb, x // 2, 4 * zh, zh, zb, x]).astype(jnp.int32)

    own, other = pack(place, hidden_in.T)
    swap = [(a * 4 + b, b * 4 + a) for a in range(4) for b in range(4)]
    straight = [(s * 2 + c, t * 2 + c) for s, t in swap for c in range(2)]
    crossed = [(s * 2 + c, t * 2 + 1 - c) for s, t in swap for c in range(2)]
    own = lax.ppermute(own, ("y", "x", "k"), straight)
    other = lax.ppermute(other, ("y", "x", "k"), crossed)
    block = jnp.where(
        k == 0, jnp.concatenate([own, other], axis=1), jnp.concatenate([other, own], axis=1)
    )
    gate_rows, up_rows = gate_weight.T, up_weight.T
    gate_peer, up_peer, down_peer = (to_peer(w) for w in (gate_rows, up_rows, down_weight))
    block, gate_peer, up_peer, down_peer = lax.optimization_barrier(
        (block, gate_peer, up_peer, down_peer)
    )
    gathered = spread(block, XZ, 32)

    at = 2 * zb + k
    flipped = []
    for r in range(4):
        bits = lax.dynamic_slice_in_dim(code_weight, (at ^ r) * 256, 256, axis=1)
        pairs = [(s * 4 + c, t * 4 + (c ^ r)) for s, t in swap for c in range(4)]
        flipped.append(lax.ppermute(bits, ("y", "x", "zb", "k"), pairs))
    rows = jnp.concatenate(flipped, axis=0)
    rows, gathered = lax.optimization_barrier((rows, gathered))
    turned = [[(i, (i + d) % 4) for i in range(4)] for d in range(4)]
    code_rows = (rows, *(lax.ppermute(rows, "zh", turned[d]) for d in (1, 2, 3)))

    parts = gate_up(place, lengths, gathered, gate_rows, up_rows, gate_peer, up_peer)
    units, counts = hidden_of(place, parts[0], *(shifted(parts[d], d) for d in (1, 2, 3)))
    groups = (units, *(shifted(units, d) for d in (1, 2, 3)))
    branch = down(place, groups, down_weight, down_peer)
    branch = lax.all_to_all(branch.reshape(32, 8, 1024), XZ, 0, 0, tiled=True)
    here = lax.dynamic_slice(
        gathered.reshape(4, 8, 64, 128), (x, 0, zh * 16 + zb * 8, 0), (1, 8, 8, 128)
    )[0]
    here = jnp.moveaxis(here, 0, 1).reshape(8, 1024)
    res, sq = residual_of(branch, here)
    sqs = (sq, *(shifted(sq, d) for d in (1, 2, 3)))
    mine = pool(place, counts, res, sqs)
    flips = [[(i, i ^ r) for i in range(4)] for r in range(4)]
    pieces = (mine[0], *(lax.ppermute(mine[r], ("zb", "k"), flips[r]) for r in (1, 2, 3)))
    part = code_part(place, pieces, code_rows)
    codes = lax.all_to_all(part, ("y", "x", "zh"), 0, 0, tiled=True)
    codes = codes.reshape(4, 16, 256).sum(axis=0).astype(BF16)
    codes = (codes, *(lax.ppermute(codes, ("zb", "k"), flips[r]) for r in (1, 2, 3)))
    lists = local_lists(place, codes, corpus_codes)
    lists = pair_lists(place, lists, to_peer(lists))
    lists = (lists[0], *(shifted(lists[d], d) for d in (1, 2, 3)))
    lists = four_lists(place, lists)
    arrived = lax.all_to_all(lists, YXZ, 0, 0, tiled=True)
    return final_lists(arrived.reshape(512, 128))


def solution(mesh):
    split = Mesh(mesh.devices.reshape(4, 4, 4, 2, 2), QUERY_CORPUS)
    return jax.shard_map(
        per_device,
        mesh=split,
        in_specs=(
            P("y", CORPUS),
            P("y"),
            P("y", CORPUS),
            P("y", CORPUS),
            P(CORPUS, "y"),
            P(CORPUS, None),
            P(QUERY_CORPUS, None),
        ),
        out_specs=P(),
        check_vma=False,
    )
```

```python
import math

import jax
import jax.numpy as jnp
from jax import lax
from jax.experimental import pallas as pl
from jax.experimental.pallas import tpu as pltpu
from jax.sharding import Mesh
from jax.sharding import PartitionSpec as P

D = 4096
SEQ = 32
TOPK = 100
Z = ("zh", "zb")
XZ = ("x", "zh", "zb")
YXZ = ("y", "x", "zh", "zb")
CORPUS = ("x", "zh", "zb", "k")
QUERY_CORPUS = ("y", "x", "zh", "zb", "k")
EPS = 1e-05
F32 = jnp.float32
BF16 = jnp.bfloat16
PARAMS = pltpu.CompilerParams(vmem_limit_bytes=32 * 1024 * 1024)
VMEM = pl.BlockSpec(memory_space=pltpu.VMEM)
SMEM = pl.BlockSpec(memory_space=pltpu.SMEM)


def shape(dims, dtype):
    return jax.ShapeDtypeStruct(dims, dtype)


def to_peer(x):
    return lax.ppermute(x, "k", [(0, 1), (1, 0)])


def shifted(x, d):
    return lax.ppermute(x, "y", [(i, (i + d) % 4) for i in range(4)])


def spread(x, axes, peers):
    copies = jnp.broadcast_to(x[None], (peers, *x.shape))
    return lax.all_to_all(copies, axes, 0, 0, tiled=True)


def lanes(like):
    return lax.broadcasted_iota(jnp.int32, like, 1)


def pack_kernel(place, h, w, own, other, w0, w1, w2, w3):
    k, zb = place[1], place[6]
    x = h[...].astype(F32).T
    for q in range(4):
        one = x[q * 32 : q * 32 + 16, :]
        two = x[q * 32 + 16 : q * 32 + 32, :]
        own[q * 16 : q * 16 + 16, :] = jnp.where(k == 0, one, two).astype(BF16)
        other[q * 16 : q * 16 + 16, :] = jnp.where(k == 0, two, one).astype(BF16)
    for r, out in enumerate((w0, w1, w2, w3)):
        at = (zb * 2 + k) ^ r
        out[...] = w[:, pl.ds(pl.multiple_of(at * 256, 256), 256)]


def pack(place, h, w):
    part, quarter = shape((64, 64), BF16), shape((64, 256), BF16)
    return pl.pallas_call(
        pack_kernel,
        out_shape=(part,) * 2 + (quarter,) * 4,
        in_specs=[SMEM, VMEM, VMEM],
        out_specs=(VMEM,) * 6,
        compiler_params=PARAMS,
        name="pack",
    )(place, h, w)


def fan_kernel(place, own, other, out):
    k = place[1]
    a, b = own[...].astype(F32), other[...].astype(F32)
    one, two = jnp.where(k == 0, a, b), jnp.where(k == 0, b, a)
    block = jnp.concatenate([one, two], axis=1).astype(BF16)
    for p in range(32):
        out[p] = block


def fan(place, own, other):
    return pl.pallas_call(
        fan_kernel,
        out_shape=shape((32, 64, 128), BF16),
        in_specs=[SMEM, VMEM, VMEM],
        out_specs=VMEM,
        compiler_params=PARAMS,
        name="fan",
    )(place, own, other)


def gate_up_kernel(place, lengths, h, g0, u0, g1, u1, o0, o1, o2, o3, lhs, wide):
    y = place[0]
    for d in range(4):
        i = (y + d) % 4
        for z in range(8):
            lhs[d * 64 : d * 64 + 64, z * 128 : z * 128 + 128] = h[i * 8 + z]
    left = lhs[...]
    widened = left.astype(F32)
    sq = jnp.sum(widened * widened, axis=1, keepdims=True)
    top = sq.astype(BF16).astype(F32)
    mid = (sq - top).astype(BF16).astype(F32)
    low = sq - top - mid
    col = lanes((256, 256))
    wide[...] = jnp.zeros((256, 256), F32)
    for b, w in enumerate((g0, u0, g1, u1)):
        wide[:, 0:224] = lax.dot_general(
            left, w[...], (((1,), (1,)), ((), ())), preferred_element_type=F32
        )
        block = wide[...]
        if b == 0:
            block = jnp.where(col == 224, top, block)
            block = jnp.where(col == 225, mid, block)
            block = jnp.where(col == 226, low, block)
            for q in range(4):
                block = jnp.where(col == 228 + q, lengths[q].astype(F32), block)
        block = block.astype(BF16)
        for d, o in enumerate((o0, o1, o2, o3)):
            o[:, b * 256 : b * 256 + 256] = block[d * 64 : d * 64 + 64]


def gate_up(place, lengths, h, g0, u0, g1, u1):
    part = shape((64, 1024), BF16)
    return pl.pallas_call(
        gate_up_kernel,
        out_shape=(part,) * 4,
        in_specs=[SMEM] * 2 + [VMEM] * 5,
        out_specs=(VMEM,) * 4,
        scratch_shapes=[pltpu.VMEM((256, 1024), BF16), pltpu.VMEM((256, 256), F32)],
        compiler_params=PARAMS,
        name="gate_up",
    )(place, lengths, h, g0, u0, g1, u1)


def hidden_kernel(place, a, b, c, d, out, counts):
    y, x = place[0], place[7]
    held = jnp.zeros((8, 128), F32)
    for s, part in enumerate((a, b, c, d)):
        held = jnp.where((y - s + 4) % 4 == x, part[0:8, 128:256].astype(F32), held)
    counts[...] = held
    total = a[...].astype(F32) + b[...].astype(F32) + c[...].astype(F32) + d[...].astype(F32)
    col = lanes((64, 256))
    first = total[:, 0:256]
    sq = jnp.sum(jnp.where((col >= 224) & (col < 227), first, 0.0), axis=1, keepdims=True)
    r = lax.rsqrt(sq / D + EPS)
    for b in range(2):
        gate = total[:, b * 512 : b * 512 + 256] * r
        up = total[:, b * 512 + 256 : b * 512 + 512] * r
        units = gate / (1.0 + jnp.exp(-gate)) * up
        out[:, b * 256 : b * 256 + 256] = jnp.where(col < 224, units, 0.0).astype(BF16)


def hidden_of(place, a, b, c, d):
    return pl.pallas_call(
        hidden_kernel,
        out_shape=(shape((64, 512), BF16), shape((8, 128), F32)),
        in_specs=[SMEM] + [VMEM] * 4,
        out_specs=(VMEM,) * 2,
        compiler_params=PARAMS,
        name="hidden_units",
    )(place, a, b, c, d)


def down_kernel(place, a, b, c, d, w0, w1, out, lhs):
    y = place[0]
    for s, part in enumerate((a, b, c, d)):
        at = pl.multiple_of(((y - s + 4) % 4) * 64, 64)
        lhs[pl.ds(at, 64), :] = part[...]
    total = jnp.dot(lhs[:, 0:224], w0[...], preferred_element_type=F32)
    total += jnp.dot(lhs[:, 256:480], w1[...], preferred_element_type=F32)
    out[...] = total.astype(BF16)


def down(place, parts, w0, w1):
    return pl.pallas_call(
        down_kernel,
        out_shape=shape((256, 1024), BF16),
        in_specs=[SMEM] + [VMEM] * 6,
        out_specs=VMEM,
        scratch_shapes=[pltpu.VMEM((256, 512), BF16)],
        compiler_params=PARAMS,
        name="down",
    )(place, *parts, w0, w1)


def residual_kernel(parts, h, res, sq):
    total = h[...].astype(F32)
    for p in range(32):
        total += parts[p].astype(F32)
    res[...] = total
    sq[...] = jnp.broadcast_to(jnp.sum(total * total, axis=1, keepdims=True), (8, 128))


def residual_of(parts, h):
    return pl.pallas_call(
        residual_kernel,
        out_shape=(shape((8, 1024), F32), shape((8, 128), F32)),
        in_specs=[VMEM] * 2,
        out_specs=(VMEM,) * 2,
        compiler_params=PARAMS,
        name="residual",
    )(parts, h)


def pool_kernel(place, counts, res, a, b, c, d, o0, o1, o2, o3):
    k, first, zh, zb = place[1], place[2], place[5], place[6]
    sq = (a[...] + b[...] + c[...] + d[...])[:, 0:1]
    slots = lax.broadcasted_iota(jnp.int32, (8, 1), 0) + first
    held = jnp.where(lanes((1, 128)) == 100 + zh, counts[0:1, :], 0.0)
    count = jnp.max(held, axis=1, keepdims=True)
    weight = jnp.where(slots.astype(F32) < count, lax.rsqrt(sq / D + EPS), 0.0)
    pooled = jnp.sum(res[...] * weight, axis=0, keepdims=True) / count
    ahead = jnp.concatenate([pooled[:, t * 256 : t * 256 + 128] for t in range(4)], axis=0)
    behind = jnp.concatenate([pooled[:, t * 256 + 128 : t * 256 + 256] for t in range(4)], axis=0)
    for r, out in enumerate((o0, o1, o2, o3)):
        one = jnp.where(zb == r // 2, ahead, behind)
        two = jnp.where(zb == r // 2, behind, ahead)
        part = jnp.concatenate([one, two], axis=0)
        out[...] = jnp.where(k == r % 2, part, pltpu.roll(part, 64, 1))


def pool(place, counts, res, sqs):
    part = shape((8, 128), F32)
    return pl.pallas_call(
        pool_kernel,
        out_shape=(part,) * 4,
        in_specs=[SMEM] + [VMEM] * 6,
        out_specs=(VMEM,) * 4,
        compiler_params=PARAMS,
        name="pool",
    )(place, counts, res, *sqs)


def code_kernel(place, a, b, c, d, w0, w1, w2, w3, out, left):
    zh = place[5]
    left[...] = a[...] + b[...] + c[...] + d[...]
    total = jnp.zeros((8, 256), F32)
    for s, w in enumerate((w0, w1, w2, w3)):
        row = (zh - s + 4) % 4
        one = jnp.broadcast_to(left[pl.ds(row, 1), :], (8, 128))
        two = jnp.broadcast_to(left[pl.ds(row + 4, 1), :], (8, 128))
        piece = jnp.concatenate([one, two], axis=1).astype(BF16)
        total += jnp.dot(piece, w[...], preferred_element_type=F32)
    for t in range(2):
        left[t : t + 1, :] = total[0:1, t * 128 : t * 128 + 128]
    out[...] = jnp.broadcast_to(left[0:2][None], (64, 2, 128))


def code_part(place, pieces, ws):
    return pl.pallas_call(
        code_kernel,
        out_shape=shape((64, 2, 128), F32),
        in_specs=[SMEM] + [VMEM] * 8,
        out_specs=VMEM,
        scratch_shapes=[pltpu.VMEM((8, 128), F32)],
        compiler_params=PARAMS,
        name="code_part",
    )(place, *pieces, *ws)


def exchange(x, step, falling):
    col = lanes(x.shape)
    upper = (col & step) != 0
    other = jnp.where(upper, pltpu.roll(x, step, 1), pltpu.roll(x, 128 - step, 1))
    return jnp.where(upper ^ falling, jnp.maximum(x, other), jnp.minimum(x, other))


def bitonic_merge(x, falling):
    for step in (64, 32, 16, 8, 4, 2, 1):
        x = exchange(x, step, falling)
    return x


def bitonic_sort(x, falling):
    col = lanes(x.shape)
    for size in (2, 4, 8, 16, 32, 64, 128):
        way = falling if size == 128 else falling ^ ((col & size) != 0)
        step = size // 2
        while step:
            x = exchange(x, step, way)
            step //= 2
    return x


def halves_far(v, apart, falling):
    out = list(v)
    for i in range(len(v)):
        if i & apart == 0:
            high, low = jnp.maximum(v[i], v[i + apart]), jnp.minimum(v[i], v[i + apart])
            way = falling(i)
            if way is True:
                out[i], out[i + apart] = high, low
            elif way is False:
                out[i], out[i + apart] = low, high
            else:
                out[i] = jnp.where(way, high, low)
                out[i + apart] = jnp.where(way, low, high)
    return out


def halves_near(v, step, falling):
    upper = (rows_of((8, 128)) & step) != 0
    out = []
    for i, x in enumerate(v):
        other = pltpu.roll(x, step, 0)
        if step != 4:
            other = jnp.where(upper, other, pltpu.roll(x, 8 - step, 0))
        way = falling(i)
        if way is True:
            take = ~upper
        elif way is False:
            take = upper
        else:
            take = upper ^ way
        out.append(jnp.where(take, jnp.maximum(x, other), jnp.minimum(x, other)))
    return out


def column_step(v, step, falling):
    if step >= 8:
        return halves_far(v, step // 8, falling)
    return halves_near(v, step, falling)


def column_merge(v, falling):
    for step in (64, 32, 16, 8, 4, 2, 1):
        v = column_step(v, step, lambda i: falling)
    return v


def column_sort(v, falling):
    sub = rows_of((8, 128))
    for size in (2, 4, 8, 16, 32, 64, 128):

        def way(i, size=size):
            if size == 128:
                return falling
            if size >= 8:
                return (i * 8) & size == 0
            return (sub & size) == 0

        step = size // 2
        while step:
            v = column_step(v, step, way)
            step //= 2
    return v


def columns_of(x):
    return [x[i * 8 : i * 8 + 8] for i in range(16)]


def rows_of(like):
    return lax.broadcasted_iota(jnp.int32, like, 0)


def score_kernel(place, c0, c1, c2, c3, docs, lists, *, scale):
    k, zb = place[1], place[6]
    at = zb * 2 + k
    dims = (((1,), (1,)), ((), ()))
    scores = jnp.zeros((16, 512), F32)
    for j in range(4):
        piece = c0[...]
        for r, c in ((1, c1), (2, c2), (3, c3)):
            piece = jnp.where(at == j ^ r, c[...], piece)
        part = docs[:, j * 256 : j * 256 + 256]
        scores += lax.dot_general(piece, part, dims, preferred_element_type=F32)
    scores = scores * scale
    x = jnp.concatenate([scores[:, c * 128 : c * 128 + 128] for c in range(4)] * 2, axis=0)
    lane = lanes((8, 128))
    v = column_sort(columns_of(x.T), lane & 32 == 0)
    v = [jnp.maximum(a, pltpu.roll(a, 96, 1)) for a in v]
    v = column_merge(v, lane & 16 == 0)
    v = [jnp.maximum(a, pltpu.roll(a, 112, 1)) for a in v]
    v = column_merge(v, lane * 0 + k == 0)
    lists[...] = jnp.concatenate(v, axis=0).T[0:16]


def local_lists(place, pieces, docs):
    def body(*refs):
        score_kernel(*refs, scale=1.0 / math.sqrt(docs.shape[1]))

    return pl.pallas_call(
        body,
        out_shape=shape((16, 128), F32),
        in_specs=[SMEM] + [VMEM] * 5,
        out_specs=VMEM,
        compiler_params=PARAMS,
        name="scores",
    )(place, *pieces, docs)


def pair_kernel(place, a, b, o0, o1, o2, o3, held):
    y = place[0]
    x = jnp.maximum(a[...], b[...])
    turn = (rows_of((16, 128)) // 4 - y + 4) % 4
    held[...] = bitonic_merge(x, turn % 2 == 0)
    for d, o in enumerate((o0, o1, o2, o3)):
        o[...] = held[pl.ds(pl.multiple_of(((y + d) % 4) * 4, 4), 4), :]


def pair_lists(place, a, b):
    four = shape((4, 128), F32)
    return pl.pallas_call(
        pair_kernel,
        out_shape=(four,) * 4,
        in_specs=[SMEM] + [VMEM] * 2,
        out_specs=(VMEM,) * 4,
        scratch_shapes=[pltpu.VMEM((16, 128), F32)],
        compiler_params=PARAMS,
        name="pair_lists",
    )(place, a, b)


def four_kernel(place, a, b, c, d, out):
    odd = place[3]
    x = jnp.concatenate(
        [jnp.maximum(a[...], b[...]), jnp.maximum(c[...], d[...])], axis=0
    )
    x = bitonic_merge(x, rows_of((8, 128)) < 4)
    x = jnp.maximum(x, pltpu.roll(x, 4, 0))
    x = bitonic_merge(x, (rows_of((8, 128)) * 0 + odd) == 0)
    out[...] = jnp.broadcast_to(x[0:4][None], (128, 4, 128))


def four_lists(place, lists):
    return pl.pallas_call(
        four_kernel,
        out_shape=shape((128, 4, 128), F32),
        in_specs=[SMEM] + [VMEM] * 4,
        out_specs=VMEM,
        compiler_params=PARAMS,
        name="four_lists",
    )(place, *lists)


def final_kernel(x_ref, out):
    lane = lanes((8, 128))
    tiles = []
    for y in range(4):
        v = columns_of(x_ref[y * 128 : y * 128 + 128, :].T)
        tiles.append([jnp.maximum(a, pltpu.roll(a, 64, 1)) for a in v])
    first = [jnp.where(lane < 64, a, b) for a, b in zip(tiles[0], tiles[1])]
    second = [jnp.where(lane < 64, a, b) for a, b in zip(tiles[2], tiles[3])]
    first = column_merge(first, lane & 32 == 0)
    second = column_merge(second, lane & 32 == 0)
    v = [
        jnp.where(
            lane & 32 == 0,
            jnp.maximum(a, pltpu.roll(a, 96, 1)),
            jnp.maximum(b, pltpu.roll(b, 32, 1)),
        )
        for a, b in zip(first, second)
    ]
    for near in (16, 8, 4):
        v = column_merge(v, lane & near == 0)
        v = [jnp.maximum(a, pltpu.roll(a, 128 - near, 1)) for a in v]
    v = column_merge(v, True)
    x = jnp.concatenate(v, axis=0).T
    for y, row in enumerate((0, 64, 32, 96)):
        out[y * 4 : y * 4 + 4, :] = x[row : row + 4, 0:TOPK]


def final_lists(x):
    return pl.pallas_call(
        final_kernel,
        out_shape=shape((16, TOPK), F32),
        in_specs=[VMEM],
        out_specs=VMEM,
        compiler_params=PARAMS,
        name="final_lists",
    )(x)


def per_device(hidden_in, lengths, gate_weight, up_weight, down_weight, code_weight, corpus_codes):
    y, x, zh, zb, k = (lax.axis_index(a) for a in QUERY_CORPUS)
    place = jnp.stack([y, k, 16 * k + 8 * zb, x // 2, 4 * zh, zh, zb, x]).astype(jnp.int32)

    own, other, *quarters = pack(place, hidden_in.T, code_weight)
    swap = [(a * 4 + b, b * 4 + a) for a in range(4) for b in range(4)]
    straight = [(s * 2 + c, t * 2 + c) for s, t in swap for c in range(2)]
    crossed = [(s * 2 + c, t * 2 + 1 - c) for s, t in swap for c in range(2)]
    own = lax.ppermute(own, ("y", "x", "k"), straight)
    other = lax.ppermute(other, ("y", "x", "k"), crossed)
    gate_rows, up_rows = gate_weight.T, up_weight.T
    gate_peer, up_peer, down_peer = (to_peer(w) for w in (gate_rows, up_rows, down_weight))
    flips = [[(i, i ^ r) for i in range(4)] for r in range(4)]
    quarters[1:] = [lax.ppermute(quarters[r], ("zb", "k"), flips[r]) for r in (1, 2, 3)]
    own, other, gate_peer, up_peer, down_peer, quarters = lax.optimization_barrier(
        (own, other, gate_peer, up_peer, down_peer, quarters)
    )
    gathered = lax.all_to_all(fan(place, own, other), XZ, 0, 0, tiled=True)

    rows = lax.ppermute(jnp.concatenate(quarters, axis=0), ("y", "x"), swap)
    rows, gathered = lax.optimization_barrier((rows, gathered))
    turned = [[(i, (i + d) % 4) for i in range(4)] for d in range(4)]
    code_rows = [rows, *(lax.ppermute(rows, "zh", turned[d]) for d in (1, 2, 3))]

    parts = gate_up(place, lengths, gathered, gate_rows, up_rows, gate_peer, up_peer)
    units, counts = hidden_of(place, parts[0], *(shifted(parts[d], d) for d in (1, 2, 3)))
    groups = (units, *(shifted(units, d) for d in (1, 2, 3)))
    groups, code_rows[2] = lax.optimization_barrier((groups, code_rows[2]))
    branch = down(place, groups, down_weight, down_peer)
    branch, code_rows[1], code_rows[3] = lax.optimization_barrier(
        (branch, code_rows[1], code_rows[3])
    )
    branch = lax.all_to_all(branch.reshape(32, 8, 1024), XZ, 0, 0, tiled=True)
    here = lax.dynamic_slice(
        gathered.reshape(4, 8, 64, 128), (x, 0, zh * 16 + zb * 8, 0), (1, 8, 8, 128)
    )[0]
    here = jnp.moveaxis(here, 0, 1).reshape(8, 1024)
    res, sq = residual_of(branch, here)
    sqs = (sq, *(shifted(sq, d) for d in (1, 2, 3)))
    mine = pool(place, counts, res, sqs)
    pieces = (mine[0], *(lax.ppermute(mine[r], ("zb", "k"), flips[r]) for r in (1, 2, 3)))
    part = code_part(place, pieces, code_rows)
    codes = lax.all_to_all(part, ("y", "x", "zh"), 0, 0, tiled=True)
    codes = codes.reshape(4, 16, 256).sum(axis=0).astype(BF16)
    codes = (codes, *(lax.ppermute(codes, ("zb", "k"), flips[r]) for r in (1, 2, 3)))
    lists = local_lists(place, codes, corpus_codes)
    lists = pair_lists(place, lists, to_peer(lists))
    lists = (lists[0], *(shifted(lists[d], d) for d in (1, 2, 3)))
    lists = four_lists(place, lists)
    arrived = lax.all_to_all(lists, YXZ, 0, 0, tiled=True)
    return final_lists(arrived.reshape(512, 128))


def solution(mesh):
    split = Mesh(mesh.devices.reshape(4, 4, 4, 2, 2), QUERY_CORPUS)
    return jax.shard_map(
        per_device,
        mesh=split,
        in_specs=(
            P("y", CORPUS),
            P("y"),
            P("y", CORPUS),
            P("y", CORPUS),
            P(CORPUS, "y"),
            P(CORPUS, None),
            P(QUERY_CORPUS, None),
        ),
        out_specs=P(),
        check_vma=False,
    )
```

```python
import math

import jax
import jax.numpy as jnp
from jax import lax
from jax.experimental import pallas as pl
from jax.experimental.pallas import tpu as pltpu
from jax.sharding import Mesh
from jax.sharding import PartitionSpec as P

D = 4096
SEQ = 32
TOPK = 100
Z = ("zh", "zb")
XZ = ("x", "zh", "zb")
YXZ = ("y", "x", "zh", "zb")
CORPUS = ("x", "zh", "zb", "k")
QUERY_CORPUS = ("y", "x", "zh", "zb", "k")
EPS = 1e-05
F32 = jnp.float32
BF16 = jnp.bfloat16
PARAMS = pltpu.CompilerParams(vmem_limit_bytes=32 * 1024 * 1024)
VMEM = pl.BlockSpec(memory_space=pltpu.VMEM)
SMEM = pl.BlockSpec(memory_space=pltpu.SMEM)


def shape(dims, dtype):
    return jax.ShapeDtypeStruct(dims, dtype)


def to_peer(x):
    return lax.ppermute(x, "k", [(0, 1), (1, 0)])


def shifted(x, d):
    return lax.ppermute(x, "y", [(i, (i + d) % 4) for i in range(4)])


def spread(x, axes, peers):
    copies = jnp.broadcast_to(x[None], (peers, *x.shape))
    return lax.all_to_all(copies, axes, 0, 0, tiled=True)


def lanes(like):
    return lax.broadcasted_iota(jnp.int32, like, 1)


def pack_kernel(place, h, own, other):
    k = place[1]
    x = h[...].astype(F32).T
    for q in range(4):
        one = x[q * 32 : q * 32 + 16, :]
        two = x[q * 32 + 16 : q * 32 + 32, :]
        own[q * 16 : q * 16 + 16, :] = jnp.where(k == 0, one, two).astype(BF16)
        other[q * 16 : q * 16 + 16, :] = jnp.where(k == 0, two, one).astype(BF16)


def pack(place, h):
    part = shape((64, 64), BF16)
    return pl.pallas_call(
        pack_kernel,
        out_shape=(part, part),
        in_specs=[SMEM, VMEM],
        out_specs=(VMEM,) * 2,
        compiler_params=PARAMS,
        name="pack",
    )(place, h)


def gate_up_kernel(place, lengths, h, g0, u0, g1, u1, o0, o1, o2, o3, lhs, wide):
    y = place[0]
    for d in range(4):
        i = (y + d) % 4
        for z in range(8):
            lhs[d * 64 : d * 64 + 64, z * 128 : z * 128 + 128] = h[i * 8 + z]
    left = lhs[...]
    widened = left.astype(F32)
    sq = jnp.sum(widened * widened, axis=1, keepdims=True)
    top = sq.astype(BF16).astype(F32)
    mid = (sq - top).astype(BF16).astype(F32)
    low = sq - top - mid
    col = lanes((256, 256))
    wide[...] = jnp.zeros((256, 256), F32)
    for b, w in enumerate((g0, u0, g1, u1)):
        wide[:, 0:224] = lax.dot_general(
            left, w[...], (((1,), (1,)), ((), ())), preferred_element_type=F32
        )
        block = wide[...]
        if b == 0:
            block = jnp.where(col == 224, top, block)
            block = jnp.where(col == 225, mid, block)
            block = jnp.where(col == 226, low, block)
            for q in range(4):
                block = jnp.where(col == 228 + q, lengths[q].astype(F32), block)
        block = block.astype(BF16)
        for d, o in enumerate((o0, o1, o2, o3)):
            o[:, b * 256 : b * 256 + 256] = block[d * 64 : d * 64 + 64]


def gate_up(place, lengths, h, g0, u0, g1, u1):
    part = shape((64, 1024), BF16)
    return pl.pallas_call(
        gate_up_kernel,
        out_shape=(part,) * 4,
        in_specs=[SMEM] * 2 + [VMEM] * 5,
        out_specs=(VMEM,) * 4,
        scratch_shapes=[pltpu.VMEM((256, 1024), BF16), pltpu.VMEM((256, 256), F32)],
        compiler_params=PARAMS,
        name="gate_up",
    )(place, lengths, h, g0, u0, g1, u1)


def hidden_kernel(place, a, b, c, d, out, counts):
    y, x = place[0], place[7]
    held = jnp.zeros((8, 128), F32)
    for s, part in enumerate((a, b, c, d)):
        held = jnp.where((y - s + 4) % 4 == x, part[0:8, 128:256].astype(F32), held)
    counts[...] = held
    total = a[...].astype(F32) + b[...].astype(F32) + c[...].astype(F32) + d[...].astype(F32)
    col = lanes((64, 256))
    first = total[:, 0:256]
    sq = jnp.sum(jnp.where((col >= 224) & (col < 227), first, 0.0), axis=1, keepdims=True)
    r = lax.rsqrt(sq / D + EPS)
    for b in range(2):
        gate = total[:, b * 512 : b * 512 + 256] * r
        up = total[:, b * 512 + 256 : b * 512 + 512] * r
        units = gate / (1.0 + jnp.exp(-gate)) * up
        out[:, b * 256 : b * 256 + 256] = jnp.where(col < 224, units, 0.0).astype(BF16)


def hidden_of(place, a, b, c, d):
    return pl.pallas_call(
        hidden_kernel,
        out_shape=(shape((64, 512), BF16), shape((8, 128), F32)),
        in_specs=[SMEM] + [VMEM] * 4,
        out_specs=(VMEM,) * 2,
        compiler_params=PARAMS,
        name="hidden_units",
    )(place, a, b, c, d)


def down_kernel(place, a, b, c, d, w0, w1, out, lhs):
    y = place[0]
    for s, part in enumerate((a, b, c, d)):
        at = pl.multiple_of(((y - s + 4) % 4) * 64, 64)
        lhs[pl.ds(at, 64), :] = part[...]
    total = jnp.dot(lhs[:, 0:224], w0[...], preferred_element_type=F32)
    total += jnp.dot(lhs[:, 256:480], w1[...], preferred_element_type=F32)
    out[...] = total.astype(BF16)


def down(place, parts, w0, w1):
    return pl.pallas_call(
        down_kernel,
        out_shape=shape((256, 1024), BF16),
        in_specs=[SMEM] + [VMEM] * 6,
        out_specs=VMEM,
        scratch_shapes=[pltpu.VMEM((256, 512), BF16)],
        compiler_params=PARAMS,
        name="down",
    )(place, *parts, w0, w1)


def residual_kernel(parts, h, res, sq):
    total = h[...].astype(F32)
    for p in range(32):
        total += parts[p].astype(F32)
    res[...] = total
    sq[...] = jnp.broadcast_to(jnp.sum(total * total, axis=1, keepdims=True), (8, 128))


def residual_of(parts, h):
    return pl.pallas_call(
        residual_kernel,
        out_shape=(shape((8, 1024), F32), shape((8, 128), F32)),
        in_specs=[VMEM] * 2,
        out_specs=(VMEM,) * 2,
        compiler_params=PARAMS,
        name="residual",
    )(parts, h)


def pool_kernel(place, counts, res, a, b, c, d, same, other):
    first, zh, zb = place[2], place[5], place[6]
    sq = (a[...] + b[...] + c[...] + d[...])[:, 0:1]
    slots = lax.broadcasted_iota(jnp.int32, (8, 1), 0) + first
    held = jnp.where(lanes((1, 128)) == 100 + zh, counts[0:1, :], 0.0)
    count = jnp.max(held, axis=1, keepdims=True)
    weight = jnp.where(slots.astype(F32) < count, lax.rsqrt(sq / D + EPS), 0.0)
    pooled = jnp.sum(res[...] * weight, axis=0, keepdims=True) / count
    ahead = jnp.concatenate([pooled[:, t * 256 : t * 256 + 128] for t in range(4)], axis=0)
    behind = jnp.concatenate([pooled[:, t * 256 + 128 : t * 256 + 256] for t in range(4)], axis=0)
    same[...] = jnp.where(zb == 0, ahead, behind)
    other[...] = jnp.where(zb == 0, behind, ahead)


def pool(place, counts, res, sqs):
    part = shape((4, 128), F32)
    return pl.pallas_call(
        pool_kernel,
        out_shape=(part,) * 2,
        in_specs=[SMEM] + [VMEM] * 6,
        out_specs=(VMEM,) * 2,
        compiler_params=PARAMS,
        name="pool",
    )(place, counts, res, *sqs)


def code_kernel(place, a, b, c, d, w0, w1, w2, w3, out, left):
    zh = place[5]
    left[...] = a[...] + b[...] + c[...] + d[...]
    total = jnp.zeros((8, 512), F32)
    for s, w in enumerate((w0, w1, w2, w3)):
        piece = jnp.broadcast_to(left[pl.ds((zh - s + 4) % 4, 1), :], (8, 128))
        total += jnp.dot(piece.astype(BF16), w[...], preferred_element_type=F32)
    for t in range(4):
        out[t : t + 1, :] = total[0:1, t * 128 : t * 128 + 128]


def code_part(place, pieces, ws):
    return pl.pallas_call(
        code_kernel,
        out_shape=shape((4, 128), F32),
        in_specs=[SMEM] + [VMEM] * 8,
        out_specs=VMEM,
        scratch_shapes=[pltpu.VMEM((4, 128), F32)],
        compiler_params=PARAMS,
        name="code_part",
    )(place, *pieces, *ws)


def exchange(x, step, falling):
    col = lanes(x.shape)
    upper = (col & step) != 0
    other = jnp.where(upper, pltpu.roll(x, step, 1), pltpu.roll(x, 128 - step, 1))
    return jnp.where(upper ^ falling, jnp.maximum(x, other), jnp.minimum(x, other))


def bitonic_merge(x, falling):
    for step in (64, 32, 16, 8, 4, 2, 1):
        x = exchange(x, step, falling)
    return x


def bitonic_sort(x, falling):
    col = lanes(x.shape)
    for size in (2, 4, 8, 16, 32, 64, 128):
        way = falling if size == 128 else falling ^ ((col & size) != 0)
        step = size // 2
        while step:
            x = exchange(x, step, way)
            step //= 2
    return x


def halves_far(v, apart, falling):
    out = list(v)
    for i in range(len(v)):
        if i & apart == 0:
            high, low = jnp.maximum(v[i], v[i + apart]), jnp.minimum(v[i], v[i + apart])
            way = falling(i)
            if way is True:
                out[i], out[i + apart] = high, low
            elif way is False:
                out[i], out[i + apart] = low, high
            else:
                out[i] = jnp.where(way, high, low)
                out[i + apart] = jnp.where(way, low, high)
    return out


def halves_near(v, step, falling):
    upper = (rows_of((8, 128)) & step) != 0
    out = []
    for i, x in enumerate(v):
        other = pltpu.roll(x, step, 0)
        if step != 4:
            other = jnp.where(upper, other, pltpu.roll(x, 8 - step, 0))
        way = falling(i)
        if way is True:
            take = ~upper
        elif way is False:
            take = upper
        else:
            take = upper ^ way
        out.append(jnp.where(take, jnp.maximum(x, other), jnp.minimum(x, other)))
    return out


def column_step(v, step, falling):
    if step >= 8:
        return halves_far(v, step // 8, falling)
    return halves_near(v, step, falling)


def column_merge(v, falling):
    for step in (64, 32, 16, 8, 4, 2, 1):
        v = column_step(v, step, lambda i: falling)
    return v


def column_sort(v, falling):
    sub = rows_of((8, 128))
    for size in (2, 4, 8, 16, 32, 64, 128):

        def way(i, size=size):
            if size == 128:
                return falling
            if size >= 8:
                return (i * 8) & size == 0
            return (sub & size) == 0

        step = size // 2
        while step:
            v = column_step(v, step, way)
            step //= 2
    return v


def columns_of(x):
    return [x[i * 8 : i * 8 + 8] for i in range(16)]


def rows_of(like):
    return lax.broadcasted_iota(jnp.int32, like, 0)


def score_kernel(place, mine, theirs, docs, lists, *, scale):
    k = place[1]
    own, peer = mine[...], theirs[...]
    low = jnp.where(k == 0, own, peer)
    high = jnp.where(k == 0, peer, own)
    dims = (((1,), (1,)), ((), ()))
    scores = lax.dot_general(low, docs[:, 0:512], dims, preferred_element_type=F32)
    scores += lax.dot_general(high, docs[:, 512:1024], dims, preferred_element_type=F32)
    scores = scores * scale
    x = jnp.concatenate([scores[:, c * 128 : c * 128 + 128] for c in range(4)] * 2, axis=0)
    lane = lanes((8, 128))
    v = column_sort(columns_of(x.T), lane & 32 == 0)
    v = [jnp.maximum(a, pltpu.roll(a, 96, 1)) for a in v]
    v = column_merge(v, lane & 16 == 0)
    v = [jnp.maximum(a, pltpu.roll(a, 112, 1)) for a in v]
    v = column_merge(v, lane * 0 + k == 0)
    lists[...] = jnp.concatenate(v, axis=0).T[0:16]


def local_lists(place, mine, theirs, docs):
    def body(*refs):
        score_kernel(*refs, scale=1.0 / math.sqrt(docs.shape[1]))

    return pl.pallas_call(
        body,
        out_shape=shape((16, 128), F32),
        in_specs=[SMEM] + [VMEM] * 3,
        out_specs=VMEM,
        compiler_params=PARAMS,
        name="scores",
    )(place, mine, theirs, docs)


def pair_kernel(place, a, b, o0, o1, o2, o3, held):
    y = place[0]
    x = jnp.maximum(a[...], b[...])
    turn = (rows_of((16, 128)) // 4 - y + 4) % 4
    held[...] = bitonic_merge(x, turn % 2 == 0)
    for d, o in enumerate((o0, o1, o2, o3)):
        o[...] = held[pl.ds(pl.multiple_of(((y + d) % 4) * 4, 4), 4), :]


def pair_lists(place, a, b):
    four = shape((4, 128), F32)
    return pl.pallas_call(
        pair_kernel,
        out_shape=(four,) * 4,
        in_specs=[SMEM] + [VMEM] * 2,
        out_specs=(VMEM,) * 4,
        scratch_shapes=[pltpu.VMEM((16, 128), F32)],
        compiler_params=PARAMS,
        name="pair_lists",
    )(place, a, b)


def four_kernel(place, a, b, c, d, out):
    odd = place[3]
    x = jnp.concatenate(
        [jnp.maximum(a[...], b[...]), jnp.maximum(c[...], d[...])], axis=0
    )
    x = bitonic_merge(x, rows_of((8, 128)) < 4)
    x = jnp.maximum(x, pltpu.roll(x, 4, 0))
    x = bitonic_merge(x, (rows_of((8, 128)) * 0 + odd) == 0)
    out[...] = jnp.broadcast_to(x[0:4][None], (128, 4, 128))


def four_lists(place, lists):
    return pl.pallas_call(
        four_kernel,
        out_shape=shape((128, 4, 128), F32),
        in_specs=[SMEM] + [VMEM] * 4,
        out_specs=VMEM,
        compiler_params=PARAMS,
        name="four_lists",
    )(place, *lists)


def final_kernel(x_ref, out):
    lane = lanes((8, 128))
    tiles = []
    for y in range(4):
        v = columns_of(x_ref[y * 128 : y * 128 + 128, :].T)
        tiles.append([jnp.maximum(a, pltpu.roll(a, 64, 1)) for a in v])
    first = [jnp.where(lane < 64, a, b) for a, b in zip(tiles[0], tiles[1])]
    second = [jnp.where(lane < 64, a, b) for a, b in zip(tiles[2], tiles[3])]
    first = column_merge(first, lane & 32 == 0)
    second = column_merge(second, lane & 32 == 0)
    v = [
        jnp.where(
            lane & 32 == 0,
            jnp.maximum(a, pltpu.roll(a, 96, 1)),
            jnp.maximum(b, pltpu.roll(b, 32, 1)),
        )
        for a, b in zip(first, second)
    ]
    for near in (16, 8, 4):
        v = column_merge(v, lane & near == 0)
        v = [jnp.maximum(a, pltpu.roll(a, 128 - near, 1)) for a in v]
    v = column_merge(v, True)
    x = jnp.concatenate(v, axis=0).T
    for y, row in enumerate((0, 64, 32, 96)):
        out[y * 4 : y * 4 + 4, :] = x[row : row + 4, 0:TOPK]


def final_lists(x):
    return pl.pallas_call(
        final_kernel,
        out_shape=shape((16, TOPK), F32),
        in_specs=[VMEM],
        out_specs=VMEM,
        compiler_params=PARAMS,
        name="final_lists",
    )(x)


def per_device(hidden_in, lengths, gate_weight, up_weight, down_weight, code_weight, corpus_codes):
    y, x, zh, zb, k = (lax.axis_index(a) for a in QUERY_CORPUS)
    place = jnp.stack([y, k, 16 * k + 8 * zb, x // 2, 4 * zh, zh, zb, x]).astype(jnp.int32)

    own, other = pack(place, hidden_in.T)
    swap = [(a * 4 + b, b * 4 + a) for a in range(4) for b in range(4)]
    straight = [(s * 2 + c, t * 2 + c) for s, t in swap for c in range(2)]
    crossed = [(s * 2 + c, t * 2 + 1 - c) for s, t in swap for c in range(2)]
    own = lax.ppermute(own, ("y", "x", "k"), straight)
    other = lax.ppermute(other, ("y", "x", "k"), crossed)
    block = jnp.where(
        k == 0, jnp.concatenate([own, other], axis=1), jnp.concatenate([other, own], axis=1)
    )
    gate_rows, up_rows = gate_weight.T, up_weight.T
    gate_peer, up_peer, down_peer = (to_peer(w) for w in (gate_rows, up_rows, down_weight))
    block, gate_peer, up_peer, down_peer = lax.optimization_barrier(
        (block, gate_peer, up_peer, down_peer)
    )
    gathered = spread(block, XZ, 32)

    low, high = code_weight[:, :512], code_weight[:, 512:]
    mine = lax.ppermute(jnp.where(k == 0, low, high), ("y", "x", "k"), straight)
    theirs = lax.ppermute(jnp.where(k == 0, high, low), ("y", "x", "k"), crossed)
    rows = jnp.concatenate(
        [jnp.where(k == 0, mine, theirs), jnp.where(k == 0, theirs, mine)], axis=0
    )
    rows, gathered = lax.optimization_barrier((rows, gathered))
    turned = [[(i, (i + d) % 4) for i in range(4)] for d in range(4)]
    code_rows = [rows, *(lax.ppermute(rows, "zh", turned[d]) for d in (1, 2, 3))]

    parts = gate_up(place, lengths, gathered, gate_rows, up_rows, gate_peer, up_peer)
    units, counts = hidden_of(place, parts[0], *(shifted(parts[d], d) for d in (1, 2, 3)))
    groups = (units, *(shifted(units, d) for d in (1, 2, 3)))
    groups, code_rows[2] = lax.optimization_barrier((groups, code_rows[2]))
    branch = down(place, groups, down_weight, down_peer)
    branch, code_rows[1], code_rows[3] = lax.optimization_barrier(
        (branch, code_rows[1], code_rows[3])
    )
    branch = lax.all_to_all(branch.reshape(32, 8, 1024), XZ, 0, 0, tiled=True)
    here = lax.dynamic_slice(
        gathered.reshape(4, 8, 64, 128), (x, 0, zh * 16 + zb * 8, 0), (1, 8, 8, 128)
    )[0]
    here = jnp.moveaxis(here, 0, 1).reshape(8, 1024)
    res, sq = residual_of(branch, here)
    sqs = (sq, *(shifted(sq, d) for d in (1, 2, 3)))
    same, other = pool(place, counts, res, sqs)
    flips = [[(i, i ^ r) for i in range(4)] for r in range(4)]
    sent = ((same, 1), (other, 2), (other, 3))
    pieces = (same, *(lax.ppermute(a, ("zb", "k"), flips[r]) for a, r in sent))
    part = code_part(place, pieces, code_rows)
    part = part + lax.ppermute(part, "zb", [(0, 1), (1, 0)])
    codes = spread(part, ("y", "x", "zh"), 64)
    codes = codes.reshape(4, 16, 512).sum(axis=0).astype(BF16)
    lists = local_lists(place, codes, to_peer(codes), corpus_codes)
    lists = pair_lists(place, lists, to_peer(lists))
    lists = (lists[0], *(shifted(lists[d], d) for d in (1, 2, 3)))
    lists = four_lists(place, lists)
    arrived = lax.all_to_all(lists, YXZ, 0, 0, tiled=True)
    return final_lists(arrived.reshape(512, 128))


def solution(mesh):
    split = Mesh(mesh.devices.reshape(4, 4, 4, 2, 2), QUERY_CORPUS)
    return jax.shard_map(
        per_device,
        mesh=split,
        in_specs=(
            P("y", CORPUS),
            P("y"),
            P("y", CORPUS),
            P("y", CORPUS),
            P(CORPUS, "y"),
            P(CORPUS, None),
            P(QUERY_CORPUS, None),
        ),
        out_specs=P(),
        check_vma=False,
    )
```

```python
import math

import jax
import jax.numpy as jnp
from jax import lax
from jax.experimental import pallas as pl
from jax.experimental.pallas import tpu as pltpu
from jax.sharding import Mesh
from jax.sharding import PartitionSpec as P

D = 4096
SEQ = 32
TOPK = 100
Z = ("zh", "zb")
XZ = ("x", "zh", "zb")
YXZ = ("y", "x", "zh", "zb")
CORPUS = ("x", "zh", "zb", "k")
QUERY_CORPUS = ("y", "x", "zh", "zb", "k")
EPS = 1e-05
F32 = jnp.float32
BF16 = jnp.bfloat16
PARAMS = pltpu.CompilerParams(vmem_limit_bytes=32 * 1024 * 1024)
VMEM = pl.BlockSpec(memory_space=pltpu.VMEM)
SMEM = pl.BlockSpec(memory_space=pltpu.SMEM)


def shape(dims, dtype):
    return jax.ShapeDtypeStruct(dims, dtype)


def to_peer(x):
    return lax.ppermute(x, "k", [(0, 1), (1, 0)])


def shifted(x, d):
    return lax.ppermute(x, "y", [(i, (i + d) % 4) for i in range(4)])


def spread(x, axes, peers):
    copies = jnp.broadcast_to(x[None], (peers, *x.shape))
    return lax.all_to_all(copies, axes, 0, 0, tiled=True)


def lanes(like):
    return lax.broadcasted_iota(jnp.int32, like, 1)


def pack_kernel(place, h, own, other):
    k = place[1]
    x = h[...].astype(F32).T
    for q in range(4):
        one = x[q * 32 : q * 32 + 16, :]
        two = x[q * 32 + 16 : q * 32 + 32, :]
        own[q * 16 : q * 16 + 16, :] = jnp.where(k == 0, one, two).astype(BF16)
        other[q * 16 : q * 16 + 16, :] = jnp.where(k == 0, two, one).astype(BF16)


def pack(place, h):
    part = shape((64, 64), BF16)
    return pl.pallas_call(
        pack_kernel,
        out_shape=(part, part),
        in_specs=[SMEM, VMEM],
        out_specs=(VMEM,) * 2,
        compiler_params=PARAMS,
        name="pack",
    )(place, h)


def gate_up_kernel(place, lengths, h, g0, u0, g1, u1, o0, o1, o2, o3, lhs, wide):
    y = place[0]
    for d in range(4):
        i = (y + d) % 4
        for z in range(8):
            lhs[d * 64 : d * 64 + 64, z * 128 : z * 128 + 128] = h[i * 8 + z]
    left = lhs[...]
    widened = left.astype(F32)
    sq = jnp.sum(widened * widened, axis=1, keepdims=True)
    top = sq.astype(BF16).astype(F32)
    mid = (sq - top).astype(BF16).astype(F32)
    low = sq - top - mid
    col = lanes((256, 256))
    wide[...] = jnp.zeros((256, 256), F32)
    for b, w in enumerate((g0, u0, g1, u1)):
        wide[:, 0:224] = lax.dot_general(
            left, w[...], (((1,), (1,)), ((), ())), preferred_element_type=F32
        )
        block = wide[...]
        if b == 0:
            block = jnp.where(col == 224, top, block)
            block = jnp.where(col == 225, mid, block)
            block = jnp.where(col == 226, low, block)
            for q in range(4):
                block = jnp.where(col == 228 + q, lengths[q].astype(F32), block)
        block = block.astype(BF16)
        for d, o in enumerate((o0, o1, o2, o3)):
            o[:, b * 256 : b * 256 + 256] = block[d * 64 : d * 64 + 64]


def gate_up(place, lengths, h, g0, u0, g1, u1):
    part = shape((64, 1024), BF16)
    return pl.pallas_call(
        gate_up_kernel,
        out_shape=(part,) * 4,
        in_specs=[SMEM] * 2 + [VMEM] * 5,
        out_specs=(VMEM,) * 4,
        scratch_shapes=[pltpu.VMEM((256, 1024), BF16), pltpu.VMEM((256, 256), F32)],
        compiler_params=PARAMS,
        name="gate_up",
    )(place, lengths, h, g0, u0, g1, u1)


def hidden_kernel(place, a, b, c, d, out, counts):
    y, x = place[0], place[7]
    held = jnp.zeros((8, 128), F32)
    for s, part in enumerate((a, b, c, d)):
        held = jnp.where((y - s + 4) % 4 == x, part[0:8, 128:256].astype(F32), held)
    counts[...] = held
    total = a[...].astype(F32) + b[...].astype(F32) + c[...].astype(F32) + d[...].astype(F32)
    col = lanes((64, 256))
    first = total[:, 0:256]
    sq = jnp.sum(jnp.where((col >= 224) & (col < 227), first, 0.0), axis=1, keepdims=True)
    r = lax.rsqrt(sq / D + EPS)
    for b in range(2):
        gate = total[:, b * 512 : b * 512 + 256] * r
        up = total[:, b * 512 + 256 : b * 512 + 512] * r
        units = gate / (1.0 + jnp.exp(-gate)) * up
        out[:, b * 256 : b * 256 + 256] = jnp.where(col < 224, units, 0.0).astype(BF16)


def hidden_of(place, a, b, c, d):
    return pl.pallas_call(
        hidden_kernel,
        out_shape=(shape((64, 512), BF16), shape((8, 128), F32)),
        in_specs=[SMEM] + [VMEM] * 4,
        out_specs=(VMEM,) * 2,
        compiler_params=PARAMS,
        name="hidden_units",
    )(place, a, b, c, d)


def down_kernel(place, a, b, c, d, w0, w1, out, lhs):
    y = place[0]
    for s, part in enumerate((a, b, c, d)):
        at = pl.multiple_of(((y - s + 4) % 4) * 64, 64)
        lhs[pl.ds(at, 64), :] = part[...]
    total = jnp.dot(lhs[:, 0:224], w0[...], preferred_element_type=F32)
    total += jnp.dot(lhs[:, 256:480], w1[...], preferred_element_type=F32)
    for t in range(8):
        tile = total[:, t * 128 : t * 128 + 128].reshape(16, 16, 128).astype(BF16)
        out[:, t % 2, :, (t // 2) * 128 : (t // 2) * 128 + 128] = tile


def down(place, parts, w0, w1):
    return pl.pallas_call(
        down_kernel,
        out_shape=shape((16, 2, 16, 512), BF16),
        in_specs=[SMEM] + [VMEM] * 6,
        out_specs=VMEM,
        scratch_shapes=[pltpu.VMEM((256, 512), BF16)],
        compiler_params=PARAMS,
        name="down",
    )(place, *parts, w0, w1)


def residual_kernel(parts, h, res, sq):
    total = h[...].astype(F32)
    for p in range(32):
        total += parts[p].astype(F32)
    res[...] = total
    sq[...] = jnp.broadcast_to(jnp.sum(total * total, axis=1, keepdims=True), (16, 128))


def residual_of(parts, h):
    return pl.pallas_call(
        residual_kernel,
        out_shape=(shape((16, 512), F32), shape((16, 128), F32)),
        in_specs=[VMEM] * 2,
        out_specs=(VMEM,) * 2,
        compiler_params=PARAMS,
        name="residual",
    )(parts, h)


def pool_kernel(place, counts, res, a, b, c, d, out):
    first, zh = place[2], place[5]
    sq = (a[...] + b[...] + c[...] + d[...])[:, 0:1]
    slots = lax.broadcasted_iota(jnp.int32, (16, 1), 0) + first
    held = jnp.where(lanes((1, 128)) == 100 + zh, counts[0:1, :], 0.0)
    count = jnp.max(held, axis=1, keepdims=True)
    weight = jnp.where(slots.astype(F32) < count, lax.rsqrt(sq / D + EPS), 0.0)
    pooled = jnp.sum(res[...] * weight, axis=0, keepdims=True) / count
    for t in range(4):
        out[t : t + 1, :] = pooled[:, t * 128 : t * 128 + 128]


def pool(place, counts, res, sqs):
    return pl.pallas_call(
        pool_kernel,
        out_shape=shape((4, 128), F32),
        in_specs=[SMEM] + [VMEM] * 6,
        out_specs=VMEM,
        compiler_params=PARAMS,
        name="pool",
    )(place, counts, res, *sqs)


def code_kernel(place, a, b, w0, w1, w2, w3, out, left):
    zh = place[5]
    left[...] = a[...] + b[...]
    total = jnp.zeros((8, 512), F32)
    for s, w in enumerate((w0, w1, w2, w3)):
        piece = jnp.broadcast_to(left[pl.ds((zh - s + 4) % 4, 1), :], (8, 128))
        total += jnp.dot(piece.astype(BF16), w[...], preferred_element_type=F32)
    for t in range(4):
        out[t : t + 1, :] = total[0:1, t * 128 : t * 128 + 128]


def code_part(place, a, b, ws):
    return pl.pallas_call(
        code_kernel,
        out_shape=shape((4, 128), F32),
        in_specs=[SMEM] + [VMEM] * 6,
        out_specs=VMEM,
        scratch_shapes=[pltpu.VMEM((4, 128), F32)],
        compiler_params=PARAMS,
        name="code_part",
    )(place, a, b, *ws)


def exchange(x, step, falling):
    col = lanes(x.shape)
    upper = (col & step) != 0
    other = jnp.where(upper, pltpu.roll(x, step, 1), pltpu.roll(x, 128 - step, 1))
    return jnp.where(upper ^ falling, jnp.maximum(x, other), jnp.minimum(x, other))


def bitonic_merge(x, falling):
    for step in (64, 32, 16, 8, 4, 2, 1):
        x = exchange(x, step, falling)
    return x


def bitonic_sort(x, falling):
    col = lanes(x.shape)
    for size in (2, 4, 8, 16, 32, 64, 128):
        way = falling if size == 128 else falling ^ ((col & size) != 0)
        step = size // 2
        while step:
            x = exchange(x, step, way)
            step //= 2
    return x


def halves_far(v, apart, falling):
    out = list(v)
    for i in range(len(v)):
        if i & apart == 0:
            high, low = jnp.maximum(v[i], v[i + apart]), jnp.minimum(v[i], v[i + apart])
            way = falling(i)
            if way is True:
                out[i], out[i + apart] = high, low
            elif way is False:
                out[i], out[i + apart] = low, high
            else:
                out[i] = jnp.where(way, high, low)
                out[i + apart] = jnp.where(way, low, high)
    return out


def halves_near(v, step, falling):
    upper = (rows_of((8, 128)) & step) != 0
    out = []
    for i, x in enumerate(v):
        other = pltpu.roll(x, step, 0)
        if step != 4:
            other = jnp.where(upper, other, pltpu.roll(x, 8 - step, 0))
        way = falling(i)
        if way is True:
            take = ~upper
        elif way is False:
            take = upper
        else:
            take = upper ^ way
        out.append(jnp.where(take, jnp.maximum(x, other), jnp.minimum(x, other)))
    return out


def column_step(v, step, falling):
    if step >= 8:
        return halves_far(v, step // 8, falling)
    return halves_near(v, step, falling)


def column_merge(v, falling):
    for step in (64, 32, 16, 8, 4, 2, 1):
        v = column_step(v, step, lambda i: falling)
    return v


def column_sort(v, falling):
    sub = rows_of((8, 128))
    for size in (2, 4, 8, 16, 32, 64, 128):

        def way(i, size=size):
            if size == 128:
                return falling
            if size >= 8:
                return (i * 8) & size == 0
            return (sub & size) == 0

        step = size // 2
        while step:
            v = column_step(v, step, way)
            step //= 2
    return v


def columns_of(x):
    return [x[i * 8 : i * 8 + 8] for i in range(16)]


def rows_of(like):
    return lax.broadcasted_iota(jnp.int32, like, 0)


def score_kernel(place, mine, theirs, docs, lists, *, scale):
    k = place[1]
    own, peer = mine[...], theirs[...]
    low = jnp.where(k == 0, own, peer)
    high = jnp.where(k == 0, peer, own)
    dims = (((1,), (1,)), ((), ()))
    scores = lax.dot_general(low, docs[:, 0:512], dims, preferred_element_type=F32)
    scores += lax.dot_general(high, docs[:, 512:1024], dims, preferred_element_type=F32)
    scores = scores * scale
    x = jnp.concatenate([scores[:, c * 128 : c * 128 + 128] for c in range(4)] * 2, axis=0)
    lane = lanes((8, 128))
    v = column_sort(columns_of(x.T), lane & 32 == 0)
    v = [jnp.maximum(a, pltpu.roll(a, 96, 1)) for a in v]
    v = column_merge(v, lane & 16 == 0)
    v = [jnp.maximum(a, pltpu.roll(a, 112, 1)) for a in v]
    v = column_merge(v, lane * 0 + k == 0)
    lists[...] = jnp.concatenate(v, axis=0).T[0:16]


def local_lists(place, mine, theirs, docs):
    def body(*refs):
        score_kernel(*refs, scale=1.0 / math.sqrt(docs.shape[1]))

    return pl.pallas_call(
        body,
        out_shape=shape((16, 128), F32),
        in_specs=[SMEM] + [VMEM] * 3,
        out_specs=VMEM,
        compiler_params=PARAMS,
        name="scores",
    )(place, mine, theirs, docs)


def pair_kernel(place, a, b, o0, o1, o2, o3, held):
    y = place[0]
    x = jnp.maximum(a[...], b[...])
    turn = (rows_of((16, 128)) // 4 - y + 4) % 4
    held[...] = bitonic_merge(x, turn % 2 == 0)
    for d, o in enumerate((o0, o1, o2, o3)):
        o[...] = held[pl.ds(pl.multiple_of(((y + d) % 4) * 4, 4), 4), :]


def pair_lists(place, a, b):
    four = shape((4, 128), F32)
    return pl.pallas_call(
        pair_kernel,
        out_shape=(four,) * 4,
        in_specs=[SMEM] + [VMEM] * 2,
        out_specs=(VMEM,) * 4,
        scratch_shapes=[pltpu.VMEM((16, 128), F32)],
        compiler_params=PARAMS,
        name="pair_lists",
    )(place, a, b)


def four_kernel(place, a, b, c, d, out):
    odd = place[3]
    x = jnp.concatenate(
        [jnp.maximum(a[...], b[...]), jnp.maximum(c[...], d[...])], axis=0
    )
    x = bitonic_merge(x, rows_of((8, 128)) < 4)
    x = jnp.maximum(x, pltpu.roll(x, 4, 0))
    x = bitonic_merge(x, (rows_of((8, 128)) * 0 + odd) == 0)
    out[...] = jnp.broadcast_to(x[0:4][None], (128, 4, 128))


def four_lists(place, lists):
    return pl.pallas_call(
        four_kernel,
        out_shape=shape((128, 4, 128), F32),
        in_specs=[SMEM] + [VMEM] * 4,
        out_specs=VMEM,
        compiler_params=PARAMS,
        name="four_lists",
    )(place, *lists)


def final_kernel(x_ref, out):
    lane = lanes((8, 128))
    tiles = []
    for y in range(4):
        v = columns_of(x_ref[y * 128 : y * 128 + 128, :].T)
        tiles.append([jnp.maximum(a, pltpu.roll(a, 64, 1)) for a in v])
    first = [jnp.where(lane < 64, a, b) for a, b in zip(tiles[0], tiles[1])]
    second = [jnp.where(lane < 64, a, b) for a, b in zip(tiles[2], tiles[3])]
    first = column_merge(first, lane & 32 == 0)
    second = column_merge(second, lane & 32 == 0)
    v = [
        jnp.where(
            lane & 32 == 0,
            jnp.maximum(a, pltpu.roll(a, 96, 1)),
            jnp.maximum(b, pltpu.roll(b, 32, 1)),
        )
        for a, b in zip(first, second)
    ]
    for near in (16, 8, 4):
        v = column_merge(v, lane & near == 0)
        v = [jnp.maximum(a, pltpu.roll(a, 128 - near, 1)) for a in v]
    v = column_merge(v, True)
    x = jnp.concatenate(v, axis=0).T
    for y, row in enumerate((0, 64, 32, 96)):
        out[y * 4 : y * 4 + 4, :] = x[row : row + 4, 0:TOPK]


def final_lists(x):
    return pl.pallas_call(
        final_kernel,
        out_shape=shape((16, TOPK), F32),
        in_specs=[VMEM],
        out_specs=VMEM,
        compiler_params=PARAMS,
        name="final_lists",
    )(x)


def per_device(hidden_in, lengths, gate_weight, up_weight, down_weight, code_weight, corpus_codes):
    y, x, zh, zb, k = (lax.axis_index(a) for a in QUERY_CORPUS)
    place = jnp.stack([y, k, 16 * k, x // 2, 4 * zh, zh, zb, x]).astype(jnp.int32)

    own, other = pack(place, hidden_in.T)
    swap = [(a * 4 + b, b * 4 + a) for a in range(4) for b in range(4)]
    straight = [(s * 2 + c, t * 2 + c) for s, t in swap for c in range(2)]
    crossed = [(s * 2 + c, t * 2 + 1 - c) for s, t in swap for c in range(2)]
    own = lax.ppermute(own, ("y", "x", "k"), straight)
    other = lax.ppermute(other, ("y", "x", "k"), crossed)
    block = jnp.where(
        k == 0, jnp.concatenate([own, other], axis=1), jnp.concatenate([other, own], axis=1)
    )
    gate_rows, up_rows = gate_weight.T, up_weight.T
    gate_peer, up_peer, down_peer = (to_peer(w) for w in (gate_rows, up_rows, down_weight))
    block, gate_peer, up_peer, down_peer = lax.optimization_barrier(
        (block, gate_peer, up_peer, down_peer)
    )
    gathered = spread(block, XZ, 32)

    low, high = code_weight[:, :512], code_weight[:, 512:]
    mine = lax.ppermute(jnp.where(k == 0, low, high), ("y", "x", "k"), straight)
    theirs = lax.ppermute(jnp.where(k == 0, high, low), ("y", "x", "k"), crossed)
    rows = jnp.concatenate(
        [jnp.where(k == 0, mine, theirs), jnp.where(k == 0, theirs, mine)], axis=0
    )
    rows, gathered = lax.optimization_barrier((rows, gathered))
    turned = [[(i, (i + d) % 4) for i in range(4)] for d in range(4)]
    code_rows = [rows, *(lax.ppermute(rows, "zh", turned[d]) for d in (1, 2, 3))]

    parts = gate_up(place, lengths, gathered, gate_rows, up_rows, gate_peer, up_peer)
    units, counts = hidden_of(place, parts[0], *(shifted(parts[d], d) for d in (1, 2, 3)))
    groups = (units, *(shifted(units, d) for d in (1, 2, 3)))
    groups, code_rows[2] = lax.optimization_barrier((groups, code_rows[2]))
    branch = down(place, groups, down_weight, down_peer)
    branch, code_rows[1], code_rows[3] = lax.optimization_barrier(
        (branch, code_rows[1], code_rows[3])
    )
    branch = lax.all_to_all(branch.reshape(32, 16, 512), XZ, 0, 0, tiled=True)
    here = lax.dynamic_slice(
        gathered.reshape(4, 4, 2, 64, 128), (x, 0, zb, zh * 16, 0), (1, 4, 1, 16, 128)
    )
    here = jnp.moveaxis(here.reshape(4, 16, 128), 0, 1).reshape(16, 512)
    res, sq = residual_of(branch, here)
    sq = sq + lax.ppermute(sq, "zb", [(0, 1), (1, 0)])
    sqs = (sq, *(shifted(sq, d) for d in (1, 2, 3)))
    pooled = pool(place, counts, res, sqs)
    part = code_part(place, pooled, to_peer(pooled), code_rows)
    part = part + lax.ppermute(part, "zb", [(0, 1), (1, 0)])
    codes = spread(part, ("y", "x", "zh"), 64)
    codes = codes.reshape(4, 16, 512).sum(axis=0).astype(BF16)
    lists = local_lists(place, codes, to_peer(codes), corpus_codes)
    lists = pair_lists(place, lists, to_peer(lists))
    lists = (lists[0], *(shifted(lists[d], d) for d in (1, 2, 3)))
    lists = four_lists(place, lists)
    arrived = lax.all_to_all(lists, YXZ, 0, 0, tiled=True)
    return final_lists(arrived.reshape(512, 128))


def solution(mesh):
    split = Mesh(mesh.devices.reshape(4, 4, 4, 2, 2), QUERY_CORPUS)
    return jax.shard_map(
        per_device,
        mesh=split,
        in_specs=(
            P("y", CORPUS),
            P("y"),
            P("y", CORPUS),
            P("y", CORPUS),
            P(CORPUS, "y"),
            P(CORPUS, None),
            P(QUERY_CORPUS, None),
        ),
        out_specs=P(),
        check_vma=False,
    )
```

```python
import math

import jax
import jax.numpy as jnp
from jax import lax
from jax.experimental import pallas as pl
from jax.experimental.pallas import tpu as pltpu
from jax.sharding import Mesh
from jax.sharding import PartitionSpec as P

D = 4096
SEQ = 32
TOPK = 100
Z = ("zh", "zb")
XZ = ("x", "zh", "zb")
YXZ = ("y", "x", "zh", "zb")
CORPUS = ("x", "zh", "zb", "k")
QUERY_CORPUS = ("y", "x", "zh", "zb", "k")
EPS = 1e-05
F32 = jnp.float32
BF16 = jnp.bfloat16
PARAMS = pltpu.CompilerParams(vmem_limit_bytes=32 * 1024 * 1024)
VMEM = pl.BlockSpec(memory_space=pltpu.VMEM)
SMEM = pl.BlockSpec(memory_space=pltpu.SMEM)


def shape(dims, dtype):
    return jax.ShapeDtypeStruct(dims, dtype)


def to_peer(x):
    return lax.ppermute(x, "k", [(0, 1), (1, 0)])


def shifted(x, d):
    return lax.ppermute(x, "y", [(i, (i + d) % 4) for i in range(4)])


def spread(x, axes, peers):
    copies = jnp.broadcast_to(x[None], (peers, *x.shape))
    return lax.all_to_all(copies, axes, 0, 0, tiled=True)


def lanes(like):
    return lax.broadcasted_iota(jnp.int32, like, 1)


def pack_kernel(place, h, own, other):
    k = place[1]
    x = h[...].astype(F32).T
    for q in range(4):
        one = x[q * 32 : q * 32 + 16, :]
        two = x[q * 32 + 16 : q * 32 + 32, :]
        own[q * 16 : q * 16 + 16, :] = jnp.where(k == 0, one, two).astype(BF16)
        other[q * 16 : q * 16 + 16, :] = jnp.where(k == 0, two, one).astype(BF16)


def pack(place, h):
    part = shape((64, 64), BF16)
    return pl.pallas_call(
        pack_kernel,
        out_shape=(part, part),
        in_specs=[SMEM, VMEM],
        out_specs=(VMEM,) * 2,
        compiler_params=PARAMS,
        name="pack",
    )(place, h)


def gate_up_kernel(place, lengths, h, g0, u0, g1, u1, o0, o1, o2, o3, lhs, wide):
    y = place[0]
    for d in range(4):
        i = (y + d) % 4
        for z in range(8):
            lhs[d * 64 : d * 64 + 64, z * 128 : z * 128 + 128] = h[i * 8 + z]
    left = lhs[...]
    widened = left.astype(F32)
    sq = jnp.sum(widened * widened, axis=1, keepdims=True)
    top = sq.astype(BF16).astype(F32)
    mid = (sq - top).astype(BF16).astype(F32)
    low = sq - top - mid
    col = lanes((256, 256))
    wide[...] = jnp.zeros((256, 256), F32)
    for b, w in enumerate((g0, u0, g1, u1)):
        wide[:, 0:224] = lax.dot_general(
            left, w[...], (((1,), (1,)), ((), ())), preferred_element_type=F32
        )
        block = wide[...]
        if b == 0:
            block = jnp.where(col == 224, top, block)
            block = jnp.where(col == 225, mid, block)
            block = jnp.where(col == 226, low, block)
            for q in range(4):
                block = jnp.where(col == 228 + q, lengths[q].astype(F32), block)
        block = block.astype(BF16)
        for d, o in enumerate((o0, o1, o2, o3)):
            o[:, b * 256 : b * 256 + 256] = block[d * 64 : d * 64 + 64]


def gate_up(place, lengths, h, g0, u0, g1, u1):
    part = shape((64, 1024), BF16)
    return pl.pallas_call(
        gate_up_kernel,
        out_shape=(part,) * 4,
        in_specs=[SMEM] * 2 + [VMEM] * 5,
        out_specs=(VMEM,) * 4,
        scratch_shapes=[pltpu.VMEM((256, 1024), BF16), pltpu.VMEM((256, 256), F32)],
        compiler_params=PARAMS,
        name="gate_up",
    )(place, lengths, h, g0, u0, g1, u1)


def hidden_kernel(place, a, b, c, d, out, counts):
    y, x = place[0], place[7]
    held = jnp.zeros((8, 128), F32)
    for s, part in enumerate((a, b, c, d)):
        held = jnp.where((y - s + 4) % 4 == x, part[0:8, 128:256].astype(F32), held)
    counts[...] = held
    total = a[...].astype(F32) + b[...].astype(F32) + c[...].astype(F32) + d[...].astype(F32)
    col = lanes((64, 256))
    first = total[:, 0:256]
    sq = jnp.sum(jnp.where((col >= 224) & (col < 227), first, 0.0), axis=1, keepdims=True)
    r = lax.rsqrt(sq / D + EPS)
    for b in range(2):
        gate = total[:, b * 512 : b * 512 + 256] * r
        up = total[:, b * 512 + 256 : b * 512 + 512] * r
        units = gate / (1.0 + jnp.exp(-gate)) * up
        out[:, b * 256 : b * 256 + 256] = jnp.where(col < 224, units, 0.0).astype(BF16)


def hidden_of(place, a, b, c, d):
    return pl.pallas_call(
        hidden_kernel,
        out_shape=(shape((64, 512), BF16), shape((8, 128), F32)),
        in_specs=[SMEM] + [VMEM] * 4,
        out_specs=(VMEM,) * 2,
        compiler_params=PARAMS,
        name="hidden_units",
    )(place, a, b, c, d)


def down_kernel(place, a, b, c, d, w0, w1, out, lhs):
    y = place[0]
    for s, part in enumerate((a, b, c, d)):
        at = pl.multiple_of(((y - s + 4) % 4) * 64, 64)
        lhs[pl.ds(at, 64), :] = part[...]
    total = jnp.dot(lhs[:, 0:224], w0[...], preferred_element_type=F32)
    total += jnp.dot(lhs[:, 256:480], w1[...], preferred_element_type=F32)
    out[...] = total.astype(BF16)


def down(place, parts, w0, w1):
    return pl.pallas_call(
        down_kernel,
        out_shape=shape((256, 1024), BF16),
        in_specs=[SMEM] + [VMEM] * 6,
        out_specs=VMEM,
        scratch_shapes=[pltpu.VMEM((256, 512), BF16)],
        compiler_params=PARAMS,
        name="down",
    )(place, *parts, w0, w1)


def residual_kernel(parts, h, res, sq):
    total = h[...].astype(F32)
    for p in range(32):
        total += parts[p].astype(F32)
    res[...] = total
    sq[...] = jnp.broadcast_to(jnp.sum(total * total, axis=1, keepdims=True), (8, 128))


def residual_of(parts, h):
    return pl.pallas_call(
        residual_kernel,
        out_shape=(shape((8, 1024), F32), shape((8, 128), F32)),
        in_specs=[VMEM] * 2,
        out_specs=(VMEM,) * 2,
        compiler_params=PARAMS,
        name="residual",
    )(parts, h)


def pool_kernel(place, counts, res, a, b, c, d, same, other):
    first, zh, zb = place[2], place[5], place[6]
    sq = (a[...] + b[...] + c[...] + d[...])[:, 0:1]
    slots = lax.broadcasted_iota(jnp.int32, (8, 1), 0) + first
    held = jnp.where(lanes((1, 128)) == 100 + zh, counts[0:1, :], 0.0)
    count = jnp.max(held, axis=1, keepdims=True)
    weight = jnp.where(slots.astype(F32) < count, lax.rsqrt(sq / D + EPS), 0.0)
    pooled = jnp.sum(res[...] * weight, axis=0, keepdims=True) / count
    ahead = jnp.concatenate([pooled[:, t * 256 : t * 256 + 128] for t in range(4)], axis=0)
    behind = jnp.concatenate([pooled[:, t * 256 + 128 : t * 256 + 256] for t in range(4)], axis=0)
    same[...] = jnp.where(zb == 0, ahead, behind)
    other[...] = jnp.where(zb == 0, behind, ahead)


def pool(place, counts, res, sqs):
    part = shape((4, 128), F32)
    return pl.pallas_call(
        pool_kernel,
        out_shape=(part,) * 2,
        in_specs=[SMEM] + [VMEM] * 6,
        out_specs=(VMEM,) * 2,
        compiler_params=PARAMS,
        name="pool",
    )(place, counts, res, *sqs)


def code_kernel(place, a, b, c, d, w0, w1, w2, w3, out, left):
    zh = place[5]
    left[...] = a[...] + b[...] + c[...] + d[...]
    total = jnp.zeros((8, 512), F32)
    for s, w in enumerate((w0, w1, w2, w3)):
        piece = jnp.broadcast_to(left[pl.ds((zh - s + 4) % 4, 1), :], (8, 128))
        total += jnp.dot(piece.astype(BF16), w[...], preferred_element_type=F32)
    for t in range(4):
        out[t : t + 1, :] = total[0:1, t * 128 : t * 128 + 128]


def code_part(place, pieces, ws):
    return pl.pallas_call(
        code_kernel,
        out_shape=shape((4, 128), F32),
        in_specs=[SMEM] + [VMEM] * 8,
        out_specs=VMEM,
        scratch_shapes=[pltpu.VMEM((4, 128), F32)],
        compiler_params=PARAMS,
        name="code_part",
    )(place, *pieces, *ws)


def exchange(x, step, falling):
    col = lanes(x.shape)
    upper = (col & step) != 0
    other = jnp.where(upper, pltpu.roll(x, step, 1), pltpu.roll(x, 128 - step, 1))
    return jnp.where(upper ^ falling, jnp.maximum(x, other), jnp.minimum(x, other))


def bitonic_merge(x, falling):
    for step in (64, 32, 16, 8, 4, 2, 1):
        x = exchange(x, step, falling)
    return x


def bitonic_sort(x, falling):
    col = lanes(x.shape)
    for size in (2, 4, 8, 16, 32, 64, 128):
        way = falling if size == 128 else falling ^ ((col & size) != 0)
        step = size // 2
        while step:
            x = exchange(x, step, way)
            step //= 2
    return x


def halves_far(v, apart, falling):
    out = list(v)
    for i in range(len(v)):
        if i & apart == 0:
            high, low = jnp.maximum(v[i], v[i + apart]), jnp.minimum(v[i], v[i + apart])
            way = falling(i)
            if way is True:
                out[i], out[i + apart] = high, low
            elif way is False:
                out[i], out[i + apart] = low, high
            else:
                out[i] = jnp.where(way, high, low)
                out[i + apart] = jnp.where(way, low, high)
    return out


def halves_near(v, step, falling):
    upper = (rows_of((8, 128)) & step) != 0
    out = []
    for i, x in enumerate(v):
        other = pltpu.roll(x, step, 0)
        if step != 4:
            other = jnp.where(upper, other, pltpu.roll(x, 8 - step, 0))
        way = falling(i)
        if way is True:
            take = ~upper
        elif way is False:
            take = upper
        else:
            take = upper ^ way
        out.append(jnp.where(take, jnp.maximum(x, other), jnp.minimum(x, other)))
    return out


def column_step(v, step, falling):
    if step >= 8:
        return halves_far(v, step // 8, falling)
    return halves_near(v, step, falling)


def column_merge(v, falling):
    for step in (64, 32, 16, 8, 4, 2, 1):
        v = column_step(v, step, lambda i: falling)
    return v


def column_sort(v, falling):
    sub = rows_of((8, 128))
    for size in (2, 4, 8, 16, 32, 64, 128):

        def way(i, size=size):
            if size == 128:
                return falling
            if size >= 8:
                return (i * 8) & size == 0
            return (sub & size) == 0

        step = size // 2
        while step:
            v = column_step(v, step, way)
            step //= 2
    return v


def columns_of(x):
    return [x[i * 8 : i * 8 + 8] for i in range(16)]


def rows_of(like):
    return lax.broadcasted_iota(jnp.int32, like, 0)


def score_kernel(place, mine, theirs, docs, lists, *, scale):
    k = place[1]
    own, peer = mine[...], theirs[...]
    low = jnp.where(k == 0, own, peer)
    high = jnp.where(k == 0, peer, own)
    dims = (((1,), (1,)), ((), ()))
    scores = lax.dot_general(low, docs[:, 0:512], dims, preferred_element_type=F32)
    scores += lax.dot_general(high, docs[:, 512:1024], dims, preferred_element_type=F32)
    scores = scores * scale
    x = jnp.concatenate([scores[:, c * 128 : c * 128 + 128] for c in range(4)] * 2, axis=0)
    lane = lanes((8, 128))
    v = column_sort(columns_of(x.T), lane & 32 == 0)
    v = [jnp.maximum(a, pltpu.roll(a, 96, 1)) for a in v]
    v = column_merge(v, lane & 16 == 0)
    v = [jnp.maximum(a, pltpu.roll(a, 112, 1)) for a in v]
    v = column_merge(v, lane * 0 + k == 0)
    lists[...] = jnp.concatenate(v, axis=0).T[0:16]


def local_lists(place, mine, theirs, docs):
    def body(*refs):
        score_kernel(*refs, scale=1.0 / math.sqrt(docs.shape[1]))

    return pl.pallas_call(
        body,
        out_shape=shape((16, 128), F32),
        in_specs=[SMEM] + [VMEM] * 3,
        out_specs=VMEM,
        compiler_params=PARAMS,
        name="scores",
    )(place, mine, theirs, docs)


def pair_kernel(place, a, b, o0, o1, o2, o3, held):
    y = place[0]
    x = jnp.maximum(a[...], b[...])
    turn = (rows_of((16, 128)) // 4 - y + 4) % 4
    held[...] = bitonic_merge(x, turn % 2 == 0)
    for d, o in enumerate((o0, o1, o2, o3)):
        o[...] = held[pl.ds(pl.multiple_of(((y + d) % 4) * 4, 4), 4), :]


def pair_lists(place, a, b):
    four = shape((4, 128), F32)
    return pl.pallas_call(
        pair_kernel,
        out_shape=(four,) * 4,
        in_specs=[SMEM] + [VMEM] * 2,
        out_specs=(VMEM,) * 4,
        scratch_shapes=[pltpu.VMEM((16, 128), F32)],
        compiler_params=PARAMS,
        name="pair_lists",
    )(place, a, b)


def four_kernel(place, a, b, c, d, out):
    odd = place[3]
    x = jnp.concatenate(
        [jnp.maximum(a[...], b[...]), jnp.maximum(c[...], d[...])], axis=0
    )
    x = bitonic_merge(x, rows_of((8, 128)) < 4)
    x = jnp.maximum(x, pltpu.roll(x, 4, 0))
    x = bitonic_merge(x, (rows_of((8, 128)) * 0 + odd) == 0)
    out[...] = jnp.broadcast_to(x[0:4][None], (128, 4, 128))


def four_lists(place, lists):
    return pl.pallas_call(
        four_kernel,
        out_shape=shape((128, 4, 128), F32),
        in_specs=[SMEM] + [VMEM] * 4,
        out_specs=VMEM,
        compiler_params=PARAMS,
        name="four_lists",
    )(place, *lists)


def final_kernel(x_ref, out):
    lane = lanes((8, 128))
    tiles = []
    for y in range(4):
        v = columns_of(x_ref[y * 128 : y * 128 + 128, :].T)
        tiles.append([jnp.maximum(a, pltpu.roll(a, 64, 1)) for a in v])
    first = [jnp.where(lane < 64, a, b) for a, b in zip(tiles[0], tiles[1])]
    second = [jnp.where(lane < 64, a, b) for a, b in zip(tiles[2], tiles[3])]
    first = column_merge(first, lane & 32 == 0)
    second = column_merge(second, lane & 32 == 0)
    v = [
        jnp.where(
            lane & 32 == 0,
            jnp.maximum(a, pltpu.roll(a, 96, 1)),
            jnp.maximum(b, pltpu.roll(b, 32, 1)),
        )
        for a, b in zip(first, second)
    ]
    for near in (16, 8, 4):
        v = column_merge(v, lane & near == 0)
        v = [jnp.maximum(a, pltpu.roll(a, 128 - near, 1)) for a in v]
    v = column_merge(v, True)
    x = jnp.concatenate(v, axis=0).T
    for y, row in enumerate((0, 64, 32, 96)):
        out[y * 4 : y * 4 + 4, :] = x[row : row + 4, 0:TOPK]


def final_lists(x):
    return pl.pallas_call(
        final_kernel,
        out_shape=shape((16, TOPK), F32),
        in_specs=[VMEM],
        out_specs=VMEM,
        compiler_params=PARAMS,
        name="final_lists",
    )(x)


def per_device(hidden_in, lengths, gate_weight, up_weight, down_weight, code_weight, corpus_codes):
    y, x, zh, zb, k = (lax.axis_index(a) for a in QUERY_CORPUS)
    place = jnp.stack([y, k, 16 * k + 8 * zb, x // 2, 4 * zh, zh, zb, x]).astype(jnp.int32)

    own, other = pack(place, hidden_in.T)
    swap = [(a * 4 + b, b * 4 + a) for a in range(4) for b in range(4)]
    straight = [(s * 2 + c, t * 2 + c) for s, t in swap for c in range(2)]
    crossed = [(s * 2 + c, t * 2 + 1 - c) for s, t in swap for c in range(2)]
    own = lax.ppermute(own, ("y", "x", "k"), straight)
    other = lax.ppermute(other, ("y", "x", "k"), crossed)
    block = jnp.where(
        k == 0, jnp.concatenate([own, other], axis=1), jnp.concatenate([other, own], axis=1)
    )
    gate_rows, up_rows = gate_weight.T, up_weight.T
    gate_peer, up_peer, down_peer = (to_peer(w) for w in (gate_rows, up_rows, down_weight))
    block, gate_peer, up_peer, down_peer = lax.optimization_barrier(
        (block, gate_peer, up_peer, down_peer)
    )
    gathered = spread(block, XZ, 32)

    low, high = code_weight[:, :512], code_weight[:, 512:]
    mine = lax.ppermute(jnp.where(k == 0, low, high), ("y", "x", "k"), straight)
    theirs = lax.ppermute(jnp.where(k == 0, high, low), ("y", "x", "k"), crossed)
    rows = jnp.concatenate(
        [jnp.where(k == 0, mine, theirs), jnp.where(k == 0, theirs, mine)], axis=0
    )
    rows, gathered = lax.optimization_barrier((rows, gathered))
    turned = [[(i, (i + d) % 4) for i in range(4)] for d in range(4)]
    code_rows = [rows, *(lax.ppermute(rows, "zh", turned[d]) for d in (1, 2, 3))]

    parts = gate_up(place, lengths, gathered, gate_rows, up_rows, gate_peer, up_peer)
    units, counts = hidden_of(place, parts[0], *(shifted(parts[d], d) for d in (1, 2, 3)))
    groups = (units, *(shifted(units, d) for d in (1, 2, 3)))
    groups, code_rows[2] = lax.optimization_barrier((groups, code_rows[2]))
    branch = down(place, groups, down_weight, down_peer)
    branch = lax.all_to_all(branch.reshape(32, 8, 1024), XZ, 0, 0, tiled=True)
    here = lax.dynamic_slice(
        gathered.reshape(4, 8, 64, 128), (x, 0, zh * 16 + zb * 8, 0), (1, 8, 8, 128)
    )[0]
    here = jnp.moveaxis(here, 0, 1).reshape(8, 1024)
    res, sq = residual_of(branch, here)
    sqs = (sq, *(shifted(sq, d) for d in (1, 2, 3)))
    same, other = pool(place, counts, res, sqs)
    flips = [[(i, i ^ r) for i in range(4)] for r in range(4)]
    sent = ((same, 1), (other, 2), (other, 3))
    pieces = (same, *(lax.ppermute(a, ("zb", "k"), flips[r]) for a, r in sent))
    part = code_part(place, pieces, code_rows)
    part = part + lax.ppermute(part, "zb", [(0, 1), (1, 0)])
    codes = spread(part, ("y", "x", "zh"), 64)
    codes = codes.reshape(4, 16, 512).sum(axis=0).astype(BF16)
    lists = local_lists(place, codes, to_peer(codes), corpus_codes)
    lists = pair_lists(place, lists, to_peer(lists))
    lists = (lists[0], *(shifted(lists[d], d) for d in (1, 2, 3)))
    lists = four_lists(place, lists)
    arrived = lax.all_to_all(lists, YXZ, 0, 0, tiled=True)
    return final_lists(arrived.reshape(512, 128))


def solution(mesh):
    split = Mesh(mesh.devices.reshape(4, 4, 4, 2, 2), QUERY_CORPUS)
    return jax.shard_map(
        per_device,
        mesh=split,
        in_specs=(
            P("y", CORPUS),
            P("y"),
            P("y", CORPUS),
            P("y", CORPUS),
            P(CORPUS, "y"),
            P(CORPUS, None),
            P(QUERY_CORPUS, None),
        ),
        out_specs=P(),
        check_vma=False,
    )
```

```python
import math

import jax
import jax.numpy as jnp
from jax import lax
from jax.experimental import pallas as pl
from jax.experimental.pallas import tpu as pltpu
from jax.sharding import Mesh
from jax.sharding import PartitionSpec as P

D = 4096
SEQ = 32
TOPK = 100
Z = ("zh", "zb")
XZ = ("x", "zh", "zb")
YXZ = ("y", "x", "zh", "zb")
CORPUS = ("x", "zh", "zb", "k")
QUERY_CORPUS = ("y", "x", "zh", "zb", "k")
EPS = 1e-05
F32 = jnp.float32
BF16 = jnp.bfloat16
PARAMS = pltpu.CompilerParams(vmem_limit_bytes=32 * 1024 * 1024)
VMEM = pl.BlockSpec(memory_space=pltpu.VMEM)
SMEM = pl.BlockSpec(memory_space=pltpu.SMEM)


def shape(dims, dtype):
    return jax.ShapeDtypeStruct(dims, dtype)


def to_peer(x):
    return lax.ppermute(x, "k", [(0, 1), (1, 0)])


def shifted(x, d):
    return lax.ppermute(x, "y", [(i, (i + d) % 4) for i in range(4)])


def spread(x, axes, peers):
    copies = jnp.broadcast_to(x[None], (peers, *x.shape))
    return lax.all_to_all(copies, axes, 0, 0, tiled=True)


def lanes(like):
    return lax.broadcasted_iota(jnp.int32, like, 1)


def pack_kernel(place, h, own, other):
    k = place[1]
    x = h[...].astype(F32).T
    for q in range(4):
        one = x[q * 32 : q * 32 + 16, :]
        two = x[q * 32 + 16 : q * 32 + 32, :]
        own[q * 16 : q * 16 + 16, :] = jnp.where(k == 0, one, two).astype(BF16)
        other[q * 16 : q * 16 + 16, :] = jnp.where(k == 0, two, one).astype(BF16)


def pack(place, h):
    part = shape((64, 64), BF16)
    return pl.pallas_call(
        pack_kernel,
        out_shape=(part, part),
        in_specs=[SMEM, VMEM],
        out_specs=(VMEM,) * 2,
        compiler_params=PARAMS,
        name="pack",
    )(place, h)


def gate_up_kernel(place, lengths, h, g0, u0, g1, u1, o0, o1, o2, o3, lhs, wide):
    y = place[0]
    for d in range(4):
        i = (y + d) % 4
        for z in range(8):
            lhs[d * 64 : d * 64 + 64, z * 128 : z * 128 + 128] = h[i * 8 + z]
    left = lhs[...]
    widened = left.astype(F32)
    sq = jnp.sum(widened * widened, axis=1, keepdims=True)
    top = sq.astype(BF16).astype(F32)
    mid = (sq - top).astype(BF16).astype(F32)
    low = sq - top - mid
    col = lanes((256, 256))
    wide[...] = jnp.zeros((256, 256), F32)
    for b, w in enumerate((g0, u0, g1, u1)):
        wide[:, 0:224] = lax.dot_general(
            left, w[...], (((1,), (1,)), ((), ())), preferred_element_type=F32
        )
        block = wide[...]
        if b == 0:
            block = jnp.where(col == 224, top, block)
            block = jnp.where(col == 225, mid, block)
            block = jnp.where(col == 226, low, block)
            for q in range(4):
                block = jnp.where(col == 228 + q, lengths[q].astype(F32), block)
        block = block.astype(BF16)
        for d, o in enumerate((o0, o1, o2, o3)):
            o[:, b * 256 : b * 256 + 256] = block[d * 64 : d * 64 + 64]


def gate_up(place, lengths, h, g0, u0, g1, u1):
    part = shape((64, 1024), BF16)
    return pl.pallas_call(
        gate_up_kernel,
        out_shape=(part,) * 4,
        in_specs=[SMEM] * 2 + [VMEM] * 5,
        out_specs=(VMEM,) * 4,
        scratch_shapes=[pltpu.VMEM((256, 1024), BF16), pltpu.VMEM((256, 256), F32)],
        compiler_params=PARAMS,
        name="gate_up",
    )(place, lengths, h, g0, u0, g1, u1)


def hidden_kernel(place, a, b, c, d, out, counts):
    y, x = place[0], place[7]
    held = jnp.zeros((8, 128), F32)
    for s, part in enumerate((a, b, c, d)):
        held = jnp.where((y - s + 4) % 4 == x, part[0:8, 128:256].astype(F32), held)
    counts[...] = held
    total = a[...].astype(F32) + b[...].astype(F32) + c[...].astype(F32) + d[...].astype(F32)
    col = lanes((64, 256))
    first = total[:, 0:256]
    sq = jnp.sum(jnp.where((col >= 224) & (col < 227), first, 0.0), axis=1, keepdims=True)
    r = lax.rsqrt(sq / D + EPS)
    for b in range(2):
        gate = total[:, b * 512 : b * 512 + 256] * r
        up = total[:, b * 512 + 256 : b * 512 + 512] * r
        units = gate / (1.0 + jnp.exp(-gate)) * up
        out[:, b * 256 : b * 256 + 256] = jnp.where(col < 224, units, 0.0).astype(BF16)


def hidden_of(place, a, b, c, d):
    return pl.pallas_call(
        hidden_kernel,
        out_shape=(shape((64, 512), BF16), shape((8, 128), F32)),
        in_specs=[SMEM] + [VMEM] * 4,
        out_specs=(VMEM,) * 2,
        compiler_params=PARAMS,
        name="hidden_units",
    )(place, a, b, c, d)


def down_kernel(place, a, b, c, d, w0, w1, out, lhs):
    y = place[0]
    for s, part in enumerate((a, b, c, d)):
        at = pl.multiple_of(((y - s + 4) % 4) * 64, 64)
        lhs[pl.ds(at, 64), :] = part[...]
    total = jnp.dot(lhs[:, 0:224], w0[...], preferred_element_type=F32)
    total += jnp.dot(lhs[:, 256:480], w1[...], preferred_element_type=F32)
    out[...] = total.astype(BF16)


def down(place, parts, w0, w1):
    return pl.pallas_call(
        down_kernel,
        out_shape=shape((256, 1024), BF16),
        in_specs=[SMEM] + [VMEM] * 6,
        out_specs=VMEM,
        scratch_shapes=[pltpu.VMEM((256, 512), BF16)],
        compiler_params=PARAMS,
        name="down",
    )(place, *parts, w0, w1)


def residual_kernel(parts, h, res, sq):
    total = h[...].astype(F32)
    for p in range(32):
        total += parts[p].astype(F32)
    res[...] = total
    sq[...] = jnp.broadcast_to(jnp.sum(total * total, axis=1, keepdims=True), (8, 128))


def residual_of(parts, h):
    return pl.pallas_call(
        residual_kernel,
        out_shape=(shape((8, 1024), F32), shape((8, 128), F32)),
        in_specs=[VMEM] * 2,
        out_specs=(VMEM,) * 2,
        compiler_params=PARAMS,
        name="residual",
    )(parts, h)


def pool_kernel(place, counts, res, a, b, c, d, same, other):
    first, zh, zb = place[2], place[5], place[6]
    sq = (a[...] + b[...] + c[...] + d[...])[:, 0:1]
    slots = lax.broadcasted_iota(jnp.int32, (8, 1), 0) + first
    held = jnp.where(lanes((1, 128)) == 100 + zh, counts[0:1, :], 0.0)
    count = jnp.max(held, axis=1, keepdims=True)
    weight = jnp.where(slots.astype(F32) < count, lax.rsqrt(sq / D + EPS), 0.0)
    pooled = jnp.sum(res[...] * weight, axis=0, keepdims=True) / count
    ahead = jnp.concatenate([pooled[:, t * 256 : t * 256 + 128] for t in range(4)], axis=0)
    behind = jnp.concatenate([pooled[:, t * 256 + 128 : t * 256 + 256] for t in range(4)], axis=0)
    same[...] = jnp.where(zb == 0, ahead, behind)
    other[...] = jnp.where(zb == 0, behind, ahead)


def pool(place, counts, res, sqs):
    part = shape((4, 128), F32)
    return pl.pallas_call(
        pool_kernel,
        out_shape=(part,) * 2,
        in_specs=[SMEM] + [VMEM] * 6,
        out_specs=(VMEM,) * 2,
        compiler_params=PARAMS,
        name="pool",
    )(place, counts, res, *sqs)


def code_kernel(place, a, b, c, d, near, far, out, left):
    zh = place[5]
    left[...] = a[...] + b[...] + c[...] + d[...]
    total = jnp.zeros((8, 512), F32)
    for w, half, flip in ((near, 0, 0), (near, 1, 1), (far, 0, 3), (far, 1, 2)):
        piece = jnp.broadcast_to(left[pl.ds(zh ^ flip, 1), :], (8, 128)).astype(BF16)
        rows = w[half * 128 : half * 128 + 128, :]
        total += jnp.dot(piece, rows, preferred_element_type=F32)
    for t in range(4):
        out[t : t + 1, :] = total[0:1, t * 128 : t * 128 + 128]


def code_part(place, pieces, ws):
    return pl.pallas_call(
        code_kernel,
        out_shape=shape((4, 128), F32),
        in_specs=[SMEM] + [VMEM] * 6,
        out_specs=VMEM,
        scratch_shapes=[pltpu.VMEM((4, 128), F32)],
        compiler_params=PARAMS,
        name="code_part",
    )(place, *pieces, *ws)


def exchange(x, step, falling):
    col = lanes(x.shape)
    upper = (col & step) != 0
    other = jnp.where(upper, pltpu.roll(x, step, 1), pltpu.roll(x, 128 - step, 1))
    return jnp.where(upper ^ falling, jnp.maximum(x, other), jnp.minimum(x, other))


def bitonic_merge(x, falling):
    for step in (64, 32, 16, 8, 4, 2, 1):
        x = exchange(x, step, falling)
    return x


def bitonic_sort(x, falling):
    col = lanes(x.shape)
    for size in (2, 4, 8, 16, 32, 64, 128):
        way = falling if size == 128 else falling ^ ((col & size) != 0)
        step = size // 2
        while step:
            x = exchange(x, step, way)
            step //= 2
    return x


def halves_far(v, apart, falling):
    out = list(v)
    for i in range(len(v)):
        if i & apart == 0:
            high, low = jnp.maximum(v[i], v[i + apart]), jnp.minimum(v[i], v[i + apart])
            way = falling(i)
            if way is True:
                out[i], out[i + apart] = high, low
            elif way is False:
                out[i], out[i + apart] = low, high
            else:
                out[i] = jnp.where(way, high, low)
                out[i + apart] = jnp.where(way, low, high)
    return out


def halves_near(v, step, falling):
    upper = (rows_of((8, 128)) & step) != 0
    out = []
    for i, x in enumerate(v):
        other = pltpu.roll(x, step, 0)
        if step != 4:
            other = jnp.where(upper, other, pltpu.roll(x, 8 - step, 0))
        way = falling(i)
        if way is True:
            take = ~upper
        elif way is False:
            take = upper
        else:
            take = upper ^ way
        out.append(jnp.where(take, jnp.maximum(x, other), jnp.minimum(x, other)))
    return out


def column_step(v, step, falling):
    if step >= 8:
        return halves_far(v, step // 8, falling)
    return halves_near(v, step, falling)


def column_merge(v, falling):
    for step in (64, 32, 16, 8, 4, 2, 1):
        v = column_step(v, step, lambda i: falling)
    return v


def column_sort(v, falling):
    sub = rows_of((8, 128))
    for size in (2, 4, 8, 16, 32, 64, 128):

        def way(i, size=size):
            if size == 128:
                return falling
            if size >= 8:
                return (i * 8) & size == 0
            return (sub & size) == 0

        step = size // 2
        while step:
            v = column_step(v, step, way)
            step //= 2
    return v


def columns_of(x):
    return [x[i * 8 : i * 8 + 8] for i in range(16)]


def rows_of(like):
    return lax.broadcasted_iota(jnp.int32, like, 0)


def score_kernel(place, mine, theirs, docs, lists, *, scale):
    k = place[1]
    own, peer = mine[...], theirs[...]
    low = jnp.where(k == 0, own, peer)
    high = jnp.where(k == 0, peer, own)
    dims = (((1,), (1,)), ((), ()))
    scores = lax.dot_general(low, docs[:, 0:512], dims, preferred_element_type=F32)
    scores += lax.dot_general(high, docs[:, 512:1024], dims, preferred_element_type=F32)
    scores = scores * scale
    x = jnp.concatenate([scores[:, c * 128 : c * 128 + 128] for c in range(4)] * 2, axis=0)
    lane = lanes((8, 128))
    v = column_sort(columns_of(x.T), lane & 32 == 0)
    v = [jnp.maximum(a, pltpu.roll(a, 96, 1)) for a in v]
    v = column_merge(v, lane & 16 == 0)
    v = [jnp.maximum(a, pltpu.roll(a, 112, 1)) for a in v]
    v = column_merge(v, lane * 0 + k == 0)
    lists[...] = jnp.concatenate(v, axis=0).T[0:16]


def local_lists(place, mine, theirs, docs):
    def body(*refs):
        score_kernel(*refs, scale=1.0 / math.sqrt(docs.shape[1]))

    return pl.pallas_call(
        body,
        out_shape=shape((16, 128), F32),
        in_specs=[SMEM] + [VMEM] * 3,
        out_specs=VMEM,
        compiler_params=PARAMS,
        name="scores",
    )(place, mine, theirs, docs)


def pair_kernel(place, a, b, o0, o1, o2, o3, held):
    y = place[0]
    x = jnp.maximum(a[...], b[...])
    turn = (rows_of((16, 128)) // 4 - y + 4) % 4
    held[...] = bitonic_merge(x, turn % 2 == 0)
    for d, o in enumerate((o0, o1, o2, o3)):
        o[...] = held[pl.ds(pl.multiple_of(((y + d) % 4) * 4, 4), 4), :]


def pair_lists(place, a, b):
    four = shape((4, 128), F32)
    return pl.pallas_call(
        pair_kernel,
        out_shape=(four,) * 4,
        in_specs=[SMEM] + [VMEM] * 2,
        out_specs=(VMEM,) * 4,
        scratch_shapes=[pltpu.VMEM((16, 128), F32)],
        compiler_params=PARAMS,
        name="pair_lists",
    )(place, a, b)


def four_kernel(place, a, b, c, d, out):
    odd = place[3]
    x = jnp.concatenate(
        [jnp.maximum(a[...], b[...]), jnp.maximum(c[...], d[...])], axis=0
    )
    x = bitonic_merge(x, rows_of((8, 128)) < 4)
    x = jnp.maximum(x, pltpu.roll(x, 4, 0))
    x = bitonic_merge(x, (rows_of((8, 128)) * 0 + odd) == 0)
    out[...] = jnp.broadcast_to(x[0:4][None], (128, 4, 128))


def four_lists(place, lists):
    return pl.pallas_call(
        four_kernel,
        out_shape=shape((128, 4, 128), F32),
        in_specs=[SMEM] + [VMEM] * 4,
        out_specs=VMEM,
        compiler_params=PARAMS,
        name="four_lists",
    )(place, *lists)


def final_kernel(x_ref, out):
    lane = lanes((8, 128))
    tiles = []
    for y in range(4):
        v = columns_of(x_ref[y * 128 : y * 128 + 128, :].T)
        tiles.append([jnp.maximum(a, pltpu.roll(a, 64, 1)) for a in v])
    first = [jnp.where(lane < 64, a, b) for a, b in zip(tiles[0], tiles[1])]
    second = [jnp.where(lane < 64, a, b) for a, b in zip(tiles[2], tiles[3])]
    first = column_merge(first, lane & 32 == 0)
    second = column_merge(second, lane & 32 == 0)
    v = [
        jnp.where(
            lane & 32 == 0,
            jnp.maximum(a, pltpu.roll(a, 96, 1)),
            jnp.maximum(b, pltpu.roll(b, 32, 1)),
        )
        for a, b in zip(first, second)
    ]
    for near in (16, 8, 4):
        v = column_merge(v, lane & near == 0)
        v = [jnp.maximum(a, pltpu.roll(a, 128 - near, 1)) for a in v]
    v = column_merge(v, True)
    x = jnp.concatenate(v, axis=0).T
    for y, row in enumerate((0, 64, 32, 96)):
        out[y * 4 : y * 4 + 4, :] = x[row : row + 4, 0:TOPK]


def final_lists(x):
    return pl.pallas_call(
        final_kernel,
        out_shape=shape((16, TOPK), F32),
        in_specs=[VMEM],
        out_specs=VMEM,
        compiler_params=PARAMS,
        name="final_lists",
    )(x)


def per_device(hidden_in, lengths, gate_weight, up_weight, down_weight, code_weight, corpus_codes):
    y, x, zh, zb, k = (lax.axis_index(a) for a in QUERY_CORPUS)
    place = jnp.stack([y, k, 16 * k + 8 * zb, x // 2, 4 * zh, zh, zb, x]).astype(jnp.int32)

    own, other = pack(place, hidden_in.T)
    swap = [(a * 4 + b, b * 4 + a) for a in range(4) for b in range(4)]
    straight = [(s * 2 + c, t * 2 + c) for s, t in swap for c in range(2)]
    crossed = [(s * 2 + c, t * 2 + 1 - c) for s, t in swap for c in range(2)]
    own = lax.ppermute(own, ("y", "x", "k"), straight)
    other = lax.ppermute(other, ("y", "x", "k"), crossed)
    block = jnp.where(
        k == 0, jnp.concatenate([own, other], axis=1), jnp.concatenate([other, own], axis=1)
    )
    gate_rows, up_rows = gate_weight.T, up_weight.T
    gate_peer, up_peer, down_peer = (to_peer(w) for w in (gate_rows, up_rows, down_weight))
    block, gate_peer, up_peer, down_peer = lax.optimization_barrier(
        (block, gate_peer, up_peer, down_peer)
    )
    gathered = spread(block, XZ, 32)

    low, high = code_weight[:, :512], code_weight[:, 512:]
    mine = lax.ppermute(jnp.where(k == 0, low, high), ("y", "x", "k"), straight)
    theirs = lax.ppermute(jnp.where(k == 0, high, low), ("y", "x", "k"), crossed)
    rows = jnp.concatenate(
        [jnp.where(k == 0, mine, theirs), jnp.where(k == 0, theirs, mine)], axis=0
    )
    rows, gathered = lax.optimization_barrier((rows, gathered))

    parts = gate_up(place, lengths, gathered, gate_rows, up_rows, gate_peer, up_peer)
    rows, parts = lax.optimization_barrier((rows, parts))
    near = lax.ppermute(rows, "zh", [(i, i ^ 1) for i in range(4)])
    near = jnp.concatenate([rows, near], axis=0)
    units, counts = hidden_of(place, parts[0], *(shifted(parts[d], d) for d in (1, 2, 3)))
    units, near = lax.optimization_barrier((units, near))
    far = lax.ppermute(near, "zh", [(i, i ^ 3) for i in range(4)])
    groups = (units, *(shifted(units, d) for d in (1, 2, 3)))
    branch = down(place, groups, down_weight, down_peer)
    branch, far = lax.optimization_barrier((branch, far))
    branch = lax.all_to_all(branch.reshape(32, 8, 1024), XZ, 0, 0, tiled=True)
    here = lax.dynamic_slice(
        gathered.reshape(4, 8, 64, 128), (x, 0, zh * 16 + zb * 8, 0), (1, 8, 8, 128)
    )[0]
    here = jnp.moveaxis(here, 0, 1).reshape(8, 1024)
    res, sq = residual_of(branch, here)
    sqs = (sq, *(shifted(sq, d) for d in (1, 2, 3)))
    same, other = pool(place, counts, res, sqs)
    flips = [[(i, i ^ r) for i in range(4)] for r in range(4)]
    sent = ((same, 1), (other, 2), (other, 3))
    pieces = (same, *(lax.ppermute(a, ("zb", "k"), flips[r]) for a, r in sent))
    part = code_part(place, pieces, (near, far))
    part = part + lax.ppermute(part, "zb", [(0, 1), (1, 0)])
    codes = spread(part, ("y", "x", "zh"), 64)
    codes = codes.reshape(4, 16, 512).sum(axis=0).astype(BF16)
    lists = local_lists(place, codes, to_peer(codes), corpus_codes)
    lists = pair_lists(place, lists, to_peer(lists))
    lists = (lists[0], *(shifted(lists[d], d) for d in (1, 2, 3)))
    lists = four_lists(place, lists)
    arrived = lax.all_to_all(lists, YXZ, 0, 0, tiled=True)
    return final_lists(arrived.reshape(512, 128))


def solution(mesh):
    split = Mesh(mesh.devices.reshape(4, 4, 4, 2, 2), QUERY_CORPUS)
    return jax.shard_map(
        per_device,
        mesh=split,
        in_specs=(
            P("y", CORPUS),
            P("y"),
            P("y", CORPUS),
            P("y", CORPUS),
            P(CORPUS, "y"),
            P(CORPUS, None),
            P(QUERY_CORPUS, None),
        ),
        out_specs=P(),
        check_vma=False,
    )
```

```python
import math

import jax
import jax.numpy as jnp
from jax import lax
from jax.experimental import pallas as pl
from jax.experimental.pallas import tpu as pltpu
from jax.sharding import Mesh
from jax.sharding import PartitionSpec as P

D = 4096
SEQ = 32
TOPK = 100
Z = ("zh", "zb")
XZ = ("x", "zh", "zb")
YXZ = ("y", "x", "zh", "zb")
CORPUS = ("x", "zh", "zb", "k")
QUERY_CORPUS = ("y", "x", "zh", "zb", "k")
EPS = 1e-05
F32 = jnp.float32
BF16 = jnp.bfloat16
PARAMS = pltpu.CompilerParams(vmem_limit_bytes=32 * 1024 * 1024)
VMEM = pl.BlockSpec(memory_space=pltpu.VMEM)
SMEM = pl.BlockSpec(memory_space=pltpu.SMEM)


def shape(dims, dtype):
    return jax.ShapeDtypeStruct(dims, dtype)


def to_peer(x):
    return lax.ppermute(x, "k", [(0, 1), (1, 0)])


def shifted(x, d):
    return lax.ppermute(x, "y", [(i, (i + d) % 4) for i in range(4)])


def spread(x, axes, peers):
    copies = jnp.broadcast_to(x[None], (peers, *x.shape))
    return lax.all_to_all(copies, axes, 0, 0, tiled=True)


def lanes(like):
    return lax.broadcasted_iota(jnp.int32, like, 1)


def pack_kernel(place, h, own, other):
    k = place[1]
    x = h[...].astype(F32).T
    for q in range(4):
        one = x[q * 32 : q * 32 + 16, :]
        two = x[q * 32 + 16 : q * 32 + 32, :]
        own[q * 16 : q * 16 + 16, :] = jnp.where(k == 0, one, two).astype(BF16)
        other[q * 16 : q * 16 + 16, :] = jnp.where(k == 0, two, one).astype(BF16)


def pack(place, h):
    part = shape((64, 64), BF16)
    return pl.pallas_call(
        pack_kernel,
        out_shape=(part, part),
        in_specs=[SMEM, VMEM],
        out_specs=(VMEM,) * 2,
        compiler_params=PARAMS,
        name="pack",
    )(place, h)


def gate_up_kernel(place, lengths, h, g0, u0, g1, u1, o0, o1, o2, o3, lhs, wide):
    y = place[0]
    for d in range(4):
        i = (y + d) % 4
        for z in range(8):
            lhs[d * 64 : d * 64 + 64, z * 128 : z * 128 + 128] = h[i * 8 + z]
    left = lhs[...]
    widened = left.astype(F32)
    sq = jnp.sum(widened * widened, axis=1, keepdims=True)
    top = sq.astype(BF16).astype(F32)
    mid = (sq - top).astype(BF16).astype(F32)
    low = sq - top - mid
    col = lanes((256, 256))
    wide[...] = jnp.zeros((256, 256), F32)
    for b, w in enumerate((g0, u0, g1, u1)):
        wide[:, 0:224] = lax.dot_general(
            left, w[...], (((1,), (1,)), ((), ())), preferred_element_type=F32
        )
        block = wide[...]
        if b == 0:
            block = jnp.where(col == 224, top, block)
            block = jnp.where(col == 225, mid, block)
            block = jnp.where(col == 226, low, block)
            for q in range(4):
                block = jnp.where(col == 228 + q, lengths[q].astype(F32), block)
        block = block.astype(BF16)
        for d, o in enumerate((o0, o1, o2, o3)):
            o[:, b * 256 : b * 256 + 256] = block[d * 64 : d * 64 + 64]


def gate_up(place, lengths, h, g0, u0, g1, u1):
    part = shape((64, 1024), BF16)
    return pl.pallas_call(
        gate_up_kernel,
        out_shape=(part,) * 4,
        in_specs=[SMEM] * 2 + [VMEM] * 5,
        out_specs=(VMEM,) * 4,
        scratch_shapes=[pltpu.VMEM((256, 1024), BF16), pltpu.VMEM((256, 256), F32)],
        compiler_params=PARAMS,
        name="gate_up",
    )(place, lengths, h, g0, u0, g1, u1)


def hidden_kernel(place, a, b, c, d, out, counts):
    y, x = place[0], place[7]
    held = jnp.zeros((8, 128), F32)
    for s, part in enumerate((a, b, c, d)):
        held = jnp.where((y - s + 4) % 4 == x, part[0:8, 128:256].astype(F32), held)
    counts[...] = held
    total = a[...].astype(F32) + b[...].astype(F32) + c[...].astype(F32) + d[...].astype(F32)
    col = lanes((64, 256))
    first = total[:, 0:256]
    sq = jnp.sum(jnp.where((col >= 224) & (col < 227), first, 0.0), axis=1, keepdims=True)
    r = lax.rsqrt(sq / D + EPS)
    for b in range(2):
        gate = total[:, b * 512 : b * 512 + 256] * r
        up = total[:, b * 512 + 256 : b * 512 + 512] * r
        units = gate / (1.0 + jnp.exp(-gate)) * up
        out[:, b * 256 : b * 256 + 256] = jnp.where(col < 224, units, 0.0).astype(BF16)


def hidden_of(place, a, b, c, d):
    return pl.pallas_call(
        hidden_kernel,
        out_shape=(shape((64, 512), BF16), shape((8, 128), F32)),
        in_specs=[SMEM] + [VMEM] * 4,
        out_specs=(VMEM,) * 2,
        compiler_params=PARAMS,
        name="hidden_units",
    )(place, a, b, c, d)


def down_kernel(place, a, b, c, d, w0, w1, out, lhs):
    y = place[0]
    for s, part in enumerate((a, b, c, d)):
        at = pl.multiple_of(((y - s + 4) % 4) * 64, 64)
        lhs[pl.ds(at, 64), :] = part[...]
    total = jnp.dot(lhs[:, 0:224], w0[...], preferred_element_type=F32)
    total += jnp.dot(lhs[:, 256:480], w1[...], preferred_element_type=F32)
    out[...] = total.astype(BF16)


def down(place, parts, w0, w1):
    return pl.pallas_call(
        down_kernel,
        out_shape=shape((256, 1024), BF16),
        in_specs=[SMEM] + [VMEM] * 6,
        out_specs=VMEM,
        scratch_shapes=[pltpu.VMEM((256, 512), BF16)],
        compiler_params=PARAMS,
        name="down",
    )(place, *parts, w0, w1)


def residual_kernel(parts, h, res, sq):
    total = h[...].astype(F32)
    for p in range(32):
        total += parts[p].astype(F32)
    res[...] = total
    sq[...] = jnp.broadcast_to(jnp.sum(total * total, axis=1, keepdims=True), (8, 128))


def residual_of(parts, h):
    return pl.pallas_call(
        residual_kernel,
        out_shape=(shape((8, 1024), F32), shape((8, 128), F32)),
        in_specs=[VMEM] * 2,
        out_specs=(VMEM,) * 2,
        compiler_params=PARAMS,
        name="residual",
    )(parts, h)


def pool_kernel(place, counts, res, a, b, c, d, same, other):
    first, zh, zb = place[2], place[5], place[6]
    sq = (a[...] + b[...] + c[...] + d[...])[:, 0:1]
    slots = lax.broadcasted_iota(jnp.int32, (8, 1), 0) + first
    held = jnp.where(lanes((1, 128)) == 100 + zh, counts[0:1, :], 0.0)
    count = jnp.max(held, axis=1, keepdims=True)
    weight = jnp.where(slots.astype(F32) < count, lax.rsqrt(sq / D + EPS), 0.0)
    pooled = jnp.sum(res[...] * weight, axis=0, keepdims=True) / count
    ahead = jnp.concatenate([pooled[:, t * 256 : t * 256 + 128] for t in range(4)], axis=0)
    behind = jnp.concatenate([pooled[:, t * 256 + 128 : t * 256 + 256] for t in range(4)], axis=0)
    same[...] = jnp.where(zb == 0, ahead, behind)
    other[...] = jnp.where(zb == 0, behind, ahead)


def pool(place, counts, res, sqs):
    part = shape((4, 128), F32)
    return pl.pallas_call(
        pool_kernel,
        out_shape=(part,) * 2,
        in_specs=[SMEM] + [VMEM] * 6,
        out_specs=(VMEM,) * 2,
        compiler_params=PARAMS,
        name="pool",
    )(place, counts, res, *sqs)


def code_kernel(place, a, b, c, d, w0, w1, w2, w3, out, left):
    zh = place[5]
    left[...] = a[...] + b[...] + c[...] + d[...]
    total = jnp.zeros((8, 512), F32)
    for s, w in enumerate((w0, w1, w2, w3)):
        piece = jnp.broadcast_to(left[pl.ds((zh - s + 4) % 4, 1), :], (8, 128))
        total += jnp.dot(piece.astype(BF16), w[...], preferred_element_type=F32)
    for t in range(4):
        out[t : t + 1, :] = total[0:1, t * 128 : t * 128 + 128]


def code_part(place, pieces, ws):
    return pl.pallas_call(
        code_kernel,
        out_shape=shape((4, 128), F32),
        in_specs=[SMEM] + [VMEM] * 8,
        out_specs=VMEM,
        scratch_shapes=[pltpu.VMEM((4, 128), F32)],
        compiler_params=PARAMS,
        name="code_part",
    )(place, *pieces, *ws)


def exchange(x, step, falling):
    col = lanes(x.shape)
    upper = (col & step) != 0
    other = jnp.where(upper, pltpu.roll(x, step, 1), pltpu.roll(x, 128 - step, 1))
    return jnp.where(upper ^ falling, jnp.maximum(x, other), jnp.minimum(x, other))


def bitonic_merge(x, falling):
    for step in (64, 32, 16, 8, 4, 2, 1):
        x = exchange(x, step, falling)
    return x


def bitonic_sort(x, falling):
    col = lanes(x.shape)
    for size in (2, 4, 8, 16, 32, 64, 128):
        way = falling if size == 128 else falling ^ ((col & size) != 0)
        step = size // 2
        while step:
            x = exchange(x, step, way)
            step //= 2
    return x


def halves_far(v, apart, falling):
    out = list(v)
    for i in range(len(v)):
        if i & apart == 0:
            high, low = jnp.maximum(v[i], v[i + apart]), jnp.minimum(v[i], v[i + apart])
            way = falling(i)
            if way is True:
                out[i], out[i + apart] = high, low
            elif way is False:
                out[i], out[i + apart] = low, high
            else:
                out[i] = jnp.where(way, high, low)
                out[i + apart] = jnp.where(way, low, high)
    return out


def halves_near(v, step, falling):
    upper = (rows_of((8, 128)) & step) != 0
    out = []
    for i, x in enumerate(v):
        other = pltpu.roll(x, step, 0)
        if step != 4:
            other = jnp.where(upper, other, pltpu.roll(x, 8 - step, 0))
        way = falling(i)
        if way is True:
            take = ~upper
        elif way is False:
            take = upper
        else:
            take = upper ^ way
        out.append(jnp.where(take, jnp.maximum(x, other), jnp.minimum(x, other)))
    return out


def column_step(v, step, falling):
    if step >= 8:
        return halves_far(v, step // 8, falling)
    return halves_near(v, step, falling)


def column_merge(v, falling):
    for step in (64, 32, 16, 8, 4, 2, 1):
        v = column_step(v, step, lambda i: falling)
    return v


def column_sort(v, falling):
    sub = rows_of((8, 128))
    for size in (2, 4, 8, 16, 32, 64, 128):

        def way(i, size=size):
            if size == 128:
                return falling
            if size >= 8:
                return (i * 8) & size == 0
            return (sub & size) == 0

        step = size // 2
        while step:
            v = column_step(v, step, way)
            step //= 2
    return v


def columns_of(x):
    return [x[i * 8 : i * 8 + 8] for i in range(16)]


def rows_of(like):
    return lax.broadcasted_iota(jnp.int32, like, 0)


def score_kernel(place, mine, theirs, docs, lists, *, scale):
    k = place[1]
    own, peer = mine[...], theirs[...]
    low = jnp.where(k == 0, own, peer)
    high = jnp.where(k == 0, peer, own)
    dims = (((1,), (1,)), ((), ()))
    scores = lax.dot_general(low, docs[:, 0:512], dims, preferred_element_type=F32)
    scores += lax.dot_general(high, docs[:, 512:1024], dims, preferred_element_type=F32)
    scores = scores * scale
    x = jnp.concatenate([scores[:, c * 128 : c * 128 + 128] for c in range(4)] * 2, axis=0)
    lane = lanes((8, 128))
    v = column_sort(columns_of(x.T), lane & 32 == 0)
    v = [jnp.maximum(a, pltpu.roll(a, 96, 1)) for a in v]
    v = column_merge(v, lane & 16 == 0)
    v = [jnp.maximum(a, pltpu.roll(a, 112, 1)) for a in v]
    v = column_merge(v, lane * 0 + k == 0)
    lists[...] = jnp.concatenate(v, axis=0).T[0:16]


def local_lists(place, mine, theirs, docs):
    def body(*refs):
        score_kernel(*refs, scale=1.0 / math.sqrt(docs.shape[1]))

    return pl.pallas_call(
        body,
        out_shape=shape((16, 128), F32),
        in_specs=[SMEM] + [VMEM] * 3,
        out_specs=VMEM,
        compiler_params=PARAMS,
        name="scores",
    )(place, mine, theirs, docs)


def pair_kernel(place, a, b, o0, o1, o2, o3, held):
    y = place[0]
    x = jnp.maximum(a[...], b[...])
    turn = (rows_of((16, 128)) // 4 - y + 4) % 4
    held[...] = bitonic_merge(x, turn % 2 == 0)
    for d, o in enumerate((o0, o1, o2, o3)):
        o[...] = held[pl.ds(pl.multiple_of(((y + d) % 4) * 4, 4), 4), :]


def pair_lists(place, a, b):
    four = shape((4, 128), F32)
    return pl.pallas_call(
        pair_kernel,
        out_shape=(four,) * 4,
        in_specs=[SMEM] + [VMEM] * 2,
        out_specs=(VMEM,) * 4,
        scratch_shapes=[pltpu.VMEM((16, 128), F32)],
        compiler_params=PARAMS,
        name="pair_lists",
    )(place, a, b)


def four_kernel(place, a, b, c, d, out):
    odd = place[3]
    x = jnp.concatenate(
        [jnp.maximum(a[...], b[...]), jnp.maximum(c[...], d[...])], axis=0
    )
    x = bitonic_merge(x, rows_of((8, 128)) < 4)
    x = jnp.maximum(x, pltpu.roll(x, 4, 0))
    x = bitonic_merge(x, (rows_of((8, 128)) * 0 + odd) == 0)
    out[...] = jnp.broadcast_to(x[0:4][None], (128, 4, 128))


def four_lists(place, lists):
    return pl.pallas_call(
        four_kernel,
        out_shape=shape((128, 4, 128), F32),
        in_specs=[SMEM] + [VMEM] * 4,
        out_specs=VMEM,
        compiler_params=PARAMS,
        name="four_lists",
    )(place, *lists)


def final_kernel(x_ref, out):
    lane = lanes((8, 128))
    tiles = []
    for y in range(4):
        v = columns_of(x_ref[y * 128 : y * 128 + 128, :].T)
        tiles.append([jnp.maximum(a, pltpu.roll(a, 64, 1)) for a in v])
    first = [jnp.where(lane < 64, a, b) for a, b in zip(tiles[0], tiles[1])]
    second = [jnp.where(lane < 64, a, b) for a, b in zip(tiles[2], tiles[3])]
    first = column_merge(first, lane & 32 == 0)
    second = column_merge(second, lane & 32 == 0)
    v = [
        jnp.where(
            lane & 32 == 0,
            jnp.maximum(a, pltpu.roll(a, 96, 1)),
            jnp.maximum(b, pltpu.roll(b, 32, 1)),
        )
        for a, b in zip(first, second)
    ]
    for near in (16, 8, 4):
        v = column_merge(v, lane & near == 0)
        v = [jnp.maximum(a, pltpu.roll(a, 128 - near, 1)) for a in v]
    v = column_merge(v, True)
    x = jnp.concatenate(v, axis=0).T
    for y, row in enumerate((0, 64, 32, 96)):
        out[y * 4 : y * 4 + 4, :] = x[row : row + 4, 0:TOPK]


def final_lists(x):
    return pl.pallas_call(
        final_kernel,
        out_shape=shape((16, TOPK), F32),
        in_specs=[VMEM],
        out_specs=VMEM,
        compiler_params=PARAMS,
        name="final_lists",
    )(x)


def per_device(hidden_in, lengths, gate_weight, up_weight, down_weight, code_weight, corpus_codes):
    y, x, zh, zb, k = (lax.axis_index(a) for a in QUERY_CORPUS)
    place = jnp.stack([y, k, 16 * k + 8 * zb, x // 2, 4 * zh, zh, zb, x]).astype(jnp.int32)

    own, other = pack(place, hidden_in.T)
    swap = [(a * 4 + b, b * 4 + a) for a in range(4) for b in range(4)]
    straight = [(s * 2 + c, t * 2 + c) for s, t in swap for c in range(2)]
    crossed = [(s * 2 + c, t * 2 + 1 - c) for s, t in swap for c in range(2)]
    own = lax.ppermute(own, ("y", "x", "k"), straight)
    other = lax.ppermute(other, ("y", "x", "k"), crossed)
    block = jnp.where(
        k == 0, jnp.concatenate([own, other], axis=1), jnp.concatenate([other, own], axis=1)
    )
    gate_rows, up_rows = gate_weight.T, up_weight.T
    gate_peer, up_peer, down_peer = (to_peer(w) for w in (gate_rows, up_rows, down_weight))
    code_weight, gate_peer, up_peer, down_peer = lax.optimization_barrier(
        (code_weight, gate_peer, up_peer, down_peer)
    )
    gathered = spread(block, XZ, 32)

    low, high = code_weight[:, :512], code_weight[:, 512:]
    mine = lax.ppermute(jnp.where(k == 0, low, high), ("y", "x", "k"), straight)
    theirs = lax.ppermute(jnp.where(k == 0, high, low), ("y", "x", "k"), crossed)
    rows = jnp.concatenate(
        [jnp.where(k == 0, mine, theirs), jnp.where(k == 0, theirs, mine)], axis=0
    )
    rows, gathered = lax.optimization_barrier((rows, gathered))
    turned = [[(i, (i + d) % 4) for i in range(4)] for d in range(4)]
    code_rows = [rows, *(lax.ppermute(rows, "zh", turned[d]) for d in (1, 2, 3))]

    parts = gate_up(place, lengths, gathered, gate_rows, up_rows, gate_peer, up_peer)
    units, counts = hidden_of(place, parts[0], *(shifted(parts[d], d) for d in (1, 2, 3)))
    groups = (units, *(shifted(units, d) for d in (1, 2, 3)))
    groups, code_rows[2] = lax.optimization_barrier((groups, code_rows[2]))
    branch = down(place, groups, down_weight, down_peer)
    branch, code_rows[1], code_rows[3] = lax.optimization_barrier(
        (branch, code_rows[1], code_rows[3])
    )
    branch = lax.all_to_all(branch.reshape(32, 8, 1024), XZ, 0, 0, tiled=True)
    here = lax.dynamic_slice(
        gathered.reshape(4, 8, 64, 128), (x, 0, zh * 16 + zb * 8, 0), (1, 8, 8, 128)
    )[0]
    here = jnp.moveaxis(here, 0, 1).reshape(8, 1024)
    res, sq = residual_of(branch, here)
    sqs = (sq, *(shifted(sq, d) for d in (1, 2, 3)))
    same, other = pool(place, counts, res, sqs)
    flips = [[(i, i ^ r) for i in range(4)] for r in range(4)]
    sent = ((same, 1), (other, 2), (other, 3))
    pieces = (same, *(lax.ppermute(a, ("zb", "k"), flips[r]) for a, r in sent))
    part = code_part(place, pieces, code_rows)
    part = part + lax.ppermute(part, "zb", [(0, 1), (1, 0)])
    codes = spread(part, ("y", "x", "zh"), 64)
    codes = codes.reshape(4, 16, 512).sum(axis=0).astype(BF16)
    lists = local_lists(place, codes, to_peer(codes), corpus_codes)
    lists = pair_lists(place, lists, to_peer(lists))
    lists = (lists[0], *(shifted(lists[d], d) for d in (1, 2, 3)))
    lists = four_lists(place, lists)
    arrived = lax.all_to_all(lists, YXZ, 0, 0, tiled=True)
    return final_lists(arrived.reshape(512, 128))


def solution(mesh):
    split = Mesh(mesh.devices.reshape(4, 4, 4, 2, 2), QUERY_CORPUS)
    return jax.shard_map(
        per_device,
        mesh=split,
        in_specs=(
            P("y", CORPUS),
            P("y"),
            P("y", CORPUS),
            P("y", CORPUS),
            P(CORPUS, "y"),
            P(CORPUS, None),
            P(QUERY_CORPUS, None),
        ),
        out_specs=P(),
        check_vma=False,
    )
```
